32 devices in a mesh: ctx: 4 (over x, core), fsdp: 8 (over z, y).
Axes of the slice: x: 2, y: 2, z: 4, core: 2. Of those that a mesh axis runs over, the one named last changes fastest.
Arguments:
- hidden_in: bfloat16 [4096, 8, 768], P(('ctx', 'fsdp')), may hold values from -6 to 6
- lengths: int32 [8], replicated, may hold values from 1 to 4096, 24576 in all
- seq_order: int32 [8], replicated, may hold values from 0 to 7, each once
- query_weight: bfloat16 [768, 768], P('fsdp'), may hold values from -0.21875 to 0.21875
- query_bias: bfloat16 [768], P('fsdp'), may hold values from -3 to 3
- key_weight: bfloat16 [768, 768], P('fsdp'), may hold values from -0.3125 to 0.3125
- value_weight: bfloat16 [768, 768], P('fsdp'), may hold values from -0.21875 to 0.21875
- value_bias: bfloat16 [768], P('fsdp'), may hold values from -0.29882812 to 0.29882812
- output_weight: bfloat16 [768, 768], P('fsdp'), may hold values from -4 to 4
- output_bias: bfloat16 [768], P('fsdp'), may hold values from -3 to 3
- norm1_gain: bfloat16 [768], P('fsdp'), may hold values from 0.5 to 1.5
- norm1_shift: bfloat16 [768], P('fsdp'), may hold values from -3 to 3
- inner_weight: bfloat16 [768, 3072], P('fsdp'), may hold values from -0.21875 to 0.21875
- inner_bias: bfloat16 [3072], P('fsdp'), may hold values from -3 to 3
- outer_weight: bfloat16 [3072, 768], P('fsdp'), may hold values from -0.109375 to 0.109375
- outer_bias: bfloat16 [768], P('fsdp'), may hold values from -3 to 3
- norm2_gain: bfloat16 [768], P('fsdp'), may hold values from 0.5 to 1.5
- norm2_shift: bfloat16 [768], P('fsdp'), may hold values from -3 to 3
- cotangent: bfloat16 [4096, 8, 768], P('ctx', 'fsdp'), may hold values from -6 to 6
Outputs:
- layer_out: bfloat16 [4096, 8, 768], P('ctx', 'fsdp')
- grad_in: bfloat16 [4096, 8, 768], P(('ctx', 'fsdp'))
- grad_query_weight: float32 [768, 768], P('fsdp')
- grad_query_bias: float32 [768], P('fsdp')
- grad_key_weight: float32 [768, 768], P('fsdp')
- grad_value_weight: float32 [768, 768], P('fsdp')
- grad_value_bias: float32 [768], P('fsdp')
- grad_output_weight: float32 [768, 768], P('fsdp')
- grad_output_bias: float32 [768], P('fsdp')
- grad_norm1_gain: float32 [768], P('fsdp')
- grad_norm1_shift: float32 [768], P('fsdp')
- grad_inner_weight: float32 [768, 3072], P('fsdp')
- grad_inner_bias: float32 [3072], P('fsdp')
- grad_outer_weight: float32 [3072, 768], P('fsdp')
- grad_outer_bias: float32 [768], P('fsdp')
- grad_norm2_gain: float32 [768], P('fsdp')
- grad_norm2_shift: float32 [768], P('fsdp')
The draws below stay inside these ranges and needn't reach their ends.
Inputs may be any that keep to these rules, and one draw needn't show every extreme that they name: The 8 lengths sum to 24576 and the largest is exactly 4096. `seq_order`: a permutation; index f of fsdp holds slot f.
All inputs are finite; a program needn't handle non-finite values.
Results may differ from the reference program's by a relative error of at most 0.02.
Values may be sent and summed in bfloat16 or wider, within the bound.
A program may use at most 192 MiB of HBM per device.

```python
import math
import jax
import jax.numpy as jnp
import numpy as np
from jax import lax

D = 768
H = 12
HD = 64
FF = 3072
L = 4096
QB = 512
NSEQ = 8


def raised(drawn, key, source, target, parts, factor):
    def block_of(axis_at):
        return (jnp.arange(drawn.shape[axis_at]) // (drawn.shape[axis_at] // parts)).reshape((-1,) + (1,) * (drawn.ndim - 1 - axis_at))

    near = jax.random.permutation(key, parts)[block_of(target)]
    far = (block_of(target) + parts // 2) % parts
    return jnp.where((block_of(source) == near) | (block_of(source) == far), factor * drawn, drawn)


def levels(rng, shape, shards, smallest, high):
    def one(dim, shards_of):
        draws = jax.random.uniform(jax.random.fold_in(jax.random.fold_in(rng, 6), dim), (shards_of,), jnp.float32, smallest / len(shards), high / len(shards))
        return jnp.repeat(jnp.exp(draws), shape[dim] // shards_of).reshape((-1,) + (1,) * (len(shape) - dim - 1))

    gain = one(*shards[0])
    for cut in shards[1:]:
        gain = gain * one(*cut)
    return gain


def split_up(amount, total, limit, skew):
    weights = [(1 << 20) // math.isqrt(rank ** skew) + 1 for rank in range(2, amount + 1)]
    spare, given = total - limit - (amount - 1), [1] * (amount - 1)
    while spare > 0:
        candidates = [i for i in range(amount - 1) if given[i] < limit]
        pool, left = sum([weights[i] for i in candidates]), spare
        for i in candidates:
            extra = min(limit - given[i], max(1, left * weights[i] // pool), spare)
            given[i] = given[i] + extra
            spare = spare - extra
    return np.array([limit] + given)


def uneven(own_key, amount, total, reach, skew):
    if amount == 2:
        one = jax.random.randint(own_key, (), max(1, total - reach), min(reach, total - 1) + 1)
        return jnp.stack([one, total - one])
    sizes = jnp.asarray(split_up(amount, total, reach, skew), jnp.int32)
    couples = (amount - 1) // 2
    giver, sink = sizes[1:1 + 2 * couples:2], sizes[2:2 + 2 * couples:2]
    margin = jnp.minimum(giver - 1, reach - sink)
    passed = jax.random.randint(jax.random.fold_in(own_key, 1), (couples,), 0, 1 << 20) % (margin + 1)
    sizes = sizes.at[1:1 + 2 * couples:2].set(giver - passed).at[2:2 + 2 * couples:2].set(sink + passed)
    return sizes[jax.random.permutation(jax.random.fold_in(own_key, 2), amount)]


def gaussian(rng, dims, scale, reach, shards=(), kind=jnp.bfloat16):
    gain = levels(rng, dims, shards, -0.22, 0.18) if shards else 1.0
    entries = jax.random.normal(rng, dims, jnp.float32) * scale * gain
    return jnp.minimum(jnp.maximum(entries, -reach), reach).astype(kind)


def noise_with(own_key, shape, width, bound, shards, heavy, held_as=jnp.bfloat16):
    array = width * jax.random.normal(own_key, shape, jnp.float32)
    if shards:
        array = array * levels(own_key, shape, shards, -0.22, 0.18)
    return jnp.clip(raised(array, jax.random.fold_in(own_key, 3), *heavy), -bound, bound).astype(held_as)


def setup_inputs(seed: int = 0) -> dict:
    key_of = jax.random.split(jax.random.key(seed), 20)
    return {
        "hidden_in": gaussian(key_of[0], (L, NSEQ, D), 1.0, 6.0, ((0, 32),)),
        "lengths": uneven(key_of[1], NSEQ, 3 * NSEQ * L // 4, L, 2).astype(jnp.int32),
        "seq_order": jax.random.permutation(key_of[2], NSEQ).astype(jnp.int32),
        "query_weight": gaussian(key_of[3], (D, D), D ** -0.5, 0.21875, ((0, 8),)),
        "query_bias": gaussian(key_of[4], (D,), 0.5, 3.0, ((0, 8),)),
        "key_weight": gaussian(key_of[5], (D, D), (D // 2) ** -0.5, 0.3125, ((0, 8),)),
        "value_weight": gaussian(key_of[6], (D, D), D ** -0.5, 0.21875, ((0, 8),)),
        "value_bias": gaussian(key_of[7], (D,), 0.05, 0.29882812, ((0, 8),)),
        "output_weight": gaussian(key_of[8], (D, D), 2 ** -0.5, 4.0, ((0, 8),)),
        "output_bias": gaussian(key_of[9], (D,), 0.5, 3.0, ((0, 8),)),
        "norm1_gain": jnp.clip(1.0 + 0.1 * jax.random.normal(key_of[10], (D,), jnp.float32), 0.5, 1.5).astype(jnp.bfloat16),
        "norm1_shift": gaussian(key_of[11], (D,), 0.5, 3.0, ((0, 8),)),
        "inner_weight": gaussian(key_of[12], (D, FF), D ** -0.5, 0.21875, ((0, 8),)),
        "inner_bias": gaussian(key_of[13], (FF,), 0.5, 3.0, ((0, 8),)),
        "outer_weight": gaussian(key_of[14], (FF, D), FF ** -0.5, 0.109375, ((0, 8),)),
        "outer_bias": gaussian(key_of[15], (D,), 0.5, 3.0, ((0, 8),)),
        "norm2_gain": jnp.clip(1.0 + 0.1 * jax.random.normal(key_of[16], (D,), jnp.float32), 0.5, 1.5).astype(jnp.bfloat16),
        "norm2_shift": gaussian(key_of[17], (D,), 0.5, 3.0, ((0, 8),)),
        "cotangent": noise_with(key_of[18], (L, NSEQ, D), 1.0, 6.0, ((0, 4), (1, 8)), (1, 2, 8, 2.0)),
    }


@jax.custom_vjp
def low(v):
    return lax.optimization_barrier(v.astype(jnp.bfloat16)).astype(jnp.float32)

@jax.custom_vjp
def low_back(v):
    return v

def low_keep(v):
    return (low(v), None)

def low_pass(kept, grad):
    return (grad,)

def back_keep(v):
    return (v, None)

def back_low(kept, grad):
    return (low(grad),)
low.defvjp(low_keep, low_pass)
low_back.defvjp(back_keep, back_low)
NORM_EPSILON = 1e-12
NEG_BIG = -1e+30
HIGHEST = lax.Precision.HIGHEST

def layer_norm(source, gain_vec, shift_vec):
    centre = source - lax.optimization_barrier(jnp.mean(source, axis=-1, keepdims=True))
    spread = lax.optimization_barrier(jnp.mean(centre * centre, axis=-1, keepdims=True))
    return centre * lax.rsqrt(spread + NORM_EPSILON) * gain_vec + shift_vec

def gelu_exact(source):
    return 0.5 * source * (1.0 + jax.scipy.special.erf(source * 0.7071067811865476))

def attend_one(packed):
    query_rows, key_rows, value_rows, length = packed
    usable = jnp.arange(L, dtype=jnp.int32) < length

    def one_block(query_tile):
        scores = jnp.einsum('qhd,khd->hqk', query_tile, key_rows, precision=HIGHEST) * HD ** (-0.5)
        scores = low_back(scores)
        scores = jnp.where(usable[None, None, :], scores, NEG_BIG)
        weights = low(jax.nn.softmax(scores, axis=-1))
        return jnp.einsum('hqk,khd->qhd', weights, value_rows, precision=HIGHEST)
    tiles = lax.map(jax.checkpoint(one_block), query_rows.reshape(L // QB, QB, H, HD))
    return tiles.reshape(L, H, HD)

def reference(hidden_in, lengths, seq_order, query_weight, query_bias, key_weight, value_weight, value_bias, output_weight, output_bias, norm1_gain, norm1_shift, inner_weight, inner_bias, outer_weight, outer_bias, norm2_gain, norm2_shift, cotangent):
    slot_lengths = lengths[seq_order]

    def forward(hidden, w_query, b_query, w_key, w_value, b_value, w_output, b_output, gain_one, shift_one, w_inner, b_inner, w_outer, b_outer, gain_two, shift_two):
        placed = hidden[:, seq_order, :]
        token_rows = placed.reshape(L * NSEQ, D)
        query_all = low_back(low(jnp.dot(token_rows, w_query, precision=HIGHEST) + b_query))
        key_all = low_back(low(jnp.dot(token_rows, w_key, precision=HIGHEST)))
        value_all = low_back(low(jnp.dot(token_rows, w_value, precision=HIGHEST) + b_value))

        def by_slot(source):
            return jnp.moveaxis(source.reshape(L, NSEQ, H, HD), 1, 0)
        attended = lax.map(jax.checkpoint(attend_one), (by_slot(query_all), by_slot(key_all), by_slot(value_all), slot_lengths))
        attended = jnp.moveaxis(attended, 0, 1).reshape(L * NSEQ, D)
        mixed_low = low_back(low(attended))
        branch = low_back(jnp.dot(mixed_low, w_output, precision=HIGHEST) + b_output)
        normed = layer_norm(token_rows + branch, gain_one, shift_one)
        inner_pre = low_back(jnp.dot(low(normed), w_inner, precision=HIGHEST) + b_inner)
        activated = low(gelu_exact(inner_pre))
        outer_out = low_back(jnp.dot(activated, w_outer, precision=HIGHEST) + b_outer)
        return layer_norm(normed + outer_out, gain_two, shift_two).reshape(L, NSEQ, D)
    floats = (hidden_in.astype(jnp.float32), query_weight.astype(jnp.float32), query_bias.astype(jnp.float32), key_weight.astype(jnp.float32), value_weight.astype(jnp.float32), value_bias.astype(jnp.float32), output_weight.astype(jnp.float32), output_bias.astype(jnp.float32), norm1_gain.astype(jnp.float32), norm1_shift.astype(jnp.float32), inner_weight.astype(jnp.float32), inner_bias.astype(jnp.float32), outer_weight.astype(jnp.float32), outer_bias.astype(jnp.float32), norm2_gain.astype(jnp.float32), norm2_shift.astype(jnp.float32))
    result, pullback = jax.vjp(forward, *floats)
    grads = pullback(cotangent.astype(jnp.float32))
    return (result.astype(jnp.bfloat16), grads[0].astype(jnp.bfloat16), grads[1], grads[2], grads[3], grads[4], grads[5], grads[6], grads[7], grads[8], grads[9], grads[10], grads[11], grads[12], grads[13], grads[14], grads[15])
```

```python
import functools

import jax
import jax.numpy as jnp
from jax import lax
from jax.experimental import pallas as pl
from jax.experimental.pallas import tpu as pltpu
from jax.sharding import PartitionSpec as P

SCALE = 64 ** (-0.5)
LOG2E = 1.4426950408889634
FORWARD_KEYS = 2048
BACKWARD_KEYS = 1024
VMEM_BYTES = 60 * 2**20

NORM_EPSILON = 1e-12
NEG_BIG = -1e30
ROOT_HALF = 0.7071067811865476
ROOT_TWO_PI = 2.5066282746310002


def norm_forward(source, gain_vec, shift_vec):
    centre = source - jnp.mean(source, axis=-1, keepdims=True)
    inv_scale = lax.rsqrt(jnp.mean(centre * centre, axis=-1, keepdims=True) + NORM_EPSILON)
    unit_rows = centre * inv_scale
    return (unit_rows * gain_vec + shift_vec, unit_rows, inv_scale)


def norm_backward(upstream, unit_rows, inv_scale, gain_vec):
    scaled = upstream * gain_vec
    plain_mean = jnp.mean(scaled, axis=-1, keepdims=True)
    cross_mean = jnp.mean(scaled * unit_rows, axis=-1, keepdims=True)
    d_source = inv_scale * (scaled - plain_mean - unit_rows * cross_mean)
    return (d_source, jnp.sum(upstream * unit_rows, axis=0), jnp.sum(upstream, axis=0))


def gelu_exact(source):
    return 0.5 * source * (1.0 + jax.scipy.special.erf(source * ROOT_HALF))


def gelu_slope(source):
    return (
        0.5 * (1.0 + jax.scipy.special.erf(source * ROOT_HALF))
        + source * jnp.exp(-0.5 * source * source) / ROOT_TWO_PI
    )


def product(left, right, dims):
    return lax.dot_general(left, right, (dims, ((), ())), preferred_element_type=jnp.float32)


def lane_is_low():
    return lax.broadcasted_iota(jnp.int32, (1, 128), 1) < 64


def split_query(query_pair, low_half):
    scaled = query_pair * (SCALE * LOG2E)
    high = scaled.astype(jnp.bfloat16).astype(jnp.float32)
    rest = pltpu.roll(scaled - high, 64, 1)
    return (
        jnp.where(low_half, high, rest).astype(jnp.bfloat16),
        jnp.where(low_half, rest, high).astype(jnp.bfloat16),
    )


def twice(pair, low_half):
    other = pltpu.roll(pair, 64, 1)
    return (
        jnp.where(low_half, pair, other).astype(jnp.bfloat16),
        jnp.where(low_half, other, pair).astype(jnp.bfloat16),
    )


def forward_kernel(limit_ref, query_ref, key_ref, value_ref, attended_ref, lse_ref, *, key_rows):
    low_half = lane_is_low()
    limit = limit_ref[0]
    queries = split_query(query_ref[...].astype(jnp.float32), low_half)
    query_rows = query_ref.shape[0]

    def step(tile, state):
        start = pl.multiple_of(tile * key_rows, key_rows)
        usable = start + lax.broadcasted_iota(jnp.int32, (key_rows, 1), 0) < limit
        key_tile = key_ref[pl.ds(start, key_rows), :].astype(jnp.float32)
        keys = twice(jnp.where(usable, key_tile, key_ref[0:1, :].astype(jnp.float32)), low_half)
        value_tile = value_ref[pl.ds(start, key_rows), :].astype(jnp.float32)
        value_tile = jnp.where(usable, value_tile, 0.0)
        count = jnp.where(usable, 1.0, 0.0)
        values = (
            jnp.where(low_half, value_tile, count).astype(jnp.bfloat16),
            jnp.where(low_half, count, value_tile).astype(jnp.bfloat16),
        )
        fresh = []
        for head in range(2):
            top, total = state[head]
            scores = product(queries[head], keys[head], ((1,), (1,)))
            new_top = jnp.maximum(top, jnp.max(scores, axis=1, keepdims=True))
            weights = jnp.exp2(scores - new_top).astype(jnp.bfloat16)
            total = total * jnp.exp2(top - new_top) + product(weights, values[head], ((1,), (0,)))
            fresh.append((new_top, total))
        return tuple(fresh)

    empty = (
        jnp.full((query_rows, 1), NEG_BIG, jnp.float32),
        jnp.zeros((query_rows, 128), jnp.float32),
    )
    (top_a, total_a), (top_b, total_b) = lax.fori_loop(
        0, key_ref.shape[0] // key_rows, step, (empty, empty)
    )
    mass_a, mass_b = total_a[:, 64:65], total_b[:, 0:1]
    attended_ref[...] = jnp.where(low_half, total_a / mass_a, total_b / mass_b)
    lse = jnp.where(low_half, top_a + jnp.log2(mass_a), top_b + jnp.log2(mass_b)).T
    lse_ref[0, 0:1, :] = lse[0:1, :]
    lse_ref[0, 1:2, :] = lse[64:65, :]


def backward_kernel(
    limit_ref,
    query_ref,
    key_ref,
    value_ref,
    grad_ref,
    attended_ref,
    lse_ref,
    d_query_ref,
    d_key_ref,
    d_value_ref,
    query_sum,
    *,
    key_rows,
):
    low_half = lane_is_low()
    high_half = jnp.logical_not(low_half)
    lane = lax.broadcasted_iota(jnp.int32, (1, 128), 1)
    limit = limit_ref[0]
    query_pair = query_ref[...].astype(jnp.float32)
    queries = split_query(query_pair, low_half)
    scaled = query_pair * SCALE
    grad_pair = grad_ref[...].astype(jnp.float32)
    overlap = grad_pair * attended_ref[...]
    own_query, own_grad, joined_grad = [], [], []
    for head in range(2):
        mine = low_half if head == 0 else high_half
        own_query.append(jnp.where(mine, scaled, 0.0).astype(jnp.bfloat16))
        own_grad.append(jnp.where(mine, grad_pair, 0.0).astype(jnp.bfloat16))
        delta = -jnp.sum(jnp.where(mine, overlap, 0.0), axis=1, keepdims=True)
        first = delta.astype(jnp.bfloat16).astype(jnp.float32)
        second = (delta - first).astype(jnp.bfloat16).astype(jnp.float32)
        third = delta - first - second
        spare = 64 * (1 - head)
        joined = jnp.where(lane == spare + 2, third, 0.0)
        joined = jnp.where(lane == spare + 1, second, joined)
        joined = jnp.where(lane == spare, first, joined)
        joined_grad.append(jnp.where(mine, grad_pair, joined).astype(jnp.bfloat16))
    query_sum[...] = jnp.zeros_like(query_sum)

    def step(tile, carry):
        start = pl.multiple_of(tile * key_rows, key_rows)
        usable = start + lax.broadcasted_iota(jnp.int32, (key_rows, 1), 0) < limit
        key_tile = key_ref[pl.ds(start, key_rows), :].astype(jnp.float32)
        value_tile = value_ref[pl.ds(start, key_rows), :].astype(jnp.float32)
        keys = twice(jnp.where(usable, key_tile, key_ref[0:1, :].astype(jnp.float32)), low_half)
        own_tile = jnp.where(usable, key_tile * SCALE, 0.0)
        key_piece = value_piece = None
        for head in range(2):
            mine = low_half if head == 0 else high_half
            values = jnp.where(mine, value_tile, 1.0).astype(jnp.bfloat16)
            own_key = jnp.where(mine, own_tile, 0.0).astype(jnp.bfloat16)
            scores = product(keys[head], queries[head], ((1,), (1,)))
            probs = jnp.exp2(scores - lse_ref[0, head : head + 1, :])
            slopes = product(values, joined_grad[head], ((1,), (1,)))
            score_grads = (probs * slopes).astype(jnp.bfloat16)
            value_term = product(probs.astype(jnp.bfloat16), own_grad[head], ((1,), (0,)))
            key_term = product(score_grads, own_query[head], ((1,), (0,)))
            value_piece = value_term if value_piece is None else value_piece + value_term
            key_piece = key_term if key_piece is None else key_piece + key_term
            query_sum[...] += product(own_key, score_grads, ((0,), (0,)))
        d_value_ref[pl.ds(start, key_rows), :] = jnp.where(usable, value_piece, 0.0).astype(
            jnp.bfloat16
        )
        d_key_ref[pl.ds(start, key_rows), :] = jnp.where(usable, key_piece, 0.0).astype(
            jnp.bfloat16
        )
        return carry

    lax.fori_loop(0, key_ref.shape[0] // key_rows, step, 0)
    d_query_ref[...] = query_sum[...].T.astype(jnp.bfloat16)


def attend_forward(queries, joined, limit):
    rows, width = queries.shape
    full = joined.shape[0]
    pairs = width // 128
    row_spec = pl.BlockSpec((rows, 128), lambda pair, *_: (0, pair))
    return pl.pallas_call(
        functools.partial(forward_kernel, key_rows=FORWARD_KEYS),
        grid_spec=pltpu.PrefetchScalarGridSpec(
            num_scalar_prefetch=1,
            grid=(pairs,),
            in_specs=[
                row_spec,
                pl.BlockSpec((full, 128), lambda pair, *_: (0, pair)),
                pl.BlockSpec((full, 128), lambda pair, *_: (0, pair + pairs)),
            ],
            out_specs=[row_spec, pl.BlockSpec((1, 2, rows), lambda pair, *_: (pair, 0, 0))],
        ),
        out_shape=[
            jax.ShapeDtypeStruct((rows, width), jnp.float32),
            jax.ShapeDtypeStruct((pairs, 2, rows), jnp.float32),
        ],
        compiler_params=pltpu.CompilerParams(vmem_limit_bytes=VMEM_BYTES),
        cost_estimate=pl.CostEstimate(
            flops=16 * rows * full * width, bytes_accessed=20_000_000, transcendentals=0
        ),
        name="attend_forward",
    )(limit, queries, joined, joined)


def attend_backward(queries, joined, limit, grad_rows, attended, lse):
    rows, width = queries.shape
    full = joined.shape[0]
    pairs = width // 128
    row_spec = pl.BlockSpec((rows, 128), lambda pair, *_: (0, pair))
    key_spec = pl.BlockSpec((full, 128), lambda pair, *_: (0, pair))
    return pl.pallas_call(
        functools.partial(backward_kernel, key_rows=BACKWARD_KEYS),
        grid_spec=pltpu.PrefetchScalarGridSpec(
            num_scalar_prefetch=1,
            grid=(pairs,),
            in_specs=[
                row_spec,
                key_spec,
                pl.BlockSpec((full, 128), lambda pair, *_: (0, pair + pairs)),
                row_spec,
                row_spec,
                pl.BlockSpec((1, 2, rows), lambda pair, *_: (pair, 0, 0)),
            ],
            out_specs=[row_spec, key_spec, key_spec],
            scratch_shapes=[pltpu.VMEM((128, rows), jnp.float32)],
        ),
        out_shape=[
            jax.ShapeDtypeStruct((rows, width), jnp.bfloat16),
            jax.ShapeDtypeStruct((full, width), jnp.bfloat16),
            jax.ShapeDtypeStruct((full, width), jnp.bfloat16),
        ],
        compiler_params=pltpu.CompilerParams(vmem_limit_bytes=VMEM_BYTES),
        cost_estimate=pl.CostEstimate(
            flops=40 * rows * full * width, bytes_accessed=40_000_000, transcendentals=0
        ),
        name="attend_backward",
    )(limit, queries, joined, joined, grad_rows, attended, lse)


def on_device(
    hidden_in,
    lengths,
    seq_order,
    query_weight,
    query_bias,
    key_weight,
    value_weight,
    value_bias,
    output_weight,
    output_bias,
    norm1_gain,
    norm1_shift,
    inner_weight,
    inner_bias,
    outer_weight,
    outer_bias,
    norm2_gain,
    norm2_shift,
    cotangent,
):
    feat_width = hidden_in.shape[2]
    per_group = hidden_in.shape[1] // lax.axis_size("fsdp")
    placed = jnp.take(hidden_in, seq_order, axis=1)
    tokens = lax.all_to_all(placed, "fsdp", split_axis=1, concat_axis=0, tiled=True)
    local_len = tokens.shape[0]
    row_count = local_len * per_group
    slot_ids = lax.axis_index("fsdp") * per_group + jnp.arange(per_group, dtype=jnp.int32)
    limits = jnp.take(lengths, jnp.take(seq_order, slot_ids))
    w_query, w_key, w_value, w_output, b_query, b_value, b_output, gain_one, shift_one = (
        lax.all_gather(query_weight, "fsdp", axis=0, tiled=True),
        lax.all_gather(key_weight, "fsdp", axis=0, tiled=True),
        lax.all_gather(value_weight, "fsdp", axis=0, tiled=True),
        lax.all_gather(output_weight, "fsdp", axis=0, tiled=True),
        lax.all_gather(query_bias, "fsdp", axis=0, tiled=True),
        lax.all_gather(value_bias, "fsdp", axis=0, tiled=True),
        lax.all_gather(output_bias, "fsdp", axis=0, tiled=True),
        lax.all_gather(norm1_gain, "fsdp", axis=0, tiled=True),
        lax.all_gather(norm1_shift, "fsdp", axis=0, tiled=True),
    )
    token_rows = tokens.reshape(row_count, feat_width)
    queries = (
        jnp.dot(token_rows, w_query, preferred_element_type=jnp.float32)
        + b_query.astype(jnp.float32)
    ).astype(jnp.bfloat16)
    key_part = jnp.dot(token_rows, w_key, preferred_element_type=jnp.float32)
    value_part = jnp.dot(token_rows, w_value, preferred_element_type=jnp.float32) + b_value.astype(
        jnp.float32
    )
    joined = (
        jnp.concatenate((key_part, value_part), axis=1)
        .astype(jnp.bfloat16)
        .reshape(local_len, per_group, 2 * feat_width)
    )
    joined_all = lax.all_gather(joined, "ctx", axis=0, tiled=True)
    full_len = joined_all.shape[0]
    joined_all = joined_all.reshape(full_len, 2 * feat_width)
    attended, lse = attend_forward(queries, joined_all, limits)
    mixed_low = attended.reshape(row_count, feat_width).astype(jnp.bfloat16)
    branch = jnp.dot(mixed_low, w_output, preferred_element_type=jnp.float32) + b_output.astype(
        jnp.float32
    )
    normed, unit_one, scale_one = norm_forward(
        token_rows.astype(jnp.float32) + branch,
        gain_one.astype(jnp.float32),
        shift_one.astype(jnp.float32),
    )
    normed_low = normed.astype(jnp.bfloat16)
    w_inner, w_outer, b_inner, b_outer, gain_two, shift_two = (
        lax.all_gather(inner_weight, "fsdp", axis=0, tiled=True),
        lax.all_gather(outer_weight, "fsdp", axis=0, tiled=True),
        lax.all_gather(inner_bias, "fsdp", axis=0, tiled=True),
        lax.all_gather(outer_bias, "fsdp", axis=0, tiled=True),
        lax.all_gather(norm2_gain, "fsdp", axis=0, tiled=True),
        lax.all_gather(norm2_shift, "fsdp", axis=0, tiled=True),
    )
    inner_pre = jnp.dot(normed_low, w_inner, preferred_element_type=jnp.float32) + b_inner.astype(
        jnp.float32
    )
    activated = gelu_exact(inner_pre).astype(jnp.bfloat16)
    outer_out = jnp.dot(activated, w_outer, preferred_element_type=jnp.float32) + b_outer.astype(
        jnp.float32
    )
    second, unit_two, scale_two = norm_forward(
        normed + outer_out, gain_two.astype(jnp.float32), shift_two.astype(jnp.float32)
    )
    layer_out = second.astype(jnp.bfloat16).reshape(local_len, per_group, feat_width)
    back_inner, back_outer, back_gain_two = (
        lax.all_gather(inner_weight, "fsdp", axis=0, tiled=True),
        lax.all_gather(outer_weight, "fsdp", axis=0, tiled=True),
        lax.all_gather(norm2_gain, "fsdp", axis=0, tiled=True),
    )
    upstream = cotangent.reshape(row_count, feat_width).astype(jnp.float32)
    d_second, grad_gain_two, grad_shift_two = norm_backward(
        upstream, unit_two, scale_two, back_gain_two.astype(jnp.float32)
    )
    d_outer = d_second.astype(jnp.bfloat16)
    grad_outer_w = jnp.einsum("tf,td->fd", activated, d_outer, preferred_element_type=jnp.float32)
    grad_outer_b = jnp.sum(d_outer.astype(jnp.float32), axis=0)
    inner_grad = jnp.einsum("td,fd->tf", d_outer, back_outer, preferred_element_type=jnp.float32)
    d_inner = (inner_grad * gelu_slope(inner_pre)).astype(jnp.bfloat16)
    grad_inner_w = jnp.einsum("td,tf->df", normed_low, d_inner, preferred_element_type=jnp.float32)
    grad_inner_b = jnp.sum(d_inner.astype(jnp.float32), axis=0)
    d_normed = d_second + jnp.einsum(
        "tf,df->td", d_inner, back_inner, preferred_element_type=jnp.float32
    )
    part_inner_w, part_outer_w, part_inner_b, part_outer_b, part_gain_two, part_shift_two = (
        lax.psum_scatter(grad_inner_w.astype(jnp.bfloat16), "fsdp", scatter_dimension=0, tiled=True),
        lax.psum_scatter(grad_outer_w.astype(jnp.bfloat16), "fsdp", scatter_dimension=0, tiled=True),
        lax.psum_scatter(grad_inner_b.astype(jnp.bfloat16), "fsdp", scatter_dimension=0, tiled=True),
        lax.psum_scatter(grad_outer_b.astype(jnp.bfloat16), "fsdp", scatter_dimension=0, tiled=True),
        lax.psum_scatter(grad_gain_two.astype(jnp.bfloat16), "fsdp", scatter_dimension=0, tiled=True),
        lax.psum_scatter(grad_shift_two.astype(jnp.bfloat16), "fsdp", scatter_dimension=0, tiled=True),
    )
    back_query, back_key, back_value, back_output, back_gain_one = (
        lax.all_gather(query_weight, "fsdp", axis=0, tiled=True),
        lax.all_gather(key_weight, "fsdp", axis=0, tiled=True),
        lax.all_gather(value_weight, "fsdp", axis=0, tiled=True),
        lax.all_gather(output_weight, "fsdp", axis=0, tiled=True),
        lax.all_gather(norm1_gain, "fsdp", axis=0, tiled=True),
    )
    d_res, grad_gain_one, grad_shift_one = norm_backward(
        d_normed, unit_one, scale_one, back_gain_one.astype(jnp.float32)
    )
    d_branch = d_res.astype(jnp.bfloat16)
    grad_output_w = jnp.einsum("td,te->de", mixed_low, d_branch, preferred_element_type=jnp.float32)
    grad_output_b = jnp.sum(d_branch.astype(jnp.float32), axis=0)
    d_mixed = jnp.einsum(
        "te,de->td", d_branch, back_output, preferred_element_type=jnp.float32
    ).astype(jnp.bfloat16)
    d_query, key_terms, value_terms = attend_backward(
        queries, joined_all, limits, d_mixed, attended, lse
    )
    key_sum, value_sum = (
        lax.psum_scatter(
            key_terms.reshape(full_len, per_group, feat_width).astype(jnp.bfloat16),
            "ctx",
            scatter_dimension=0,
            tiled=True,
        ).astype(jnp.float32),
        lax.psum_scatter(
            value_terms.reshape(full_len, per_group, feat_width).astype(jnp.bfloat16),
            "ctx",
            scatter_dimension=0,
            tiled=True,
        ).astype(jnp.float32),
    )
    d_keys = key_sum.reshape(row_count, feat_width).astype(jnp.bfloat16)
    d_values = value_sum.reshape(row_count, feat_width).astype(jnp.bfloat16)
    grad_query_w = jnp.einsum("td,te->de", token_rows, d_query, preferred_element_type=jnp.float32)
    grad_query_b = jnp.sum(d_query.astype(jnp.float32), axis=0)
    grad_key_w = jnp.einsum("td,te->de", token_rows, d_keys, preferred_element_type=jnp.float32)
    grad_value_w = jnp.einsum("td,te->de", token_rows, d_values, preferred_element_type=jnp.float32)
    grad_value_b = jnp.sum(d_values.astype(jnp.float32), axis=0)
    d_placed = d_res + jnp.einsum(
        "te,de->td", d_query, back_query, preferred_element_type=jnp.float32
    )
    d_placed = d_placed + jnp.einsum(
        "te,de->td", d_keys, back_key, preferred_element_type=jnp.float32
    )
    d_placed = d_placed + jnp.einsum(
        "te,de->td", d_values, back_value, preferred_element_type=jnp.float32
    )
    back_rows = d_placed.astype(jnp.bfloat16).reshape(local_len, per_group, feat_width)
    returned = lax.all_to_all(back_rows, "fsdp", split_axis=0, concat_axis=1, tiled=True)
    inverse = (
        jnp.zeros(seq_order.shape, jnp.int32)
        .at[seq_order]
        .set(jnp.arange(seq_order.shape[0], dtype=jnp.int32))
    )
    grad_in = jnp.take(returned, inverse, axis=1)
    (
        part_query_w,
        part_query_b,
        part_key_w,
        part_value_w,
        part_value_b,
        part_output_w,
        part_output_b,
        part_gain_one,
        part_shift_one,
    ) = (
        lax.psum_scatter(grad_query_w.astype(jnp.bfloat16), "fsdp", scatter_dimension=0, tiled=True),
        lax.psum_scatter(grad_query_b.astype(jnp.bfloat16), "fsdp", scatter_dimension=0, tiled=True),
        lax.psum_scatter(grad_key_w.astype(jnp.bfloat16), "fsdp", scatter_dimension=0, tiled=True),
        lax.psum_scatter(grad_value_w.astype(jnp.bfloat16), "fsdp", scatter_dimension=0, tiled=True),
        lax.psum_scatter(grad_value_b.astype(jnp.bfloat16), "fsdp", scatter_dimension=0, tiled=True),
        lax.psum_scatter(grad_output_w.astype(jnp.bfloat16), "fsdp", scatter_dimension=0, tiled=True),
        lax.psum_scatter(grad_output_b.astype(jnp.bfloat16), "fsdp", scatter_dimension=0, tiled=True),
        lax.psum_scatter(grad_gain_one.astype(jnp.bfloat16), "fsdp", scatter_dimension=0, tiled=True),
        lax.psum_scatter(grad_shift_one.astype(jnp.bfloat16), "fsdp", scatter_dimension=0, tiled=True),
    )
    summed = (
        lax.psum(part_query_w.astype(jnp.bfloat16), "ctx").astype(jnp.float32),
        lax.psum(part_query_b.astype(jnp.bfloat16), "ctx").astype(jnp.float32),
        lax.psum(part_key_w.astype(jnp.bfloat16), "ctx").astype(jnp.float32),
        lax.psum(part_value_w.astype(jnp.bfloat16), "ctx").astype(jnp.float32),
        lax.psum(part_value_b.astype(jnp.bfloat16), "ctx").astype(jnp.float32),
        lax.psum(part_output_w.astype(jnp.bfloat16), "ctx").astype(jnp.float32),
        lax.psum(part_output_b.astype(jnp.bfloat16), "ctx").astype(jnp.float32),
        lax.psum(part_gain_one.astype(jnp.bfloat16), "ctx").astype(jnp.float32),
        lax.psum(part_shift_one.astype(jnp.bfloat16), "ctx").astype(jnp.float32),
        lax.psum(part_inner_w.astype(jnp.bfloat16), "ctx").astype(jnp.float32),
        lax.psum(part_inner_b.astype(jnp.bfloat16), "ctx").astype(jnp.float32),
        lax.psum(part_outer_w.astype(jnp.bfloat16), "ctx").astype(jnp.float32),
        lax.psum(part_outer_b.astype(jnp.bfloat16), "ctx").astype(jnp.float32),
        lax.psum(part_gain_two.astype(jnp.bfloat16), "ctx").astype(jnp.float32),
        lax.psum(part_shift_two.astype(jnp.bfloat16), "ctx").astype(jnp.float32),
    )
    return (
        layer_out,
        grad_in,
        summed[0],
        summed[1],
        summed[2],
        summed[3],
        summed[4],
        summed[5],
        summed[6],
        summed[7],
        summed[8],
        summed[9],
        summed[10],
        summed[11],
        summed[12],
        summed[13],
        summed[14],
    )


def solution(mesh):
    placed = (
        P(("ctx", "fsdp"), None, None),
        P(),
        P(),
        P("fsdp", None),
        P("fsdp"),
        P("fsdp", None),
        P("fsdp", None),
        P("fsdp"),
        P("fsdp", None),
        P("fsdp"),
        P("fsdp"),
        P("fsdp"),
        P("fsdp", None),
        P("fsdp"),
        P("fsdp", None),
        P("fsdp"),
        P("fsdp"),
        P("fsdp"),
        P("ctx", "fsdp", None),
    )
    return jax.shard_map(
        on_device,
        mesh=mesh,
        in_specs=placed,
        out_specs=(
            P("ctx", "fsdp", None),
            P(("ctx", "fsdp"), None, None),
            P("fsdp", None),
            P("fsdp"),
            P("fsdp", None),
            P("fsdp", None),
            P("fsdp"),
            P("fsdp", None),
            P("fsdp"),
            P("fsdp"),
            P("fsdp"),
            P("fsdp", None),
            P("fsdp"),
            P("fsdp", None),
            P("fsdp"),
            P("fsdp"),
            P("fsdp"),
        ),
        check_vma=False,
    )
```

```python
import functools

import jax
import jax.numpy as jnp
from jax import lax
from jax.experimental import pallas as pl
from jax.experimental.pallas import tpu as pltpu
from jax.sharding import PartitionSpec as P

SCALE = 64 ** (-0.5)
LOG2E = 1.4426950408889634
FORWARD_KEYS = 2048
BACKWARD_KEYS = 1024
VMEM_BYTES = 60 * 2**20

NORM_EPSILON = 1e-12
NEG_BIG = -1e30
ROOT_HALF = 0.7071067811865476
ROOT_TWO_PI = 2.5066282746310002


def norm_forward(source, gain_vec, shift_vec):
    centre = source - jnp.mean(source, axis=-1, keepdims=True)
    inv_scale = lax.rsqrt(jnp.mean(centre * centre, axis=-1, keepdims=True) + NORM_EPSILON)
    unit_rows = centre * inv_scale
    return (unit_rows * gain_vec + shift_vec, unit_rows, inv_scale)


def norm_backward(upstream, unit_rows, inv_scale, gain_vec):
    scaled = upstream * gain_vec
    plain_mean = jnp.mean(scaled, axis=-1, keepdims=True)
    cross_mean = jnp.mean(scaled * unit_rows, axis=-1, keepdims=True)
    d_source = inv_scale * (scaled - plain_mean - unit_rows * cross_mean)
    return (d_source, jnp.sum(upstream * unit_rows, axis=0), jnp.sum(upstream, axis=0))


def gelu_exact(source):
    return 0.5 * source * (1.0 + jax.scipy.special.erf(source * ROOT_HALF))


def gelu_slope(source):
    return (
        0.5 * (1.0 + jax.scipy.special.erf(source * ROOT_HALF))
        + source * jnp.exp(-0.5 * source * source) / ROOT_TWO_PI
    )


def product(left, right, dims):
    return lax.dot_general(left, right, (dims, ((), ())), preferred_element_type=jnp.float32)


def lane_is_low():
    return lax.broadcasted_iota(jnp.int32, (1, 128), 1) < 64


def split_query(query_pair, low_half):
    scaled = query_pair * (SCALE * LOG2E)
    high = scaled.astype(jnp.bfloat16).astype(jnp.float32)
    rest = pltpu.roll(scaled - high, 64, 1)
    return (
        jnp.where(low_half, high, rest).astype(jnp.bfloat16),
        jnp.where(low_half, rest, high).astype(jnp.bfloat16),
    )


def twice(pair, low_half):
    other = pltpu.roll(pair, 64, 1)
    return (
        jnp.where(low_half, pair, other).astype(jnp.bfloat16),
        jnp.where(low_half, other, pair).astype(jnp.bfloat16),
    )


def forward_kernel(limit_ref, query_ref, key_ref, value_ref, attended_ref, lse_ref, *, key_rows):
    low_half = lane_is_low()
    limit = limit_ref[0]
    queries = split_query(query_ref[...].astype(jnp.float32), low_half)
    query_rows = query_ref.shape[0]

    def step(tile, state):
        start = pl.multiple_of(tile * key_rows, key_rows)
        usable = start + lax.broadcasted_iota(jnp.int32, (key_rows, 1), 0) < limit
        key_tile = key_ref[pl.ds(start, key_rows), :].astype(jnp.float32)
        keys = twice(jnp.where(usable, key_tile, key_ref[0:1, :].astype(jnp.float32)), low_half)
        value_tile = value_ref[pl.ds(start, key_rows), :].astype(jnp.float32)
        value_tile = jnp.where(usable, value_tile, 0.0)
        count = jnp.where(usable, 1.0, 0.0)
        values = (
            jnp.where(low_half, value_tile, count).astype(jnp.bfloat16),
            jnp.where(low_half, count, value_tile).astype(jnp.bfloat16),
        )
        fresh = []
        for head in range(2):
            top, total = state[head]
            scores = product(queries[head], keys[head], ((1,), (1,)))
            new_top = jnp.maximum(top, jnp.max(scores, axis=1, keepdims=True))
            weights = jnp.exp2(scores - new_top).astype(jnp.bfloat16)
            total = total * jnp.exp2(top - new_top) + product(weights, values[head], ((1,), (0,)))
            fresh.append((new_top, total))
        return tuple(fresh)

    empty = (
        jnp.full((query_rows, 1), NEG_BIG, jnp.float32),
        jnp.zeros((query_rows, 128), jnp.float32),
    )
    (top_a, total_a), (top_b, total_b) = lax.fori_loop(
        0, key_ref.shape[0] // key_rows, step, (empty, empty)
    )
    mass_a, mass_b = total_a[:, 64:65], total_b[:, 0:1]
    attended_ref[...] = jnp.where(low_half, total_a / mass_a, total_b / mass_b)
    lse = jnp.where(low_half, top_a + jnp.log2(mass_a), top_b + jnp.log2(mass_b)).T
    lse_ref[0, 0:1, :] = lse[0:1, :]
    lse_ref[0, 1:2, :] = lse[64:65, :]


def backward_kernel(
    limit_ref,
    query_ref,
    key_ref,
    value_ref,
    grad_ref,
    attended_ref,
    lse_ref,
    d_query_ref,
    d_key_ref,
    d_value_ref,
    query_sum,
    *,
    key_rows,
):
    low_half = lane_is_low()
    high_half = jnp.logical_not(low_half)
    lane = lax.broadcasted_iota(jnp.int32, (1, 128), 1)
    limit = limit_ref[0]
    query_pair = query_ref[...].astype(jnp.float32)
    queries = split_query(query_pair, low_half)
    scaled = query_pair * SCALE
    grad_pair = grad_ref[...].astype(jnp.float32)
    overlap = grad_pair * attended_ref[...]
    own_query, own_grad, joined_grad = [], [], []
    for head in range(2):
        mine = low_half if head == 0 else high_half
        own_query.append(jnp.where(mine, scaled, 0.0).astype(jnp.bfloat16))
        own_grad.append(jnp.where(mine, grad_pair, 0.0).astype(jnp.bfloat16))
        delta = -jnp.sum(jnp.where(mine, overlap, 0.0), axis=1, keepdims=True)
        first = delta.astype(jnp.bfloat16).astype(jnp.float32)
        second = (delta - first).astype(jnp.bfloat16).astype(jnp.float32)
        third = delta - first - second
        spare = 64 * (1 - head)
        joined = jnp.where(lane == spare + 2, third, 0.0)
        joined = jnp.where(lane == spare + 1, second, joined)
        joined = jnp.where(lane == spare, first, joined)
        joined_grad.append(jnp.where(mine, grad_pair, joined).astype(jnp.bfloat16))
    query_sum[...] = jnp.zeros_like(query_sum)

    def step(tile, carry):
        start = pl.multiple_of(tile * key_rows, key_rows)
        usable = start + lax.broadcasted_iota(jnp.int32, (key_rows, 1), 0) < limit
        key_tile = key_ref[pl.ds(start, key_rows), :].astype(jnp.float32)
        value_tile = value_ref[pl.ds(start, key_rows), :].astype(jnp.float32)
        keys = twice(jnp.where(usable, key_tile, key_ref[0:1, :].astype(jnp.float32)), low_half)
        own_tile = jnp.where(usable, key_tile * SCALE, 0.0)
        key_piece = value_piece = None
        for head in range(2):
            mine = low_half if head == 0 else high_half
            values = jnp.where(mine, value_tile, 1.0).astype(jnp.bfloat16)
            own_key = jnp.where(mine, own_tile, 0.0).astype(jnp.bfloat16)
            scores = product(keys[head], queries[head], ((1,), (1,)))
            probs = jnp.exp2(scores - lse_ref[0, head : head + 1, :])
            slopes = product(values, joined_grad[head], ((1,), (1,)))
            score_grads = (probs * slopes).astype(jnp.bfloat16)
            value_term = product(probs.astype(jnp.bfloat16), own_grad[head], ((1,), (0,)))
            key_term = product(score_grads, own_query[head], ((1,), (0,)))
            value_piece = value_term if value_piece is None else value_piece + value_term
            key_piece = key_term if key_piece is None else key_piece + key_term
            query_sum[...] += product(own_key, score_grads, ((0,), (0,)))
        d_value_ref[pl.ds(start, key_rows), :] = jnp.where(usable, value_piece, 0.0).astype(
            jnp.bfloat16
        )
        d_key_ref[pl.ds(start, key_rows), :] = jnp.where(usable, key_piece, 0.0).astype(
            jnp.bfloat16
        )
        return carry

    lax.fori_loop(0, key_ref.shape[0] // key_rows, step, 0)
    d_query_ref[...] = query_sum[...].T.astype(jnp.bfloat16)


def attend_forward(queries, keys, values, limit):
    rows, width = queries.shape
    full = keys.shape[0]
    pairs = width // 128
    row_spec = pl.BlockSpec((rows, 128), lambda pair, *_: (0, pair))
    return pl.pallas_call(
        functools.partial(forward_kernel, key_rows=FORWARD_KEYS),
        grid_spec=pltpu.PrefetchScalarGridSpec(
            num_scalar_prefetch=1,
            grid=(pairs,),
            in_specs=[
                row_spec,
                pl.BlockSpec((full, 128), lambda pair, *_: (0, pair)),
                pl.BlockSpec((full, 128), lambda pair, *_: (0, pair)),
            ],
            out_specs=[row_spec, pl.BlockSpec((1, 2, rows), lambda pair, *_: (pair, 0, 0))],
        ),
        out_shape=[
            jax.ShapeDtypeStruct((rows, width), jnp.float32),
            jax.ShapeDtypeStruct((pairs, 2, rows), jnp.float32),
        ],
        compiler_params=pltpu.CompilerParams(vmem_limit_bytes=VMEM_BYTES),
        cost_estimate=pl.CostEstimate(
            flops=16 * rows * full * width, bytes_accessed=20_000_000, transcendentals=0
        ),
        name="attend_forward",
    )(limit, queries, keys, values)


def attend_backward(queries, keys, values, limit, grad_rows, attended, lse):
    rows, width = queries.shape
    full = keys.shape[0]
    pairs = width // 128
    row_spec = pl.BlockSpec((rows, 128), lambda pair, *_: (0, pair))
    key_spec = pl.BlockSpec((full, 128), lambda pair, *_: (0, pair))
    return pl.pallas_call(
        functools.partial(backward_kernel, key_rows=BACKWARD_KEYS),
        grid_spec=pltpu.PrefetchScalarGridSpec(
            num_scalar_prefetch=1,
            grid=(pairs,),
            in_specs=[
                row_spec,
                key_spec,
                pl.BlockSpec((full, 128), lambda pair, *_: (0, pair)),
                row_spec,
                row_spec,
                pl.BlockSpec((1, 2, rows), lambda pair, *_: (pair, 0, 0)),
            ],
            out_specs=[row_spec, key_spec, key_spec],
            scratch_shapes=[pltpu.VMEM((128, rows), jnp.float32)],
        ),
        out_shape=[
            jax.ShapeDtypeStruct((rows, width), jnp.bfloat16),
            jax.ShapeDtypeStruct((full, width), jnp.bfloat16),
            jax.ShapeDtypeStruct((full, width), jnp.bfloat16),
        ],
        compiler_params=pltpu.CompilerParams(vmem_limit_bytes=VMEM_BYTES),
        cost_estimate=pl.CostEstimate(
            flops=40 * rows * full * width, bytes_accessed=40_000_000, transcendentals=0
        ),
        name="attend_backward",
    )(limit, queries, keys, values, grad_rows, attended, lse)


MESH = pl.DeviceIdType.MESH
DMA = pltpu.SemaphoreType.DMA
ANY = pl.BlockSpec(memory_space=pl.ANY)
STAGES = ("start", "after_core", "after_across", "after_group", "finish")


def places():
    ctx, group = lax.axis_index("ctx"), lax.axis_index("fsdp")
    return ctx, group, lax.rem(ctx + 2, 4), ctx + 1 - 2 * lax.rem(ctx, 2)


def remote(source, target, send_sem, recv_sem, where):
    return pltpu.make_async_remote_copy(
        src_ref=source,
        dst_ref=target,
        send_sem=send_sem,
        recv_sem=recv_sem,
        device_id=where,
        device_id_type=MESH,
    )


def greet(count):
    ctx, group, _, _ = places()
    barrier = pltpu.get_barrier_semaphore()

    def one(step, carry):
        pl.semaphore_signal(
            barrier,
            inc=1,
            device_id={"fsdp": lax.rem(group + step, count)},
            device_id_type=MESH,
        )
        return carry

    lax.fori_loop(1, count, one, 0)
    for other in range(1, 4):
        pl.semaphore_signal(
            barrier, inc=1, device_id={"ctx": lax.rem(ctx + other, 4)}, device_id_type=MESH
        )
    pl.semaphore_wait(barrier, count - 1 + 3)


def arrival_kernel(
    placed,
    weights,
    small,
    tokens,
    gathered,
    small_all,
    tok_stage,
    w_stage,
    small_stage,
    local_sem,
    tok_send,
    tok_recv,
    w_send,
    w_recv,
    small_send,
    small_recv,
    x_send,
    x_recv,
    s_send,
    s_recv,
    r_send,
    r_recv,
    *,
    count,
):
    ctx, group, across, sibling = places()
    own_tok = pltpu.make_async_copy(placed.at[group], tok_stage, local_sem.at[0])
    own_w = pltpu.make_async_copy(weights.at[ctx], w_stage, local_sem.at[1])
    own_small = pltpu.make_async_copy(small, small_stage, local_sem.at[2])
    own_tok.start()
    own_w.start()
    own_small.start()
    greet(count)

    def tok_copy(peer, step):
        return remote(
            placed.at[peer],
            tokens.at[ctx, group],
            tok_send.at[step],
            tok_recv.at[step],
            {"fsdp": peer},
        )

    def w_copy(peer, step):
        return remote(
            weights.at[ctx],
            gathered.at[ctx, group],
            w_send.at[step],
            w_recv.at[step],
            {"fsdp": peer},
        )

    def small_copy(peer, step):
        return remote(
            small, small_all.at[group], small_send.at[step], small_recv.at[step], {"fsdp": peer}
        )

    def send(step, carry):
        peer = lax.rem(group + step, count)
        w_copy(peer, step).start()
        tok_copy(peer, step).start()
        small_copy(peer, step).start()
        return carry

    lax.fori_loop(1, count, send, 0)
    own_tok.wait()
    own_w.wait()
    own_small.wait()
    put_tok = pltpu.make_async_copy(tok_stage, tokens.at[ctx, group], local_sem.at[0])
    put_w = pltpu.make_async_copy(w_stage, gathered.at[ctx, group], local_sem.at[1])
    put_small = pltpu.make_async_copy(small_stage, small_all.at[group], local_sem.at[2])
    put_tok.start()
    put_w.start()
    put_small.start()

    def across_copy(kind, block):
        where = gathered if kind == 0 else tokens
        return remote(
            where.at[ctx, block],
            where.at[ctx, block],
            x_send.at[kind, block],
            x_recv.at[kind, block],
            {"ctx": across},
        )

    def sibling_copy(kind, block):
        where = gathered if kind == 0 else tokens
        return remote(
            where.at[ctx, block],
            where.at[ctx, block],
            s_send.at[kind, block],
            s_recv.at[kind, block],
            {"ctx": sibling},
        )

    def relay_copy(kind, block):
        where = gathered if kind == 0 else tokens
        return remote(
            where.at[across, block],
            where.at[across, block],
            r_send.at[kind, block],
            r_recv.at[kind, block],
            {"ctx": sibling},
        )

    put_w.wait()
    across_copy(0, group).start()
    sibling_copy(0, group).start()
    put_tok.wait()
    across_copy(1, group).start()
    sibling_copy(1, group).start()
    put_small.wait()

    def arrive(step, carry):
        origin = lax.rem(group - step + count, count)
        w_copy(origin, step).wait_recv()
        across_copy(0, origin).start()
        sibling_copy(0, origin).start()
        tok_copy(origin, step).wait_recv()
        across_copy(1, origin).start()
        sibling_copy(1, origin).start()
        return carry

    lax.fori_loop(1, count, arrive, 0)

    def passed(step, carry):
        origin = lax.rem(group - step + count, count)
        for kind in range(2):
            across_copy(kind, origin).wait_recv()
            relay_copy(kind, origin).start()
        return carry

    lax.fori_loop(0, count, passed, 0)

    def finish(step, carry):
        origin = lax.rem(group - step + count, count)
        for kind in range(2):
            across_copy(kind, origin).wait_send()
            sibling_copy(kind, origin).wait()
            relay_copy(kind, origin).wait()
        return carry

    lax.fori_loop(0, count, finish, 0)

    def sent(step, carry):
        peer = lax.rem(group + step, count)
        w_copy(peer, step).wait_send()
        tok_copy(peer, step).wait_send()
        small_copy(peer, step).wait()
        return carry

    lax.fori_loop(1, count, sent, 0)


def bring_in(placed, weights, small):
    count, rows, width = placed.shape
    return pl.pallas_call(
        functools.partial(arrival_kernel, count=count),
        in_specs=[ANY] * 3,
        out_specs=[ANY] * 3,
        out_shape=[
            jax.ShapeDtypeStruct((4, count, rows, width), jnp.bfloat16),
            jax.ShapeDtypeStruct((4, count) + weights.shape[1:], jnp.bfloat16),
            jax.ShapeDtypeStruct((count,) + small.shape, jnp.bfloat16),
        ],
        scratch_shapes=[
            pltpu.VMEM((rows, width), jnp.bfloat16),
            pltpu.VMEM(weights.shape[1:], jnp.bfloat16),
            pltpu.VMEM(small.shape, jnp.bfloat16),
            DMA((3,)),
        ]
        + [DMA((count,))] * 6
        + [DMA((2, count))] * 6,
        compiler_params=pltpu.CompilerParams(
            collective_id=0, has_side_effects=True, vmem_limit_bytes=8 * 2**20
        ),
        name="bring_in",
    )(placed, weights, small)


class Sum:
    SCRATCH = 16

    def __init__(self, kind, ref, out, scratch, count):
        self.kind, self.ref, self.out, self.count = kind, ref, out, count
        self.near, self.far, self.got_near, self.got_far = scratch[:4]
        self.got_across, self.got_group, self.done = scratch[4:7]
        self.load, self.c_send, self.c_recv, self.x_send, self.x_recv = scratch[7:12]
        self.g_send, self.g_recv, self.o_send, self.o_recv = scratch[12:16]
        self.ctx, self.group, self.across, self.sibling = places()
        self.width = self.near.shape[-1]

    @staticmethod
    def scratch(count, rows, width):
        return (
            [pltpu.VMEM((count, rows, width), jnp.bfloat16)] * 6
            + [pltpu.VMEM((rows, width), jnp.bfloat16)]
            + [DMA((2,))] * 3
            + [DMA((count,))] * 4
            + [DMA((4,))] * 2
        )

    def quarter(self, index):
        if self.kind == 0:
            return self.ref.at[index]
        if self.kind == 1:
            start = pl.multiple_of(index * self.width, self.width)
            return self.ref.at[:, :, pl.ds(start, self.width)]
        return self.ref.at[:, index]

    def loads(self):
        return (
            pltpu.make_async_copy(self.quarter(self.across), self.far, self.load.at[0]),
            pltpu.make_async_copy(self.quarter(self.ctx), self.near, self.load.at[1]),
        )

    def cores(self):
        beyond = lax.rem(self.sibling + 2, 4)
        there = {"ctx": self.sibling}
        return (
            remote(self.quarter(beyond), self.got_far, self.c_send.at[0], self.c_recv.at[0], there),
            remote(
                self.quarter(self.sibling),
                self.got_near,
                self.c_send.at[1],
                self.c_recv.at[1],
                there,
            ),
        )

    def x_copy(self, block):
        return remote(
            self.far.at[block],
            self.got_across.at[block],
            self.x_send.at[block],
            self.x_recv.at[block],
            {"ctx": self.across},
        )

    def g_copy(self, peer, step):
        return remote(
            self.near.at[peer],
            self.got_group.at[step],
            self.g_send.at[step],
            self.g_recv.at[step],
            {"fsdp": peer},
        )

    def o_copy(self, other):
        return remote(
            self.done,
            self.out.at[self.ctx],
            self.o_send.at[other],
            self.o_recv.at[other],
            {"ctx": lax.rem(self.ctx + other, 4)},
        )

    def own_out(self):
        return pltpu.make_async_copy(self.done, self.out.at[self.ctx], self.load.at[0])

    def add(self, total, other):
        def one(block, carry):
            both = total[block].astype(jnp.float32) + other[block].astype(jnp.float32)
            total[block] = both.astype(jnp.bfloat16)
            return carry

        lax.fori_loop(0, self.count, one, 0)

    def start(self):
        for copy in self.loads() + self.cores():
            copy.start()

    def after_core(self):
        loads, cores = self.loads(), self.cores()
        loads[0].wait()
        cores[0].wait_recv()
        self.add(self.far, self.got_far)

        def send(step, carry):
            self.x_copy(lax.rem(self.group + 1 + step, self.count)).start()
            return carry

        lax.fori_loop(0, self.count, send, 0)
        loads[1].wait()
        cores[1].wait_recv()
        self.add(self.near, self.got_near)
        cores[0].wait_send()
        cores[1].wait_send()

    def after_across(self):
        def one(step, carry):
            block = lax.rem(self.group + step, self.count)
            self.x_copy(block).wait()
            both = self.near[block].astype(jnp.float32) + self.got_across[block].astype(jnp.float32)
            self.near[block] = both.astype(jnp.bfloat16)
            self.g_copy(block, step).start()
            return carry

        lax.fori_loop(1, self.count, one, 0)
        self.x_copy(self.group).wait()

    def after_group(self):
        group = self.group
        total = self.near[group].astype(jnp.float32) + self.got_across[group].astype(jnp.float32)

        def one(step, total):
            self.g_copy(lax.rem(group + step, self.count), step).wait()
            return total + self.got_group[step].astype(jnp.float32)

        self.done[...] = lax.fori_loop(1, self.count, one, total).astype(jnp.bfloat16)
        self.own_out().start()
        for other in range(1, 4):
            self.o_copy(other).start()

    def finish(self):
        self.own_out().wait()
        for other in range(1, 4):
            self.o_copy(other).wait()


class VectorSum:
    SCRATCH = 9

    def __init__(self, ref, out, scratch, count):
        self.ref, self.out, self.count = ref, out, count
        self.total, self.got_ctx, self.got_group = scratch[:3]
        self.load, self.c_send, self.c_recv, self.g_send, self.g_recv = scratch[3:8]
        self.result = scratch[8]
        self.ctx, self.group, _, _ = places()

    @staticmethod
    def scratch(count, rows, width):
        return [
            pltpu.VMEM((rows, width), jnp.float32),
            pltpu.VMEM((4, rows, width), jnp.float32),
            pltpu.VMEM((count, rows, width), jnp.float32),
            DMA((2,)),
            DMA((4,)),
            DMA((4,)),
            DMA((count,)),
            DMA((count,)),
            pltpu.VMEM((rows, width), jnp.float32),
        ]

    def own(self):
        return pltpu.make_async_copy(self.ref, self.total, self.load.at[0])

    def own_out(self):
        return pltpu.make_async_copy(self.result, self.out, self.load.at[1])

    def c_copy(self, other):
        return remote(
            self.ref,
            self.got_ctx.at[other],
            self.c_send.at[other],
            self.c_recv.at[other],
            {"ctx": lax.rem(self.ctx + other, 4)},
        )

    def g_copy(self, step):
        return remote(
            self.total,
            self.got_group.at[step],
            self.g_send.at[step],
            self.g_recv.at[step],
            {"fsdp": lax.rem(self.group + step, self.count)},
        )

    def start(self):
        self.own().start()
        for other in range(1, 4):
            self.c_copy(other).start()

    def after_core(self):
        self.own().wait()
        total = self.total[...]
        for other in range(1, 4):
            self.c_copy(other).wait()
            total = total + self.got_ctx[other]
        self.total[...] = total

        def one(step, carry):
            self.g_copy(step).start()
            return carry

        lax.fori_loop(1, self.count, one, 0)

    def after_across(self):
        pass

    def after_group(self):
        def one(step, total):
            self.g_copy(step).wait()
            return total + self.got_group[step]

        self.result[...] = lax.fori_loop(1, self.count, one, self.total[...])
        self.own_out().start()

    def finish(self):
        self.own_out().wait()


def sums_kernel(*refs, kinds, count):
    parts = len(kinds)
    ins, outs, rest = refs[: parts + 1], refs[parts + 1 : 2 * parts + 2], refs[2 * parts + 2 :]
    jobs = [VectorSum(ins[parts], outs[parts], rest[: VectorSum.SCRATCH], count)]
    rest = rest[VectorSum.SCRATCH :]
    for index, kind in enumerate(kinds):
        own = rest[index * Sum.SCRATCH : (index + 1) * Sum.SCRATCH]
        jobs.append(Sum(kind, ins[index], outs[index], own, count))
    greet(count)
    for stage in STAGES:
        for job in jobs:
            getattr(job, stage)()


def sum_gradients(parts, kinds, vectors, rows, width, count):
    scratch = VectorSum.scratch(count, *vectors.shape)
    for _ in kinds:
        scratch += Sum.scratch(count, rows, width)
    return pl.pallas_call(
        functools.partial(sums_kernel, kinds=kinds, count=count),
        in_specs=[ANY] * (len(kinds) + 1),
        out_specs=[ANY] * (len(kinds) + 1),
        out_shape=[jax.ShapeDtypeStruct((4, rows, width), jnp.bfloat16)] * len(kinds)
        + [jax.ShapeDtypeStruct(vectors.shape, jnp.float32)],
        scratch_shapes=scratch,
        compiler_params=pltpu.CompilerParams(
            collective_id=1, has_side_effects=True, vmem_limit_bytes=VMEM_BYTES
        ),
        name="sum_gradients",
    )(*parts, vectors)


def on_device(
    hidden_in,
    lengths,
    seq_order,
    query_weight,
    query_bias,
    key_weight,
    value_weight,
    value_bias,
    output_weight,
    output_bias,
    norm1_gain,
    norm1_shift,
    inner_weight,
    inner_bias,
    outer_weight,
    outer_bias,
    norm2_gain,
    norm2_shift,
    cotangent,
):
    width = hidden_in.shape[2]
    count = lax.axis_size("fsdp")
    group = lax.axis_index("fsdp")
    shard = query_bias.shape[0]
    low = jnp.bfloat16
    placed = jnp.swapaxes(jnp.take(hidden_in, seq_order, axis=1), 0, 1)
    vectors = jnp.concatenate(
        (
            jnp.stack(
                (
                    query_bias,
                    value_bias,
                    output_bias,
                    norm1_gain,
                    norm1_shift,
                    outer_bias,
                    norm2_gain,
                    norm2_shift,
                )
            ),
            inner_bias.reshape(4, shard),
        )
    )
    vectors = jnp.pad(vectors, ((0, 4), (0, 128 - shard)))
    weights = jnp.stack((query_weight, key_weight, value_weight, output_weight))
    tokens, weights, vectors = bring_in(placed, weights, vectors)
    w_inner = lax.all_gather(inner_weight, "fsdp", axis=0, tiled=True)
    w_outer = lax.all_gather(outer_weight, "fsdp", axis=0, tiled=True)
    w_query, w_key, w_value, w_output = (weights[i].reshape(width, width) for i in range(4))
    vectors = vectors[:, :12, :shard].astype(jnp.float32)
    b_query, b_value, b_output, gain_one, shift_one, b_outer, gain_two, shift_two = (
        vectors[:, i].reshape(width) for i in range(8)
    )
    b_inner = vectors[:, 8:].reshape(-1)
    limits = jnp.take(lengths, jnp.take(seq_order, group[None]))
    all_rows = tokens.reshape(-1, width)
    local_len = all_rows.shape[0] // 4
    token_rows = lax.dynamic_index_in_dim(tokens, lax.axis_index("ctx"), 0, False)
    token_rows = token_rows.reshape(local_len, width)
    queries = (product(token_rows, w_query, ((1,), (0,))) + b_query).astype(low)
    keys = product(all_rows, w_key, ((1,), (0,))).astype(low)
    values = (product(all_rows, w_value, ((1,), (0,))) + b_value).astype(low)
    attended, lse = attend_forward(queries, keys, values, limits)
    mixed_low = attended.astype(low)
    branch = product(mixed_low, w_output, ((1,), (0,))) + b_output
    normed, unit_one, scale_one = norm_forward(
        token_rows.astype(jnp.float32) + branch, gain_one, shift_one
    )
    normed_low = normed.astype(low)
    inner_pre = product(normed_low, w_inner, ((1,), (0,))) + b_inner
    activated = gelu_exact(inner_pre).astype(low)
    outer_out = product(activated, w_outer, ((1,), (0,))) + b_outer
    second, unit_two, scale_two = norm_forward(normed + outer_out, gain_two, shift_two)
    layer_out = second.astype(low).reshape(local_len, 1, width)
    upstream = cotangent.reshape(local_len, width).astype(jnp.float32)
    d_second, grad_gain_two, grad_shift_two = norm_backward(upstream, unit_two, scale_two, gain_two)
    d_outer = d_second.astype(low)
    grad_outer_w = product(activated, d_outer, ((0,), (0,))).astype(low)
    grad_outer_b = jnp.sum(d_outer.astype(jnp.float32), axis=0)
    inner_grad = product(d_outer, w_outer, ((1,), (1,)))
    d_inner = (inner_grad * gelu_slope(inner_pre)).astype(low)
    grad_inner_w = product(normed_low, d_inner, ((0,), (0,))).astype(low)
    grad_inner_b = jnp.sum(d_inner.astype(jnp.float32), axis=0)
    d_normed = d_second + product(d_inner, w_inner, ((1,), (1,)))
    d_res, grad_gain_one, grad_shift_one = norm_backward(d_normed, unit_one, scale_one, gain_one)
    d_branch = d_res.astype(low)
    grad_output_w = product(mixed_low, d_branch, ((0,), (0,))).astype(low)
    grad_output_b = jnp.sum(d_branch.astype(jnp.float32), axis=0)
    d_mixed = product(d_branch, w_output, ((1,), (1,))).astype(low)
    d_query, key_terms, value_terms = attend_backward(
        queries, keys, values, limits, d_mixed, attended, lse
    )
    d_keys = lax.psum_scatter(key_terms, "ctx", scatter_dimension=0, tiled=True)
    d_values = lax.psum_scatter(value_terms, "ctx", scatter_dimension=0, tiled=True)
    grad_query_w = product(token_rows, d_query, ((0,), (0,))).astype(low)
    grad_query_b = jnp.sum(d_query.astype(jnp.float32), axis=0)
    grad_key_w = product(token_rows, d_keys, ((0,), (0,))).astype(low)
    grad_value_w = product(token_rows, d_values, ((0,), (0,))).astype(low)
    grad_value_b = jnp.sum(d_values.astype(jnp.float32), axis=0)
    d_placed = d_res + product(d_query, w_query, ((1,), (1,)))
    d_placed = d_placed + product(d_keys, w_key, ((1,), (1,)))
    d_placed = d_placed + product(d_values, w_value, ((1,), (1,)))
    back_rows = d_placed.astype(low).reshape(count, local_len // count, width)
    returned = lax.all_to_all(back_rows, "fsdp", split_axis=0, concat_axis=0, tiled=True)
    inverse = jnp.argmax(seq_order[:, None] == jnp.arange(count), axis=0)
    grad_in = jnp.take(jnp.swapaxes(returned, 0, 1), inverse, axis=1)
    attention_w = jnp.stack((grad_query_w, grad_key_w, grad_value_w, grad_output_w))
    small_sums = jnp.concatenate(
        (
            jnp.stack(
                (
                    grad_query_b,
                    grad_value_b,
                    grad_output_b,
                    grad_gain_one,
                    grad_shift_one,
                    grad_outer_b,
                    grad_gain_two,
                    grad_shift_two,
                )
            ),
            grad_inner_b.reshape(4, width),
            jnp.zeros((4, width), jnp.float32),
        )
    )
    attention_w, inner_w, outer_w, small_sums = sum_gradients(
        (
            attention_w.reshape(4, count, shard, width),
            grad_inner_w.reshape(count, shard, 4 * width),
            grad_outer_w.reshape(count, 4, shard, width),
        ),
        (0, 1, 2),
        small_sums,
        shard,
        width,
        count,
    )
    attention_w = attention_w.astype(jnp.float32)
    inner_w = jnp.swapaxes(inner_w, 0, 1).reshape(shard, 4 * width).astype(jnp.float32)
    outer_w = outer_w.reshape(4 * shard, width).astype(jnp.float32)
    small = lax.dynamic_slice_in_dim(small_sums[:8], group * shard, shard, axis=1)
    inner_b = lax.dynamic_slice_in_dim(
        small_sums[8:12].reshape(-1), group * 4 * shard, 4 * shard, axis=0
    )
    return (
        layer_out,
        grad_in,
        attention_w[0],
        small[0],
        attention_w[1],
        attention_w[2],
        small[1],
        attention_w[3],
        small[2],
        small[3],
        small[4],
        inner_w,
        inner_b,
        outer_w,
        small[5],
        small[6],
        small[7],
    )


def solution(mesh):
    placed = (
        P(("ctx", "fsdp"), None, None),
        P(),
        P(),
        P("fsdp", None),
        P("fsdp"),
        P("fsdp", None),
        P("fsdp", None),
        P("fsdp"),
        P("fsdp", None),
        P("fsdp"),
        P("fsdp"),
        P("fsdp"),
        P("fsdp", None),
        P("fsdp"),
        P("fsdp", None),
        P("fsdp"),
        P("fsdp"),
        P("fsdp"),
        P("ctx", "fsdp", None),
    )
    return jax.shard_map(
        on_device,
        mesh=mesh,
        in_specs=placed,
        out_specs=(
            P("ctx", "fsdp", None),
            P(("ctx", "fsdp"), None, None),
            P("fsdp", None),
            P("fsdp"),
            P("fsdp", None),
            P("fsdp", None),
            P("fsdp"),
            P("fsdp", None),
            P("fsdp"),
            P("fsdp"),
            P("fsdp"),
            P("fsdp", None),
            P("fsdp"),
            P("fsdp", None),
            P("fsdp"),
            P("fsdp"),
            P("fsdp"),
        ),
        check_vma=False,
    )
```

```python
import functools

import jax
import jax.numpy as jnp
from jax import lax
from jax.experimental import pallas as pl
from jax.experimental.pallas import tpu as pltpu
from jax.sharding import PartitionSpec as P

SCALE = 64 ** (-0.5)
LOG2E = 1.4426950408889634
FORWARD_KEYS = 2048
VMEM_BYTES = 60 * 2**20

NORM_EPSILON = 1e-12
NEG_BIG = -1e30
ROOT_HALF = 0.7071067811865476
ROOT_TWO_PI = 2.5066282746310002


def norm_forward(source, gain_vec, shift_vec):
    centre = source - jnp.mean(source, axis=-1, keepdims=True)
    inv_scale = lax.rsqrt(jnp.mean(centre * centre, axis=-1, keepdims=True) + NORM_EPSILON)
    unit_rows = centre * inv_scale
    return (unit_rows * gain_vec + shift_vec, unit_rows, inv_scale)


def norm_backward(upstream, unit_rows, inv_scale, gain_vec):
    scaled = upstream * gain_vec
    plain_mean = jnp.mean(scaled, axis=-1, keepdims=True)
    cross_mean = jnp.mean(scaled * unit_rows, axis=-1, keepdims=True)
    d_source = inv_scale * (scaled - plain_mean - unit_rows * cross_mean)
    return (d_source, jnp.sum(upstream * unit_rows, axis=0), jnp.sum(upstream, axis=0))


def gelu_exact(source):
    return 0.5 * source * (1.0 + jax.scipy.special.erf(source * ROOT_HALF))


def gelu_slope(source):
    return (
        0.5 * (1.0 + jax.scipy.special.erf(source * ROOT_HALF))
        + source * jnp.exp(-0.5 * source * source) / ROOT_TWO_PI
    )


def product(left, right, dims):
    return lax.dot_general(left, right, (dims, ((), ())), preferred_element_type=jnp.float32)


def lane_is_low():
    return lax.broadcasted_iota(jnp.int32, (1, 128), 1) < 64


def split_query(query_pair, low_half):
    scaled = query_pair * (SCALE * LOG2E)
    high = scaled.astype(jnp.bfloat16).astype(jnp.float32)
    rest = pltpu.roll(scaled - high, 64, 1)
    return (
        jnp.where(low_half, high, rest).astype(jnp.bfloat16),
        jnp.where(low_half, rest, high).astype(jnp.bfloat16),
    )


def twice(pair, low_half):
    other = pltpu.roll(pair, 64, 1)
    return (
        jnp.where(low_half, pair, other).astype(jnp.bfloat16),
        jnp.where(low_half, other, pair).astype(jnp.bfloat16),
    )


def forward_kernel(limit_ref, query_ref, key_ref, value_ref, attended_ref, lse_ref, *, key_rows):
    low_half = lane_is_low()
    limit = limit_ref[0]
    queries = split_query(query_ref[...].astype(jnp.float32), low_half)
    query_rows = query_ref.shape[0]

    def step(tile, state):
        start = pl.multiple_of(tile * key_rows, key_rows)
        usable = start + lax.broadcasted_iota(jnp.int32, (key_rows, 1), 0) < limit
        key_tile = key_ref[pl.ds(start, key_rows), :].astype(jnp.float32)
        keys = twice(jnp.where(usable, key_tile, key_ref[0:1, :].astype(jnp.float32)), low_half)
        value_tile = value_ref[pl.ds(start, key_rows), :].astype(jnp.float32)
        value_tile = jnp.where(usable, value_tile, 0.0)
        count = jnp.where(usable, 1.0, 0.0)
        values = (
            jnp.where(low_half, value_tile, count).astype(jnp.bfloat16),
            jnp.where(low_half, count, value_tile).astype(jnp.bfloat16),
        )
        fresh = []
        for head in range(2):
            top, total = state[head]
            scores = product(queries[head], keys[head], ((1,), (1,)))
            new_top = jnp.maximum(top, jnp.max(scores, axis=1, keepdims=True))
            weights = jnp.exp2(scores - new_top).astype(jnp.bfloat16)
            total = total * jnp.exp2(top - new_top) + product(weights, values[head], ((1,), (0,)))
            fresh.append((new_top, total))
        return tuple(fresh)

    empty = (
        jnp.full((query_rows, 1), NEG_BIG, jnp.float32),
        jnp.zeros((query_rows, 128), jnp.float32),
    )
    (top_a, total_a), (top_b, total_b) = lax.fori_loop(
        0, key_ref.shape[0] // key_rows, step, (empty, empty)
    )
    mass_a, mass_b = total_a[:, 64:65], total_b[:, 0:1]
    attended_ref[...] = jnp.where(low_half, total_a / mass_a, total_b / mass_b)
    lse = jnp.where(low_half, top_a + jnp.log2(mass_a), top_b + jnp.log2(mass_b)).T
    lse_ref[0, 0:1, :] = lse[0:1, :]
    lse_ref[0, 1:2, :] = lse[64:65, :]


def attend_forward(queries, keys, values, limit):
    rows, width = queries.shape
    full = keys.shape[0]
    pairs = width // 128
    row_spec = pl.BlockSpec((rows, 128), lambda pair, *_: (0, pair))
    return pl.pallas_call(
        functools.partial(forward_kernel, key_rows=FORWARD_KEYS),
        grid_spec=pltpu.PrefetchScalarGridSpec(
            num_scalar_prefetch=1,
            grid=(pairs,),
            in_specs=[
                row_spec,
                pl.BlockSpec((full, 128), lambda pair, *_: (0, pair)),
                pl.BlockSpec((full, 128), lambda pair, *_: (0, pair)),
            ],
            out_specs=[row_spec, pl.BlockSpec((1, 2, rows), lambda pair, *_: (pair, 0, 0))],
        ),
        out_shape=[
            jax.ShapeDtypeStruct((rows, width), jnp.float32),
            jax.ShapeDtypeStruct((pairs, 2, rows), jnp.float32),
        ],
        compiler_params=pltpu.CompilerParams(vmem_limit_bytes=VMEM_BYTES),
        cost_estimate=pl.CostEstimate(
            flops=16 * rows * full * width, bytes_accessed=20_000_000, transcendentals=0
        ),
        name="attend_forward",
    )(limit, queries, keys, values)


MESH = pl.DeviceIdType.MESH
DMA = pltpu.SemaphoreType.DMA
ANY = pl.BlockSpec(memory_space=pl.ANY)
STAGES = ("start", "after_core", "after_across", "after_group", "finish")


def places():
    ctx, group = lax.axis_index("ctx"), lax.axis_index("fsdp")
    return ctx, group, lax.rem(ctx + 2, 4), ctx + 1 - 2 * lax.rem(ctx, 2)


def remote(source, target, send_sem, recv_sem, where):
    return pltpu.make_async_remote_copy(
        src_ref=source,
        dst_ref=target,
        send_sem=send_sem,
        recv_sem=recv_sem,
        device_id=where,
        device_id_type=MESH,
    )


def greet(count):
    ctx, group, _, _ = places()
    barrier = pltpu.get_barrier_semaphore()

    def one(step, carry):
        pl.semaphore_signal(
            barrier,
            inc=1,
            device_id={"fsdp": lax.rem(group + step, count)},
            device_id_type=MESH,
        )
        return carry

    lax.fori_loop(1, count, one, 0)
    for other in range(1, 4):
        pl.semaphore_signal(
            barrier, inc=1, device_id={"ctx": lax.rem(ctx + other, 4)}, device_id_type=MESH
        )
    pl.semaphore_wait(barrier, count - 1 + 3)


def arrival_kernel(
    placed,
    weights,
    small,
    tokens,
    gathered,
    small_all,
    tok_stage,
    w_stage,
    small_stage,
    local_sem,
    tok_send,
    tok_recv,
    w_send,
    w_recv,
    small_send,
    small_recv,
    x_send,
    x_recv,
    s_send,
    s_recv,
    r_send,
    r_recv,
    *,
    count,
):
    ctx, group, across, sibling = places()
    own_tok = pltpu.make_async_copy(placed.at[group], tok_stage, local_sem.at[0])
    own_w = pltpu.make_async_copy(weights.at[ctx], w_stage, local_sem.at[1])
    own_small = pltpu.make_async_copy(small, small_stage, local_sem.at[2])
    own_tok.start()
    own_w.start()
    own_small.start()
    greet(count)

    def tok_copy(peer, step):
        return remote(
            placed.at[peer],
            tokens.at[ctx, group],
            tok_send.at[step],
            tok_recv.at[step],
            {"fsdp": peer},
        )

    def w_copy(peer, step):
        return remote(
            weights.at[ctx],
            gathered.at[ctx, group],
            w_send.at[step],
            w_recv.at[step],
            {"fsdp": peer},
        )

    def small_copy(peer, step):
        return remote(
            small, small_all.at[group], small_send.at[step], small_recv.at[step], {"fsdp": peer}
        )

    def send(step, carry):
        peer = lax.rem(group + step, count)
        w_copy(peer, step).start()
        tok_copy(peer, step).start()
        small_copy(peer, step).start()
        return carry

    lax.fori_loop(1, count, send, 0)
    own_tok.wait()
    own_w.wait()
    own_small.wait()
    put_tok = pltpu.make_async_copy(tok_stage, tokens.at[ctx, group], local_sem.at[0])
    put_w = pltpu.make_async_copy(w_stage, gathered.at[ctx, group], local_sem.at[1])
    put_small = pltpu.make_async_copy(small_stage, small_all.at[group], local_sem.at[2])
    put_tok.start()
    put_w.start()
    put_small.start()

    def across_copy(kind, block):
        where = gathered if kind == 0 else tokens
        return remote(
            where.at[ctx, block],
            where.at[ctx, block],
            x_send.at[kind, block],
            x_recv.at[kind, block],
            {"ctx": across},
        )

    def sibling_copy(kind, block):
        where = gathered if kind == 0 else tokens
        return remote(
            where.at[ctx, block],
            where.at[ctx, block],
            s_send.at[kind, block],
            s_recv.at[kind, block],
            {"ctx": sibling},
        )

    def relay_copy(kind, block):
        where = gathered if kind == 0 else tokens
        return remote(
            where.at[across, block],
            where.at[across, block],
            r_send.at[kind, block],
            r_recv.at[kind, block],
            {"ctx": sibling},
        )

    put_w.wait()
    across_copy(0, group).start()
    sibling_copy(0, group).start()
    put_tok.wait()
    across_copy(1, group).start()
    sibling_copy(1, group).start()
    put_small.wait()

    def arrive(step, carry):
        origin = lax.rem(group - step + count, count)
        w_copy(origin, step).wait_recv()
        across_copy(0, origin).start()
        sibling_copy(0, origin).start()
        tok_copy(origin, step).wait_recv()
        across_copy(1, origin).start()
        sibling_copy(1, origin).start()
        return carry

    lax.fori_loop(1, count, arrive, 0)

    def passed(step, carry):
        origin = lax.rem(group - step + count, count)
        for kind in range(2):
            across_copy(kind, origin).wait_recv()
            relay_copy(kind, origin).start()
        return carry

    lax.fori_loop(0, count, passed, 0)

    def finish(step, carry):
        origin = lax.rem(group - step + count, count)
        for kind in range(2):
            across_copy(kind, origin).wait_send()
            sibling_copy(kind, origin).wait()
            relay_copy(kind, origin).wait()
        return carry

    lax.fori_loop(0, count, finish, 0)

    def sent(step, carry):
        peer = lax.rem(group + step, count)
        w_copy(peer, step).wait_send()
        tok_copy(peer, step).wait_send()
        small_copy(peer, step).wait()
        return carry

    lax.fori_loop(1, count, sent, 0)


def bring_in(placed, weights, small):
    count, rows, width = placed.shape
    return pl.pallas_call(
        functools.partial(arrival_kernel, count=count),
        in_specs=[ANY] * 3,
        out_specs=[ANY] * 3,
        out_shape=[
            jax.ShapeDtypeStruct((4, count, rows, width), jnp.bfloat16),
            jax.ShapeDtypeStruct((4, count) + weights.shape[1:], jnp.bfloat16),
            jax.ShapeDtypeStruct((count,) + small.shape, jnp.bfloat16),
        ],
        scratch_shapes=[
            pltpu.VMEM((rows, width), jnp.bfloat16),
            pltpu.VMEM(weights.shape[1:], jnp.bfloat16),
            pltpu.VMEM(small.shape, jnp.bfloat16),
            DMA((3,)),
        ]
        + [DMA((count,))] * 6
        + [DMA((2, count))] * 6,
        compiler_params=pltpu.CompilerParams(
            collective_id=0, has_side_effects=True, vmem_limit_bytes=8 * 2**20
        ),
        name="bring_in",
    )(placed, weights, small)


class Sum:
    SCRATCH = 16

    def __init__(self, kind, ref, out, scratch, count):
        self.kind, self.ref, self.out, self.count = kind, ref, out, count
        self.near, self.far, self.got_near, self.got_far = scratch[:4]
        self.got_across, self.got_group, self.done = scratch[4:7]
        self.load, self.c_send, self.c_recv, self.x_send, self.x_recv = scratch[7:12]
        self.g_send, self.g_recv, self.o_send, self.o_recv = scratch[12:16]
        self.ctx, self.group, self.across, self.sibling = places()
        self.width = self.near.shape[-1]

    @staticmethod
    def scratch(count, rows, width):
        return (
            [pltpu.VMEM((count, rows, width), jnp.bfloat16)] * 6
            + [pltpu.VMEM((rows, width), jnp.bfloat16)]
            + [DMA((2,))] * 3
            + [DMA((count,))] * 4
            + [DMA((4,))] * 2
        )

    def quarter(self, index):
        if self.kind == 0:
            return self.ref.at[index]
        if self.kind == 1:
            start = pl.multiple_of(index * self.width, self.width)
            return self.ref.at[:, :, pl.ds(start, self.width)]
        return self.ref.at[:, index]

    def loads(self):
        return (
            pltpu.make_async_copy(self.quarter(self.across), self.far, self.load.at[0]),
            pltpu.make_async_copy(self.quarter(self.ctx), self.near, self.load.at[1]),
        )

    def cores(self):
        beyond = lax.rem(self.sibling + 2, 4)
        there = {"ctx": self.sibling}
        return (
            remote(self.quarter(beyond), self.got_far, self.c_send.at[0], self.c_recv.at[0], there),
            remote(
                self.quarter(self.sibling),
                self.got_near,
                self.c_send.at[1],
                self.c_recv.at[1],
                there,
            ),
        )

    def x_copy(self, block):
        return remote(
            self.far.at[block],
            self.got_across.at[block],
            self.x_send.at[block],
            self.x_recv.at[block],
            {"ctx": self.across},
        )

    def g_copy(self, peer, step):
        return remote(
            self.near.at[peer],
            self.got_group.at[step],
            self.g_send.at[step],
            self.g_recv.at[step],
            {"fsdp": peer},
        )

    def o_copy(self, other):
        return remote(
            self.done,
            self.out.at[self.ctx],
            self.o_send.at[other],
            self.o_recv.at[other],
            {"ctx": lax.rem(self.ctx + other, 4)},
        )

    def own_out(self):
        return pltpu.make_async_copy(self.done, self.out.at[self.ctx], self.load.at[0])

    def add(self, total, other):
        def one(block, carry):
            both = total[block].astype(jnp.float32) + other[block].astype(jnp.float32)
            total[block] = both.astype(jnp.bfloat16)
            return carry

        lax.fori_loop(0, self.count, one, 0)

    def start(self):
        for copy in self.loads() + self.cores():
            copy.start()

    def after_core(self):
        loads, cores = self.loads(), self.cores()
        loads[0].wait()
        cores[0].wait_recv()
        self.add(self.far, self.got_far)

        def send(step, carry):
            self.x_copy(lax.rem(self.group + 1 + step, self.count)).start()
            return carry

        lax.fori_loop(0, self.count, send, 0)
        loads[1].wait()
        cores[1].wait_recv()
        self.add(self.near, self.got_near)
        cores[0].wait_send()
        cores[1].wait_send()

    def after_across(self):
        def one(step, carry):
            block = lax.rem(self.group + step, self.count)
            self.x_copy(block).wait()
            both = self.near[block].astype(jnp.float32) + self.got_across[block].astype(jnp.float32)
            self.near[block] = both.astype(jnp.bfloat16)
            self.g_copy(block, step).start()
            return carry

        lax.fori_loop(1, self.count, one, 0)
        self.x_copy(self.group).wait()

    def after_group(self):
        group = self.group
        total = self.near[group].astype(jnp.float32) + self.got_across[group].astype(jnp.float32)

        def one(step, total):
            self.g_copy(lax.rem(group + step, self.count), step).wait()
            return total + self.got_group[step].astype(jnp.float32)

        self.done[...] = lax.fori_loop(1, self.count, one, total).astype(jnp.bfloat16)
        self.own_out().start()
        for other in range(1, 4):
            self.o_copy(other).start()

    def finish(self):
        self.own_out().wait()
        for other in range(1, 4):
            self.o_copy(other).wait()


class VectorSum:
    SCRATCH = 9

    def __init__(self, ref, out, scratch, count):
        self.ref, self.out, self.count = ref, out, count
        self.total, self.got_ctx, self.got_group = scratch[:3]
        self.load, self.c_send, self.c_recv, self.g_send, self.g_recv = scratch[3:8]
        self.result = scratch[8]
        self.ctx, self.group, _, _ = places()

    @staticmethod
    def scratch(count, rows, width):
        return [
            pltpu.VMEM((rows, width), jnp.float32),
            pltpu.VMEM((4, rows, width), jnp.float32),
            pltpu.VMEM((count, rows, width), jnp.float32),
            DMA((2,)),
            DMA((4,)),
            DMA((4,)),
            DMA((count,)),
            DMA((count,)),
            pltpu.VMEM((rows, width), jnp.float32),
        ]

    def own(self):
        return pltpu.make_async_copy(self.ref, self.total, self.load.at[0])

    def own_out(self):
        return pltpu.make_async_copy(self.result, self.out, self.load.at[1])

    def c_copy(self, other):
        return remote(
            self.ref,
            self.got_ctx.at[other],
            self.c_send.at[other],
            self.c_recv.at[other],
            {"ctx": lax.rem(self.ctx + other, 4)},
        )

    def g_copy(self, step):
        return remote(
            self.total,
            self.got_group.at[step],
            self.g_send.at[step],
            self.g_recv.at[step],
            {"fsdp": lax.rem(self.group + step, self.count)},
        )

    def start(self):
        self.own().start()
        for other in range(1, 4):
            self.c_copy(other).start()

    def after_core(self):
        self.own().wait()
        total = self.total[...]
        for other in range(1, 4):
            self.c_copy(other).wait()
            total = total + self.got_ctx[other]
        self.total[...] = total

        def one(step, carry):
            self.g_copy(step).start()
            return carry

        lax.fori_loop(1, self.count, one, 0)

    def after_across(self):
        pass

    def after_group(self):
        def one(step, total):
            self.g_copy(step).wait()
            return total + self.got_group[step]

        self.result[...] = lax.fori_loop(1, self.count, one, self.total[...])
        self.own_out().start()

    def finish(self):
        self.own_out().wait()


class LateSum:
    SCRATCH = 16

    def __init__(self, kind, ref, out, scratch, count):
        self.kind, self.ref, self.out, self.count = kind, ref, out, count
        self.near, self.got, self.got_group, self.half, self.got_across, self.done = scratch[:6]
        self.load, self.c_send, self.c_recv, self.g_send, self.g_recv = scratch[6:11]
        self.x_send, self.x_recv, self.o_send, self.o_recv, self.put = scratch[11:16]
        self.ctx, self.group, self.across, self.sibling = places()
        self.core = lax.rem(self.ctx, 2)
        self.width = self.near.shape[-1]

    @staticmethod
    def scratch(count, rows, width):
        return (
            [pltpu.VMEM((count, 2, rows, width), jnp.bfloat16)] * 3
            + [pltpu.VMEM((2, rows, width), jnp.bfloat16)] * 3
            + [DMA((2,))] * 3
            + [DMA((count,))] * 2
            + [DMA((2,))] * 5
        )

    def quarter(self, index):
        if self.kind == 1:
            start = pl.multiple_of(index * self.width, self.width)
            return self.ref.at[:, :, pl.ds(start, self.width)]
        return self.ref.at[:, index]

    def load_copy(self, half):
        return pltpu.make_async_copy(
            self.quarter(2 * half + self.core), self.near.at[:, half], self.load.at[half]
        )

    def core_copy(self, half):
        return remote(
            self.quarter(2 * half + 1 - self.core),
            self.got.at[:, half],
            self.c_send.at[half],
            self.c_recv.at[half],
            {"ctx": self.sibling},
        )

    def group_copy(self, step):
        peer = lax.rem(self.group + step, self.count)
        return remote(
            self.near.at[peer],
            self.got_group.at[step],
            self.g_send.at[step],
            self.g_recv.at[step],
            {"fsdp": peer},
        )

    def x_copy(self):
        return remote(
            self.half, self.got_across, self.x_send.at[0], self.x_recv.at[0], {"ctx": self.across}
        )

    def out_copy(self, half):
        return remote(
            self.done.at[half],
            self.out.at[2 * half + self.core],
            self.o_send.at[half],
            self.o_recv.at[half],
            {"ctx": self.sibling},
        )

    def own_out(self, half):
        return pltpu.make_async_copy(
            self.done.at[half], self.out.at[2 * half + self.core], self.put.at[half]
        )

    def start(self):
        for half in range(2):
            self.load_copy(half).start()
            self.core_copy(half).start()

    def after_core(self):
        for half in range(2):
            self.load_copy(half).wait()
            self.core_copy(half).wait()

        def one(step, carry):
            block = lax.rem(self.group + step, self.count)
            both = self.near[block].astype(jnp.float32) + self.got[block].astype(jnp.float32)
            self.near[block] = both.astype(jnp.bfloat16)
            return carry

        lax.fori_loop(0, self.count, one, 0)

        def send(step, carry):
            self.group_copy(step).start()
            return carry

        lax.fori_loop(1, self.count, send, 0)

    def after_group(self):
        def one(step, total):
            self.group_copy(step).wait()
            return total + self.got_group[step].astype(jnp.float32)

        total = lax.fori_loop(1, self.count, one, self.near[self.group].astype(jnp.float32))
        self.half[...] = total.astype(jnp.bfloat16)
        self.x_copy().start()

    def after_across(self):
        self.x_copy().wait()
        both = self.half[...].astype(jnp.float32) + self.got_across[...].astype(jnp.float32)
        self.done[...] = both.astype(jnp.bfloat16)
        for half in range(2):
            self.own_out(half).start()
            self.out_copy(half).start()

    def finish(self):
        for half in range(2):
            self.own_out(half).wait()
            self.out_copy(half).wait()


def sums_kernel(*refs, kinds, count):
    parts = len(kinds)
    ins, outs, rest = refs[: parts + 1], refs[parts + 1 : 2 * parts + 2], refs[2 * parts + 2 :]
    jobs = [VectorSum(ins[parts], outs[parts], rest[: VectorSum.SCRATCH], count)]
    rest = rest[VectorSum.SCRATCH :]
    for index, kind in enumerate(kinds):
        own = rest[index * Sum.SCRATCH : (index + 1) * Sum.SCRATCH]
        jobs.append(Sum(kind, ins[index], outs[index], own, count))
    greet(count)
    for stage in STAGES:
        for job in jobs:
            getattr(job, stage)()


def sum_gradients(parts, kinds, vectors, rows, width, count):
    scratch = VectorSum.scratch(count, *vectors.shape)
    for _ in kinds:
        scratch += Sum.scratch(count, rows, width)
    return pl.pallas_call(
        functools.partial(sums_kernel, kinds=kinds, count=count),
        in_specs=[ANY] * (len(kinds) + 1),
        out_specs=[ANY] * (len(kinds) + 1),
        out_shape=[jax.ShapeDtypeStruct((4, rows, width), jnp.bfloat16)] * len(kinds)
        + [jax.ShapeDtypeStruct(vectors.shape, jnp.float32)],
        scratch_shapes=scratch,
        compiler_params=pltpu.CompilerParams(
            collective_id=1, has_side_effects=True, vmem_limit_bytes=VMEM_BYTES
        ),
        name="sum_gradients",
    )(*parts, vectors)


def backward_kernel(
    limit_ref,
    query_ref,
    key_ref,
    value_ref,
    grad_ref,
    attended_ref,
    lse_ref,
    inner_ref,
    outer_ref,
    d_query_ref,
    d_key_ref,
    d_value_ref,
    inner_out,
    outer_out,
    query_sum,
    part,
    got_core,
    far,
    near,
    got_x,
    core_send,
    core_recv,
    x_send,
    x_recv,
    *rest,
    count,
):
    pair = pl.program_id(0)
    pairs = pl.num_programs(0) - 1
    slot = lax.rem(pair, 2)
    ctx, _, across, sibling = places()
    key_rows = query_ref.shape[0]
    jobs = [
        LateSum(1, inner_ref, inner_out, rest[: LateSum.SCRATCH], count),
        LateSum(2, outer_ref, outer_out, rest[LateSum.SCRATCH :], count),
    ]

    def core_copy(which):
        return remote(
            part.at[which],
            got_core.at[slot, which],
            core_send.at[which],
            core_recv.at[slot, which],
            {"ctx": sibling},
        )

    def x_copy(where):
        return remote(
            far.at[where], got_x.at[where], x_send.at[where], x_recv.at[where], {"ctx": across}
        )

    def settle():
        where = 1 - slot
        x_copy(where).wait()
        for kind, ref in enumerate((d_key_ref, d_value_ref)):
            both = near[where, kind].astype(jnp.float32) + got_x[where, kind].astype(jnp.float32)
            ref[...] = both.astype(jnp.bfloat16)

    @pl.when(pair == 0)
    def _():
        greet(count)
        for job in jobs:
            job.start()

    @pl.when(pair == 1)
    def _():
        for job in jobs:
            job.after_core()

    @pl.when(pair < pairs)
    def _():
        low_half = lane_is_low()
        high_half = jnp.logical_not(low_half)
        lane = lax.broadcasted_iota(jnp.int32, (1, 128), 1)
        limit = limit_ref[0]
        query_pair = query_ref[...].astype(jnp.float32)
        queries = split_query(query_pair, low_half)
        scaled = query_pair * SCALE
        grad_pair = grad_ref[...].astype(jnp.float32)
        overlap = grad_pair * attended_ref[...]
        own_query, own_grad, joined_grad = [], [], []
        for head in range(2):
            mine = low_half if head == 0 else high_half
            own_query.append(jnp.where(mine, scaled, 0.0).astype(jnp.bfloat16))
            own_grad.append(jnp.where(mine, grad_pair, 0.0).astype(jnp.bfloat16))
            delta = -jnp.sum(jnp.where(mine, overlap, 0.0), axis=1, keepdims=True)
            first = delta.astype(jnp.bfloat16).astype(jnp.float32)
            second = (delta - first).astype(jnp.bfloat16).astype(jnp.float32)
            third = delta - first - second
            spare = 64 * (1 - head)
            joined = jnp.where(lane == spare + 2, third, 0.0)
            joined = jnp.where(lane == spare + 1, second, joined)
            joined = jnp.where(lane == spare, first, joined)
            joined_grad.append(jnp.where(mine, grad_pair, joined).astype(jnp.bfloat16))
        query_sum[...] = jnp.zeros_like(query_sum)

        def step(tile, carry):
            odd = lax.rem(tile, 2)
            quarter = lax.rem(sibling + odd * (ctx - sibling) + 2 * (1 - tile // 2), 4)
            start = pl.multiple_of(quarter * key_rows, key_rows)
            usable = start + lax.broadcasted_iota(jnp.int32, (key_rows, 1), 0) < limit
            key_tile = key_ref[pl.ds(start, key_rows), :].astype(jnp.float32)
            value_tile = value_ref[pl.ds(start, key_rows), :].astype(jnp.float32)
            keys = twice(jnp.where(usable, key_tile, key_ref[0:1, :].astype(jnp.float32)), low_half)
            own_tile = jnp.where(usable, key_tile * SCALE, 0.0)
            key_piece = value_piece = None
            for head in range(2):
                mine = low_half if head == 0 else high_half
                values = jnp.where(mine, value_tile, 1.0).astype(jnp.bfloat16)
                own_key = jnp.where(mine, own_tile, 0.0).astype(jnp.bfloat16)
                scores = product(keys[head], queries[head], ((1,), (1,)))
                probs = jnp.exp2(scores - lse_ref[0, head : head + 1, :])
                slopes = product(values, joined_grad[head], ((1,), (1,)))
                score_grads = (probs * slopes).astype(jnp.bfloat16)
                value_term = product(probs.astype(jnp.bfloat16), own_grad[head], ((1,), (0,)))
                key_term = product(score_grads, own_query[head], ((1,), (0,)))
                value_piece = value_term if value_piece is None else value_piece + value_term
                key_piece = key_term if key_piece is None else key_piece + key_term
                query_sum[...] += product(own_key, score_grads, ((0,), (0,)))
            pieces = (jnp.where(usable, key_piece, 0.0), jnp.where(usable, value_piece, 0.0))

            @pl.when(odd == 0)
            def _():
                which = tile // 2
                for kind in range(2):
                    part[which, kind] = pieces[kind].astype(jnp.bfloat16)
                core_copy(which).start()

            @pl.when(tile == 1)
            def _():
                @pl.when(pair > 0)
                def _():
                    settle()

                core_copy(0).wait_recv()
                for kind in range(2):
                    both = pieces[kind] + got_core[slot, 0, kind].astype(jnp.float32)
                    far[slot, kind] = both.astype(jnp.bfloat16)
                x_copy(slot).start()

            @pl.when(tile == 3)
            def _():
                core_copy(1).wait_recv()
                for kind in range(2):
                    both = pieces[kind] + got_core[slot, 1, kind].astype(jnp.float32)
                    near[slot, kind] = both.astype(jnp.bfloat16)
                core_copy(0).wait_send()
                core_copy(1).wait_send()

            return carry

        lax.fori_loop(0, 4, step, 0)
        d_query_ref[...] = query_sum[...].T.astype(jnp.bfloat16)

    @pl.when(pair == pairs)
    def _():
        for job in jobs:
            job.after_group()
        settle()
        for job in jobs:
            job.after_across()
        for job in jobs:
            job.finish()


def attend_backward(queries, keys, values, limit, grad_rows, attended, lse, inner_part, outer_part):
    rows, width = queries.shape
    full = keys.shape[0]
    pairs = width // 128
    count, shard = inner_part.shape[:2]
    now = lambda pair, *_: (0, jnp.minimum(pair, pairs - 1))
    before = lambda pair, *_: (0, jnp.maximum(pair - 1, 0))
    row_spec = pl.BlockSpec((rows, 128), now)
    key_spec = pl.BlockSpec((full, 128), now)
    sum_spec = pl.BlockSpec((rows, 128), before)
    tile = (2, rows, 128)
    return pl.pallas_call(
        functools.partial(backward_kernel, count=count),
        grid_spec=pltpu.PrefetchScalarGridSpec(
            num_scalar_prefetch=1,
            grid=(pairs + 1,),
            in_specs=[
                row_spec,
                key_spec,
                key_spec,
                row_spec,
                row_spec,
                pl.BlockSpec((1, 2, rows), lambda pair, *_: (jnp.minimum(pair, pairs - 1), 0, 0)),
                ANY,
                ANY,
            ],
            out_specs=[row_spec, sum_spec, sum_spec, ANY, ANY],
            scratch_shapes=[
                pltpu.VMEM((128, rows), jnp.float32),
                pltpu.VMEM((2,) + tile, jnp.bfloat16),
                pltpu.VMEM((2, 2) + tile, jnp.bfloat16),
                pltpu.VMEM((2,) + tile, jnp.bfloat16),
                pltpu.VMEM((2,) + tile, jnp.bfloat16),
                pltpu.VMEM((2,) + tile, jnp.bfloat16),
                DMA((2,)),
                DMA((2, 2)),
                DMA((2,)),
                DMA((2,)),
            ]
            + LateSum.scratch(count, shard, width) * 2,
        ),
        out_shape=[jax.ShapeDtypeStruct((rows, width), jnp.bfloat16)] * 3
        + [jax.ShapeDtypeStruct((4, shard, width), jnp.bfloat16)] * 2,
        compiler_params=pltpu.CompilerParams(
            collective_id=2, has_side_effects=True, vmem_limit_bytes=VMEM_BYTES
        ),
        cost_estimate=pl.CostEstimate(
            flops=40 * rows * full * width, bytes_accessed=40_000_000, transcendentals=0
        ),
        name="attend_backward",
    )(limit, queries, keys, values, grad_rows, attended, lse, inner_part, outer_part)


def on_device(
    hidden_in,
    lengths,
    seq_order,
    query_weight,
    query_bias,
    key_weight,
    value_weight,
    value_bias,
    output_weight,
    output_bias,
    norm1_gain,
    norm1_shift,
    inner_weight,
    inner_bias,
    outer_weight,
    outer_bias,
    norm2_gain,
    norm2_shift,
    cotangent,
):
    width = hidden_in.shape[2]
    count = lax.axis_size("fsdp")
    group = lax.axis_index("fsdp")
    shard = query_bias.shape[0]
    low = jnp.bfloat16
    placed = jnp.swapaxes(jnp.take(hidden_in, seq_order, axis=1), 0, 1)
    vectors = jnp.concatenate(
        (
            jnp.stack(
                (
                    query_bias,
                    value_bias,
                    output_bias,
                    norm1_gain,
                    norm1_shift,
                    outer_bias,
                    norm2_gain,
                    norm2_shift,
                )
            ),
            inner_bias.reshape(4, shard),
        )
    )
    vectors = jnp.pad(vectors, ((0, 4), (0, 128 - shard)))
    weights = jnp.stack((query_weight, key_weight, value_weight, output_weight))
    tokens, weights, vectors = bring_in(placed, weights, vectors)
    w_inner = lax.all_gather(inner_weight, "fsdp", axis=0, tiled=True)
    w_outer = lax.all_gather(outer_weight, "fsdp", axis=0, tiled=True)
    w_query, w_key, w_value, w_output = (weights[i].reshape(width, width) for i in range(4))
    vectors = vectors[:, :12, :shard].astype(jnp.float32)
    b_query, b_value, b_output, gain_one, shift_one, b_outer, gain_two, shift_two = (
        vectors[:, i].reshape(width) for i in range(8)
    )
    b_inner = vectors[:, 8:].reshape(-1)
    limits = jnp.take(lengths, jnp.take(seq_order, group[None]))
    all_rows = tokens.reshape(-1, width)
    local_len = all_rows.shape[0] // 4
    token_rows = lax.dynamic_index_in_dim(tokens, lax.axis_index("ctx"), 0, False)
    token_rows = token_rows.reshape(local_len, width)
    queries = (product(token_rows, w_query, ((1,), (0,))) + b_query).astype(low)
    keys = product(all_rows, w_key, ((1,), (0,))).astype(low)
    values = (product(all_rows, w_value, ((1,), (0,))) + b_value).astype(low)
    attended, lse = attend_forward(queries, keys, values, limits)
    mixed_low = attended.astype(low)
    branch = product(mixed_low, w_output, ((1,), (0,))) + b_output
    normed, unit_one, scale_one = norm_forward(
        token_rows.astype(jnp.float32) + branch, gain_one, shift_one
    )
    normed_low = normed.astype(low)
    inner_pre = product(normed_low, w_inner, ((1,), (0,))) + b_inner
    activated = gelu_exact(inner_pre).astype(low)
    outer_out = product(activated, w_outer, ((1,), (0,))) + b_outer
    second, unit_two, scale_two = norm_forward(normed + outer_out, gain_two, shift_two)
    layer_out = second.astype(low).reshape(local_len, 1, width)
    upstream = cotangent.reshape(local_len, width).astype(jnp.float32)
    d_second, grad_gain_two, grad_shift_two = norm_backward(upstream, unit_two, scale_two, gain_two)
    d_outer = d_second.astype(low)
    grad_outer_w = product(activated, d_outer, ((0,), (0,))).astype(low)
    grad_outer_b = jnp.sum(d_outer.astype(jnp.float32), axis=0)
    inner_grad = product(d_outer, w_outer, ((1,), (1,)))
    d_inner = (inner_grad * gelu_slope(inner_pre)).astype(low)
    grad_inner_w = product(normed_low, d_inner, ((0,), (0,))).astype(low)
    grad_inner_b = jnp.sum(d_inner.astype(jnp.float32), axis=0)
    d_normed = d_second + product(d_inner, w_inner, ((1,), (1,)))
    d_res, grad_gain_one, grad_shift_one = norm_backward(d_normed, unit_one, scale_one, gain_one)
    d_branch = d_res.astype(low)
    grad_output_w = product(mixed_low, d_branch, ((0,), (0,))).astype(low)
    grad_output_b = jnp.sum(d_branch.astype(jnp.float32), axis=0)
    d_mixed = product(d_branch, w_output, ((1,), (1,))).astype(low)
    d_query, d_keys, d_values, inner_w, outer_w = attend_backward(
        queries,
        keys,
        values,
        limits,
        d_mixed,
        attended,
        lse,
        grad_inner_w.reshape(count, shard, 4 * width),
        grad_outer_w.reshape(count, 4, shard, width),
    )
    grad_query_w = product(token_rows, d_query, ((0,), (0,))).astype(low)
    grad_query_b = jnp.sum(d_query.astype(jnp.float32), axis=0)
    grad_key_w = product(token_rows, d_keys, ((0,), (0,))).astype(low)
    grad_value_w = product(token_rows, d_values, ((0,), (0,))).astype(low)
    grad_value_b = jnp.sum(d_values.astype(jnp.float32), axis=0)
    d_placed = d_res + product(d_query, w_query, ((1,), (1,)))
    d_placed = d_placed + product(d_keys, w_key, ((1,), (1,)))
    d_placed = d_placed + product(d_values, w_value, ((1,), (1,)))
    back_rows = d_placed.astype(low).reshape(count, local_len // count, width)
    returned = lax.all_to_all(back_rows, "fsdp", split_axis=0, concat_axis=0, tiled=True)
    inverse = jnp.argmax(seq_order[:, None] == jnp.arange(count), axis=0)
    grad_in = jnp.take(jnp.swapaxes(returned, 0, 1), inverse, axis=1)
    attention_w = jnp.stack((grad_query_w, grad_key_w, grad_value_w, grad_output_w))
    small_sums = jnp.concatenate(
        (
            jnp.stack(
                (
                    grad_query_b,
                    grad_value_b,
                    grad_output_b,
                    grad_gain_one,
                    grad_shift_one,
                    grad_outer_b,
                    grad_gain_two,
                    grad_shift_two,
                )
            ),
            grad_inner_b.reshape(4, width),
            jnp.zeros((4, width), jnp.float32),
        )
    )
    attention_w, small_sums = sum_gradients(
        (attention_w.reshape(4, count, shard, width),),
        (0,),
        small_sums,
        shard,
        width,
        count,
    )
    attention_w = attention_w.astype(jnp.float32)
    inner_w = jnp.swapaxes(inner_w, 0, 1).reshape(shard, 4 * width).astype(jnp.float32)
    outer_w = outer_w.reshape(4 * shard, width).astype(jnp.float32)
    small = lax.dynamic_slice_in_dim(small_sums[:8], group * shard, shard, axis=1)
    inner_b = lax.dynamic_slice_in_dim(
        small_sums[8:12].reshape(-1), group * 4 * shard, 4 * shard, axis=0
    )
    return (
        layer_out,
        grad_in,
        attention_w[0],
        small[0],
        attention_w[1],
        attention_w[2],
        small[1],
        attention_w[3],
        small[2],
        small[3],
        small[4],
        inner_w,
        inner_b,
        outer_w,
        small[5],
        small[6],
        small[7],
    )


def solution(mesh):
    placed = (
        P(("ctx", "fsdp"), None, None),
        P(),
        P(),
        P("fsdp", None),
        P("fsdp"),
        P("fsdp", None),
        P("fsdp", None),
        P("fsdp"),
        P("fsdp", None),
        P("fsdp"),
        P("fsdp"),
        P("fsdp"),
        P("fsdp", None),
        P("fsdp"),
        P("fsdp", None),
        P("fsdp"),
        P("fsdp"),
        P("fsdp"),
        P("ctx", "fsdp", None),
    )
    return jax.shard_map(
        on_device,
        mesh=mesh,
        in_specs=placed,
        out_specs=(
            P("ctx", "fsdp", None),
            P(("ctx", "fsdp"), None, None),
            P("fsdp", None),
            P("fsdp"),
            P("fsdp", None),
            P("fsdp", None),
            P("fsdp"),
            P("fsdp", None),
            P("fsdp"),
            P("fsdp"),
            P("fsdp"),
            P("fsdp", None),
            P("fsdp"),
            P("fsdp", None),
            P("fsdp"),
            P("fsdp"),
            P("fsdp"),
        ),
        check_vma=False,
    )
```

```python
import functools

import jax
import jax.numpy as jnp
from jax import lax
from jax.experimental import pallas as pl
from jax.experimental.pallas import tpu as pltpu
from jax.sharding import PartitionSpec as P

SCALE = 64 ** (-0.5)
LOG2E = 1.4426950408889634
FORWARD_KEYS = 2048
VMEM_BYTES = 60 * 2**20

NORM_EPSILON = 1e-12
NEG_BIG = -1e30
ROOT_HALF = 0.7071067811865476
ROOT_TWO_PI = 2.5066282746310002


def norm_forward(source, gain_vec, shift_vec):
    centre = source - jnp.mean(source, axis=-1, keepdims=True)
    inv_scale = lax.rsqrt(jnp.mean(centre * centre, axis=-1, keepdims=True) + NORM_EPSILON)
    unit_rows = centre * inv_scale
    return (unit_rows * gain_vec + shift_vec, unit_rows, inv_scale)


def norm_backward(upstream, unit_rows, inv_scale, gain_vec):
    scaled = upstream * gain_vec
    plain_mean = jnp.mean(scaled, axis=-1, keepdims=True)
    cross_mean = jnp.mean(scaled * unit_rows, axis=-1, keepdims=True)
    d_source = inv_scale * (scaled - plain_mean - unit_rows * cross_mean)
    return (d_source, jnp.sum(upstream * unit_rows, axis=0), jnp.sum(upstream, axis=0))


def gelu_exact(source):
    return 0.5 * source * (1.0 + jax.scipy.special.erf(source * ROOT_HALF))


def gelu_slope(source):
    return (
        0.5 * (1.0 + jax.scipy.special.erf(source * ROOT_HALF))
        + source * jnp.exp(-0.5 * source * source) / ROOT_TWO_PI
    )


def product(left, right, dims):
    return lax.dot_general(left, right, (dims, ((), ())), preferred_element_type=jnp.float32)


def lane_is_low():
    return lax.broadcasted_iota(jnp.int32, (1, 128), 1) < 64


def split_query(query_pair, low_half):
    scaled = query_pair * (SCALE * LOG2E)
    high = scaled.astype(jnp.bfloat16).astype(jnp.float32)
    rest = pltpu.roll(scaled - high, 64, 1)
    return (
        jnp.where(low_half, high, rest).astype(jnp.bfloat16),
        jnp.where(low_half, rest, high).astype(jnp.bfloat16),
    )


def twice(pair, low_half):
    other = pltpu.roll(pair, 64, 1)
    return (
        jnp.where(low_half, pair, other).astype(jnp.bfloat16),
        jnp.where(low_half, other, pair).astype(jnp.bfloat16),
    )


MESH = pl.DeviceIdType.MESH
DMA = pltpu.SemaphoreType.DMA
ANY = pl.BlockSpec(memory_space=pl.ANY)
STAGES = ("start", "after_core", "after_across", "after_group", "finish")


def places():
    ctx, group = lax.axis_index("ctx"), lax.axis_index("fsdp")
    return ctx, group, lax.rem(ctx + 2, 4), ctx + 1 - 2 * lax.rem(ctx, 2)


def remote(source, target, send_sem, recv_sem, where):
    return pltpu.make_async_remote_copy(
        src_ref=source,
        dst_ref=target,
        send_sem=send_sem,
        recv_sem=recv_sem,
        device_id=where,
        device_id_type=MESH,
    )


def greet(count):
    ctx, group, _, _ = places()
    barrier = pltpu.get_barrier_semaphore()

    def one(step, carry):
        pl.semaphore_signal(
            barrier,
            inc=1,
            device_id={"fsdp": lax.rem(group + step, count)},
            device_id_type=MESH,
        )
        return carry

    lax.fori_loop(1, count, one, 0)
    for other in range(1, 4):
        pl.semaphore_signal(
            barrier, inc=1, device_id={"ctx": lax.rem(ctx + other, 4)}, device_id_type=MESH
        )
    pl.semaphore_wait(barrier, count - 1 + 3)


def arrival_kernel(
    placed,
    weights,
    small,
    tokens,
    gathered,
    small_all,
    tok_stage,
    w_stage,
    small_stage,
    local_sem,
    tok_send,
    tok_recv,
    w_send,
    w_recv,
    small_send,
    small_recv,
    x_send,
    x_recv,
    s_send,
    s_recv,
    r_send,
    r_recv,
    *,
    count,
):
    ctx, group, across, sibling = places()
    own_tok = pltpu.make_async_copy(placed.at[group], tok_stage, local_sem.at[0])
    own_w = pltpu.make_async_copy(weights, w_stage, local_sem.at[1])
    own_small = pltpu.make_async_copy(small, small_stage, local_sem.at[2])
    own_tok.start()
    own_w.start()
    own_small.start()
    greet(count)

    def tok_copy(peer, step):
        return remote(
            placed.at[peer],
            tokens.at[ctx, group],
            tok_send.at[step],
            tok_recv.at[step],
            {"fsdp": peer},
        )

    def w_copy(peer, step):
        return remote(
            weights.at[ctx],
            gathered.at[ctx, group],
            w_send.at[step],
            w_recv.at[step],
            {"fsdp": peer},
        )

    def small_copy(peer, step):
        return remote(
            small, small_all.at[group], small_send.at[step], small_recv.at[step], {"fsdp": peer}
        )

    def send(step, carry):
        peer = lax.rem(group + step, count)
        w_copy(peer, step).start()
        tok_copy(peer, step).start()
        small_copy(peer, step).start()
        return carry

    lax.fori_loop(1, count, send, 0)
    own_tok.wait()
    own_w.wait()
    own_small.wait()
    put_tok = pltpu.make_async_copy(tok_stage, tokens.at[ctx, group], local_sem.at[0])
    put_w = pltpu.make_async_copy(w_stage, gathered.at[:, group], local_sem.at[1])
    put_small = pltpu.make_async_copy(small_stage, small_all.at[group], local_sem.at[2])
    put_tok.start()
    put_w.start()
    put_small.start()

    def across_copy(kind, block):
        where = gathered if kind == 0 else tokens
        return remote(
            where.at[ctx, block],
            where.at[ctx, block],
            x_send.at[kind, block],
            x_recv.at[kind, block],
            {"ctx": across},
        )

    def sibling_copy(kind, block):
        where = gathered if kind == 0 else tokens
        return remote(
            where.at[ctx, block],
            where.at[ctx, block],
            s_send.at[kind, block],
            s_recv.at[kind, block],
            {"ctx": sibling},
        )

    def relay_copy(kind, block):
        where = gathered if kind == 0 else tokens
        return remote(
            where.at[across, block],
            where.at[across, block],
            r_send.at[kind, block],
            r_recv.at[kind, block],
            {"ctx": sibling},
        )

    put_tok.wait()
    across_copy(1, group).start()
    sibling_copy(1, group).start()
    put_w.wait()
    put_small.wait()

    def arrive(step, carry):
        origin = lax.rem(group - step + count, count)
        w_copy(origin, step).wait_recv()
        across_copy(0, origin).start()
        sibling_copy(0, origin).start()
        tok_copy(origin, step).wait_recv()
        across_copy(1, origin).start()
        sibling_copy(1, origin).start()
        return carry

    lax.fori_loop(1, count, arrive, 0)

    across_copy(1, group).wait_recv()
    relay_copy(1, group).start()

    def passed(step, carry):
        origin = lax.rem(group - step + count, count)
        for kind in range(2):
            across_copy(kind, origin).wait_recv()
            relay_copy(kind, origin).start()
        return carry

    lax.fori_loop(1, count, passed, 0)
    across_copy(1, group).wait_send()
    sibling_copy(1, group).wait()
    relay_copy(1, group).wait()

    def finish(step, carry):
        origin = lax.rem(group - step + count, count)
        for kind in range(2):
            across_copy(kind, origin).wait_send()
            sibling_copy(kind, origin).wait()
            relay_copy(kind, origin).wait()
        return carry

    lax.fori_loop(1, count, finish, 0)

    def sent(step, carry):
        peer = lax.rem(group + step, count)
        w_copy(peer, step).wait_send()
        tok_copy(peer, step).wait_send()
        small_copy(peer, step).wait()
        return carry

    lax.fori_loop(1, count, sent, 0)


def bring_in(placed, weights, small):
    count, rows, width = placed.shape
    return pl.pallas_call(
        functools.partial(arrival_kernel, count=count),
        in_specs=[ANY] * 3,
        out_specs=[ANY] * 3,
        out_shape=[
            jax.ShapeDtypeStruct((4, count, rows, width), jnp.bfloat16),
            jax.ShapeDtypeStruct((4, count) + weights.shape[1:], jnp.bfloat16),
            jax.ShapeDtypeStruct((count,) + small.shape, jnp.bfloat16),
        ],
        scratch_shapes=[
            pltpu.VMEM((rows, width), jnp.bfloat16),
            pltpu.VMEM((4,) + weights.shape[1:], jnp.bfloat16),
            pltpu.VMEM(small.shape, jnp.bfloat16),
            DMA((3,)),
        ]
        + [DMA((count,))] * 6
        + [DMA((2, count))] * 6,
        compiler_params=pltpu.CompilerParams(
            collective_id=0, has_side_effects=True, vmem_limit_bytes=8 * 2**20
        ),
        name="bring_in",
    )(placed, weights, small)


class Sum:
    SCRATCH = 16

    def __init__(self, kind, ref, out, scratch, count):
        self.kind, self.ref, self.out, self.count = kind, ref, out, count
        self.near, self.far, self.got_near, self.got_far = scratch[:4]
        self.got_across, self.got_group, self.done = scratch[4:7]
        self.load, self.c_send, self.c_recv, self.x_send, self.x_recv = scratch[7:12]
        self.g_send, self.g_recv, self.o_send, self.o_recv = scratch[12:16]
        self.ctx, self.group, self.across, self.sibling = places()
        self.width = self.near.shape[-1]

    @staticmethod
    def scratch(count, rows, width):
        return (
            [pltpu.VMEM((count, rows, width), jnp.bfloat16)] * 6
            + [pltpu.VMEM((rows, width), jnp.bfloat16)]
            + [DMA((2,))] * 3
            + [DMA((count,))] * 4
            + [DMA((4,))] * 2
        )

    def quarter(self, index):
        if self.kind == 0:
            return self.ref.at[index]
        if self.kind == 1:
            start = pl.multiple_of(index * self.width, self.width)
            return self.ref.at[:, :, pl.ds(start, self.width)]
        return self.ref.at[:, index]

    def loads(self):
        return (
            pltpu.make_async_copy(self.quarter(self.across), self.far, self.load.at[0]),
            pltpu.make_async_copy(self.quarter(self.ctx), self.near, self.load.at[1]),
        )

    def cores(self):
        beyond = lax.rem(self.sibling + 2, 4)
        there = {"ctx": self.sibling}
        return (
            remote(self.quarter(beyond), self.got_far, self.c_send.at[0], self.c_recv.at[0], there),
            remote(
                self.quarter(self.sibling),
                self.got_near,
                self.c_send.at[1],
                self.c_recv.at[1],
                there,
            ),
        )

    def x_copy(self, block):
        return remote(
            self.far.at[block],
            self.got_across.at[block],
            self.x_send.at[block],
            self.x_recv.at[block],
            {"ctx": self.across},
        )

    def g_copy(self, peer, step):
        return remote(
            self.near.at[peer],
            self.got_group.at[step],
            self.g_send.at[step],
            self.g_recv.at[step],
            {"fsdp": peer},
        )

    def o_copy(self, other):
        return remote(
            self.done,
            self.out.at[self.ctx],
            self.o_send.at[other],
            self.o_recv.at[other],
            {"ctx": lax.rem(self.ctx + other, 4)},
        )

    def own_out(self):
        return pltpu.make_async_copy(self.done, self.out.at[self.ctx], self.load.at[0])

    def add(self, total, other):
        def one(block, carry):
            both = total[block].astype(jnp.float32) + other[block].astype(jnp.float32)
            total[block] = both.astype(jnp.bfloat16)
            return carry

        lax.fori_loop(0, self.count, one, 0)

    def start(self):
        for copy in self.loads() + self.cores():
            copy.start()

    def after_core(self):
        loads, cores = self.loads(), self.cores()
        loads[0].wait()
        cores[0].wait_recv()
        self.add(self.far, self.got_far)

        def send(step, carry):
            self.x_copy(lax.rem(self.group + 1 + step, self.count)).start()
            return carry

        lax.fori_loop(0, self.count, send, 0)
        loads[1].wait()
        cores[1].wait_recv()
        self.add(self.near, self.got_near)
        cores[0].wait_send()
        cores[1].wait_send()

    def after_across(self):
        def one(step, carry):
            block = lax.rem(self.group + step, self.count)
            self.x_copy(block).wait()
            both = self.near[block].astype(jnp.float32) + self.got_across[block].astype(jnp.float32)
            self.near[block] = both.astype(jnp.bfloat16)
            self.g_copy(block, step).start()
            return carry

        lax.fori_loop(1, self.count, one, 0)
        self.x_copy(self.group).wait()

    def after_group(self):
        group = self.group
        total = self.near[group].astype(jnp.float32) + self.got_across[group].astype(jnp.float32)

        def one(step, total):
            self.g_copy(lax.rem(group + step, self.count), step).wait()
            return total + self.got_group[step].astype(jnp.float32)

        self.done[...] = lax.fori_loop(1, self.count, one, total).astype(jnp.bfloat16)
        self.own_out().start()
        for other in range(1, 4):
            self.o_copy(other).start()

    def finish(self):
        self.own_out().wait()
        for other in range(1, 4):
            self.o_copy(other).wait()


class VectorSum:
    SCRATCH = 9

    def __init__(self, ref, out, scratch, count):
        self.ref, self.out, self.count = ref, out, count
        self.total, self.got_ctx, self.got_group = scratch[:3]
        self.load, self.c_send, self.c_recv, self.g_send, self.g_recv = scratch[3:8]
        self.result = scratch[8]
        self.ctx, self.group, _, _ = places()

    @staticmethod
    def scratch(count, rows, width):
        return [
            pltpu.VMEM((rows, width), jnp.float32),
            pltpu.VMEM((4, rows, width), jnp.float32),
            pltpu.VMEM((count, rows, width), jnp.float32),
            DMA((2,)),
            DMA((4,)),
            DMA((4,)),
            DMA((count,)),
            DMA((count,)),
            pltpu.VMEM((rows, width), jnp.float32),
        ]

    def own(self):
        return pltpu.make_async_copy(self.ref, self.total, self.load.at[0])

    def own_out(self):
        return pltpu.make_async_copy(self.result, self.out, self.load.at[1])

    def c_copy(self, other):
        return remote(
            self.ref,
            self.got_ctx.at[other],
            self.c_send.at[other],
            self.c_recv.at[other],
            {"ctx": lax.rem(self.ctx + other, 4)},
        )

    def g_copy(self, step):
        return remote(
            self.total,
            self.got_group.at[step],
            self.g_send.at[step],
            self.g_recv.at[step],
            {"fsdp": lax.rem(self.group + step, self.count)},
        )

    def start(self):
        self.own().start()
        for other in range(1, 4):
            self.c_copy(other).start()

    def after_core(self):
        self.own().wait()
        total = self.total[...]
        for other in range(1, 4):
            self.c_copy(other).wait()
            total = total + self.got_ctx[other]
        self.total[...] = total

        def one(step, carry):
            self.g_copy(step).start()
            return carry

        lax.fori_loop(1, self.count, one, 0)

    def after_across(self):
        pass

    def after_group(self):
        def one(step, total):
            self.g_copy(step).wait()
            return total + self.got_group[step]

        self.result[...] = lax.fori_loop(1, self.count, one, self.total[...])
        self.own_out().start()

    def finish(self):
        self.own_out().wait()


class LateSum:
    SCRATCH = 16

    def __init__(self, kind, ref, out, scratch, count):
        self.kind, self.ref, self.out, self.count = kind, ref, out, count
        self.near, self.got, self.got_group, self.half, self.got_across, self.done = scratch[:6]
        self.load, self.c_send, self.c_recv, self.g_send, self.g_recv = scratch[6:11]
        self.x_send, self.x_recv, self.o_send, self.o_recv, self.put = scratch[11:16]
        self.ctx, self.group, self.across, self.sibling = places()
        self.core = lax.rem(self.ctx, 2)
        self.width = self.near.shape[-1]

    @staticmethod
    def scratch(count, rows, width):
        return (
            [pltpu.VMEM((count, 2, rows, width), jnp.bfloat16)] * 3
            + [pltpu.VMEM((2, rows, width), jnp.bfloat16)] * 3
            + [DMA((2,))] * 3
            + [DMA((count,))] * 2
            + [DMA((2,))] * 5
        )

    def quarter(self, index):
        if self.kind == 1:
            start = pl.multiple_of(index * self.width, self.width)
            return self.ref.at[:, :, pl.ds(start, self.width)]
        return self.ref.at[:, index]

    def load_copy(self, half):
        return pltpu.make_async_copy(
            self.quarter(2 * half + self.core), self.near.at[:, half], self.load.at[half]
        )

    def core_copy(self, half):
        return remote(
            self.quarter(2 * half + 1 - self.core),
            self.got.at[:, half],
            self.c_send.at[half],
            self.c_recv.at[half],
            {"ctx": self.sibling},
        )

    def group_copy(self, step):
        peer = lax.rem(self.group + step, self.count)
        return remote(
            self.near.at[peer],
            self.got_group.at[step],
            self.g_send.at[step],
            self.g_recv.at[step],
            {"fsdp": peer},
        )

    def x_copy(self):
        return remote(
            self.half, self.got_across, self.x_send.at[0], self.x_recv.at[0], {"ctx": self.across}
        )

    def out_copy(self, half):
        return remote(
            self.done.at[half],
            self.out.at[2 * half + self.core],
            self.o_send.at[half],
            self.o_recv.at[half],
            {"ctx": self.sibling},
        )

    def own_out(self, half):
        return pltpu.make_async_copy(
            self.done.at[half], self.out.at[2 * half + self.core], self.put.at[half]
        )

    def start(self):
        for half in range(2):
            self.load_copy(half).start()
            self.core_copy(half).start()

    def after_core(self):
        for half in range(2):
            self.load_copy(half).wait()
            self.core_copy(half).wait()

        def one(step, carry):
            block = lax.rem(self.group + step, self.count)
            both = self.near[block].astype(jnp.float32) + self.got[block].astype(jnp.float32)
            self.near[block] = both.astype(jnp.bfloat16)
            return carry

        lax.fori_loop(0, self.count, one, 0)

        def send(step, carry):
            self.group_copy(step).start()
            return carry

        lax.fori_loop(1, self.count, send, 0)

    def after_group(self):
        def one(step, total):
            self.group_copy(step).wait()
            return total + self.got_group[step].astype(jnp.float32)

        total = lax.fori_loop(1, self.count, one, self.near[self.group].astype(jnp.float32))
        self.half[...] = total.astype(jnp.bfloat16)
        self.x_copy().start()

    def after_across(self):
        self.x_copy().wait()
        both = self.half[...].astype(jnp.float32) + self.got_across[...].astype(jnp.float32)
        self.done[...] = both.astype(jnp.bfloat16)
        for half in range(2):
            self.own_out(half).start()
            self.out_copy(half).start()

    def finish(self):
        for half in range(2):
            self.own_out(half).wait()
            self.out_copy(half).wait()


def sums_kernel(*refs, kinds, count):
    parts = len(kinds)
    ins, outs, rest = refs[: parts + 1], refs[parts + 1 : 2 * parts + 2], refs[2 * parts + 2 :]
    jobs = [VectorSum(ins[parts], outs[parts], rest[: VectorSum.SCRATCH], count)]
    rest = rest[VectorSum.SCRATCH :]
    for index, kind in enumerate(kinds):
        own = rest[index * Sum.SCRATCH : (index + 1) * Sum.SCRATCH]
        jobs.append(Sum(kind, ins[index], outs[index], own, count))
    greet(count)
    for stage in STAGES:
        for job in jobs:
            getattr(job, stage)()


def sum_gradients(parts, kinds, vectors, rows, width, count):
    scratch = VectorSum.scratch(count, *vectors.shape)
    for _ in kinds:
        scratch += Sum.scratch(count, rows, width)
    return pl.pallas_call(
        functools.partial(sums_kernel, kinds=kinds, count=count),
        in_specs=[ANY] * (len(kinds) + 1),
        out_specs=[ANY] * (len(kinds) + 1),
        out_shape=[jax.ShapeDtypeStruct((4, rows, width), jnp.bfloat16)] * len(kinds)
        + [jax.ShapeDtypeStruct(vectors.shape, jnp.float32)],
        scratch_shapes=scratch,
        compiler_params=pltpu.CompilerParams(
            collective_id=1, has_side_effects=True, vmem_limit_bytes=VMEM_BYTES
        ),
        name="sum_gradients",
    )(*parts, vectors)


class Gather:
    SCRATCH = 11

    def __init__(self, inner, outer, inner_all, outer_all, scratch, count):
        self.own, self.all, self.count = (inner, outer), (inner_all, outer_all), count
        self.stages, self.local = scratch[:2], scratch[2]
        self.g_send, self.g_recv, self.x_send, self.x_recv = scratch[3:7]
        self.s_send, self.s_recv, self.r_send, self.r_recv = scratch[7:11]
        self.ctx, self.group, self.across, self.sibling = places()
        self.width = outer.shape[-1]

    @staticmethod
    def scratch(count, rows, width):
        return [
            pltpu.VMEM((rows, 4 * width), jnp.bfloat16),
            pltpu.VMEM((4, rows, width), jnp.bfloat16),
            DMA((4,)),
        ] + [DMA((2, count))] * 8

    def columns(self, quarter):
        return pl.ds(pl.multiple_of(quarter * self.width, self.width), self.width)

    def mine(self, kind):
        if kind == 0:
            return self.own[0].at[:, self.columns(self.ctx)]
        return self.own[1].at[self.ctx]

    def place(self, kind, block, quarter):
        if kind == 0:
            return self.all[0].at[block, :, self.columns(quarter)]
        return self.all[1].at[block, quarter]

    def origin(self, step):
        return lax.rem(self.group - step + self.count, self.count)

    def group_copy(self, kind, step):
        return remote(
            self.mine(kind),
            self.place(kind, self.group, self.ctx),
            self.g_send.at[kind, step],
            self.g_recv.at[kind, step],
            {"fsdp": lax.rem(self.group + step, self.count)},
        )

    def pass_on(self, kind, step, quarter, send, recv, target):
        place = self.place(kind, self.origin(step), quarter)
        block = self.origin(step)
        return remote(place, place, send.at[kind, block], recv.at[kind, block], {"ctx": target})

    def across_copy(self, kind, step):
        return self.pass_on(kind, step, self.ctx, self.x_send, self.x_recv, self.across)

    def sibling_copy(self, kind, step):
        return self.pass_on(kind, step, self.ctx, self.s_send, self.s_recv, self.sibling)

    def relay_copy(self, kind, step):
        return self.pass_on(kind, step, self.across, self.r_send, self.r_recv, self.sibling)

    def load(self, kind):
        return pltpu.make_async_copy(self.own[kind], self.stages[kind], self.local.at[kind])

    def put(self, kind):
        return pltpu.make_async_copy(
            self.stages[kind], self.all[kind].at[self.group], self.local.at[2 + kind]
        )

    def over(self, first, last, body):
        def one(step, carry):
            for kind in range(2):
                body(kind, step)
            return carry

        if first < last:
            lax.fori_loop(first, last, one, 0)

    def start(self):
        for kind in range(2):
            self.load(kind).start()
        self.over(1, self.count, lambda kind, step: self.group_copy(kind, step).start())
        for kind in range(2):
            self.load(kind).wait()
            self.put(kind).start()

    def arrive(self, first, last):
        def body(kind, step):
            self.group_copy(kind, step).wait_recv()
            self.across_copy(kind, step).start()
            self.sibling_copy(kind, step).start()

        self.over(first, last, body)

    def relay(self, first, last):
        def body(kind, step):
            self.across_copy(kind, step).wait_recv()
            self.relay_copy(kind, step).start()

        self.over(first, last, body)

    def finish(self):
        def body(kind, step):
            self.group_copy(kind, step).wait_send()
            self.across_copy(kind, step).wait_send()
            self.sibling_copy(kind, step).wait()
            self.relay_copy(kind, step).wait()

        self.over(1, self.count, body)
        for kind in range(2):
            self.put(kind).wait()


def forward_kernel(
    limit_ref,
    query_ref,
    key_ref,
    value_ref,
    inner_ref,
    outer_ref,
    attended_ref,
    lse_ref,
    inner_all,
    outer_all,
    *scratch,
    key_rows,
    count,
    arrivals,
):
    pair = pl.program_id(0)
    pairs = pl.num_programs(0) - 1
    gather = Gather(inner_ref, outer_ref, inner_all, outer_all, scratch, count)
    for when, (first, last, relay_first, relay_last) in enumerate(arrivals):

        @pl.when(pair == when)
        def _():
            if when == 0:
                greet(count)
                gather.start()
            gather.arrive(first, last)
            gather.relay(relay_first, relay_last)
            if when == len(arrivals) - 1:
                gather.finish()

    @pl.when(pair < pairs)
    def _():
        low_half = lane_is_low()
        limit = limit_ref[0]
        queries = split_query(query_ref[...].astype(jnp.float32), low_half)
        query_rows = query_ref.shape[0]

        def step(tile, state):
            start = pl.multiple_of(tile * key_rows, key_rows)
            usable = start + lax.broadcasted_iota(jnp.int32, (key_rows, 1), 0) < limit
            key_tile = key_ref[pl.ds(start, key_rows), :].astype(jnp.float32)
            keys = twice(jnp.where(usable, key_tile, key_ref[0:1, :].astype(jnp.float32)), low_half)
            value_tile = value_ref[pl.ds(start, key_rows), :].astype(jnp.float32)
            value_tile = jnp.where(usable, value_tile, 0.0)
            count = jnp.where(usable, 1.0, 0.0)
            values = (
                jnp.where(low_half, value_tile, count).astype(jnp.bfloat16),
                jnp.where(low_half, count, value_tile).astype(jnp.bfloat16),
            )
            fresh = []
            for head in range(2):
                top, total = state[head]
                scores = product(queries[head], keys[head], ((1,), (1,)))
                new_top = jnp.maximum(top, jnp.max(scores, axis=1, keepdims=True))
                weights = jnp.exp2(scores - new_top).astype(jnp.bfloat16)
                total = total * jnp.exp2(top - new_top) + product(weights, values[head], ((1,), (0,)))
                fresh.append((new_top, total))
            return tuple(fresh)

        empty = (
            jnp.full((query_rows, 1), NEG_BIG, jnp.float32),
            jnp.zeros((query_rows, 128), jnp.float32),
        )
        (top_a, total_a), (top_b, total_b) = lax.fori_loop(
            0, key_ref.shape[0] // key_rows, step, (empty, empty)
        )
        mass_a, mass_b = total_a[:, 64:65], total_b[:, 0:1]
        attended_ref[...] = jnp.where(low_half, total_a / mass_a, total_b / mass_b)
        lse = jnp.where(low_half, top_a + jnp.log2(mass_a), top_b + jnp.log2(mass_b)).T
        lse_ref[0, 0:1, :] = lse[0:1, :]
        lse_ref[0, 1:2, :] = lse[64:65, :]


def attend_forward(queries, keys, values, limit, inner, outer, count):
    rows, width = queries.shape
    full = keys.shape[0]
    pairs = width // 128
    shard = inner.shape[0]
    sevenths = (0, 0, 1, 3, 5) + (7,) * (pairs - 3)
    marks = [1 + (count - 1) * n // 7 for n in sevenths]
    marks = marks[: pairs + 2]
    late = [1, 1, 1] + marks[2 : pairs]
    late = late[: pairs + 1] + [count]
    arrivals = [
        (marks[i], marks[i + 1], late[i], late[i + 1]) for i in range(pairs + 1)
    ]
    now = lambda pair, *_: (0, jnp.minimum(pair, pairs - 1))
    row_spec = pl.BlockSpec((rows, 128), now)
    key_spec = pl.BlockSpec((full, 128), now)
    return pl.pallas_call(
        functools.partial(forward_kernel, key_rows=FORWARD_KEYS, count=count, arrivals=arrivals),
        grid_spec=pltpu.PrefetchScalarGridSpec(
            num_scalar_prefetch=1,
            grid=(pairs + 1,),
            in_specs=[row_spec, key_spec, key_spec, ANY, ANY],
            out_specs=[
                row_spec,
                pl.BlockSpec((1, 2, rows), lambda pair, *_: (jnp.minimum(pair, pairs - 1), 0, 0)),
                ANY,
                ANY,
            ],
            scratch_shapes=Gather.scratch(count, shard, width),
        ),
        out_shape=[
            jax.ShapeDtypeStruct((rows, width), jnp.float32),
            jax.ShapeDtypeStruct((pairs, 2, rows), jnp.float32),
            jax.ShapeDtypeStruct((count, shard, 4 * width), jnp.bfloat16),
            jax.ShapeDtypeStruct((count, 4, shard, width), jnp.bfloat16),
        ],
        compiler_params=pltpu.CompilerParams(
            collective_id=3, has_side_effects=True, vmem_limit_bytes=VMEM_BYTES
        ),
        cost_estimate=pl.CostEstimate(
            flops=16 * rows * full * width, bytes_accessed=20_000_000, transcendentals=0
        ),
        name="attend_forward",
    )(limit, queries, keys, values, inner, outer)


def backward_kernel(
    limit_ref,
    query_ref,
    key_ref,
    value_ref,
    grad_ref,
    attended_ref,
    lse_ref,
    inner_ref,
    outer_ref,
    d_query_ref,
    d_key_ref,
    d_value_ref,
    inner_out,
    outer_out,
    query_sum,
    part,
    got_core,
    far,
    near,
    got_x,
    core_send,
    core_recv,
    x_send,
    x_recv,
    *rest,
    count,
):
    pair = pl.program_id(0)
    pairs = pl.num_programs(0) - 1
    slot = lax.rem(pair, 2)
    ctx, _, across, sibling = places()
    key_rows = query_ref.shape[0]
    jobs = [
        LateSum(1, inner_ref, inner_out, rest[: LateSum.SCRATCH], count),
        LateSum(2, outer_ref, outer_out, rest[LateSum.SCRATCH :], count),
    ]

    def core_copy(which):
        return remote(
            part.at[which],
            got_core.at[slot, which],
            core_send.at[which],
            core_recv.at[slot, which],
            {"ctx": sibling},
        )

    def x_copy(where):
        return remote(
            far.at[where], got_x.at[where], x_send.at[where], x_recv.at[where], {"ctx": across}
        )

    def settle():
        where = 1 - slot
        x_copy(where).wait()
        for kind, ref in enumerate((d_key_ref, d_value_ref)):
            both = near[where, kind].astype(jnp.float32) + got_x[where, kind].astype(jnp.float32)
            ref[...] = both.astype(jnp.bfloat16)

    @pl.when(pair == 0)
    def _():
        greet(count)
        for job in jobs:
            job.start()

    @pl.when(pair == 1)
    def _():
        for job in jobs:
            job.after_core()

    @pl.when(pair < pairs)
    def _():
        low_half = lane_is_low()
        high_half = jnp.logical_not(low_half)
        lane = lax.broadcasted_iota(jnp.int32, (1, 128), 1)
        limit = limit_ref[0]
        query_pair = query_ref[...].astype(jnp.float32)
        queries = split_query(query_pair, low_half)
        scaled = query_pair * SCALE
        grad_pair = grad_ref[...].astype(jnp.float32)
        overlap = grad_pair * attended_ref[...]
        own_query, own_grad, joined_grad = [], [], []
        for head in range(2):
            mine = low_half if head == 0 else high_half
            own_query.append(jnp.where(mine, scaled, 0.0).astype(jnp.bfloat16))
            own_grad.append(jnp.where(mine, grad_pair, 0.0).astype(jnp.bfloat16))
            delta = -jnp.sum(jnp.where(mine, overlap, 0.0), axis=1, keepdims=True)
            first = delta.astype(jnp.bfloat16).astype(jnp.float32)
            second = (delta - first).astype(jnp.bfloat16).astype(jnp.float32)
            third = delta - first - second
            spare = 64 * (1 - head)
            joined = jnp.where(lane == spare + 2, third, 0.0)
            joined = jnp.where(lane == spare + 1, second, joined)
            joined = jnp.where(lane == spare, first, joined)
            joined_grad.append(jnp.where(mine, grad_pair, joined).astype(jnp.bfloat16))
        query_sum[...] = jnp.zeros_like(query_sum)

        def step(tile, carry):
            odd = lax.rem(tile, 2)
            quarter = lax.rem(sibling + odd * (ctx - sibling) + 2 * (1 - tile // 2), 4)
            start = pl.multiple_of(quarter * key_rows, key_rows)
            usable = start + lax.broadcasted_iota(jnp.int32, (key_rows, 1), 0) < limit
            key_tile = key_ref[pl.ds(start, key_rows), :].astype(jnp.float32)
            value_tile = value_ref[pl.ds(start, key_rows), :].astype(jnp.float32)
            keys = twice(jnp.where(usable, key_tile, key_ref[0:1, :].astype(jnp.float32)), low_half)
            own_tile = jnp.where(usable, key_tile * SCALE, 0.0)
            key_piece = value_piece = None
            for head in range(2):
                mine = low_half if head == 0 else high_half
                values = jnp.where(mine, value_tile, 1.0).astype(jnp.bfloat16)
                own_key = jnp.where(mine, own_tile, 0.0).astype(jnp.bfloat16)
                scores = product(keys[head], queries[head], ((1,), (1,)))
                probs = jnp.exp2(scores - lse_ref[0, head : head + 1, :])
                slopes = product(values, joined_grad[head], ((1,), (1,)))
                score_grads = (probs * slopes).astype(jnp.bfloat16)
                value_term = product(probs.astype(jnp.bfloat16), own_grad[head], ((1,), (0,)))
                key_term = product(score_grads, own_query[head], ((1,), (0,)))
                value_piece = value_term if value_piece is None else value_piece + value_term
                key_piece = key_term if key_piece is None else key_piece + key_term
                query_sum[...] += product(own_key, score_grads, ((0,), (0,)))
            pieces = (jnp.where(usable, key_piece, 0.0), jnp.where(usable, value_piece, 0.0))

            @pl.when(odd == 0)
            def _():
                which = tile // 2
                for kind in range(2):
                    part[which, kind] = pieces[kind].astype(jnp.bfloat16)
                core_copy(which).start()

            @pl.when(tile == 1)
            def _():
                @pl.when(pair > 0)
                def _():
                    settle()

                core_copy(0).wait_recv()
                for kind in range(2):
                    both = pieces[kind] + got_core[slot, 0, kind].astype(jnp.float32)
                    far[slot, kind] = both.astype(jnp.bfloat16)
                x_copy(slot).start()

            @pl.when(tile == 3)
            def _():
                core_copy(1).wait_recv()
                for kind in range(2):
                    both = pieces[kind] + got_core[slot, 1, kind].astype(jnp.float32)
                    near[slot, kind] = both.astype(jnp.bfloat16)
                core_copy(0).wait_send()
                core_copy(1).wait_send()

            return carry

        lax.fori_loop(0, 4, step, 0)
        d_query_ref[...] = query_sum[...].T.astype(jnp.bfloat16)

    @pl.when(pair == pairs)
    def _():
        for job in jobs:
            job.after_group()
        settle()
        for job in jobs:
            job.after_across()
        for job in jobs:
            job.finish()


def attend_backward(queries, keys, values, limit, grad_rows, attended, lse, inner_part, outer_part):
    rows, width = queries.shape
    full = keys.shape[0]
    pairs = width // 128
    count, shard = inner_part.shape[:2]
    now = lambda pair, *_: (0, jnp.minimum(pair, pairs - 1))
    before = lambda pair, *_: (0, jnp.maximum(pair - 1, 0))
    row_spec = pl.BlockSpec((rows, 128), now)
    key_spec = pl.BlockSpec((full, 128), now)
    sum_spec = pl.BlockSpec((rows, 128), before)
    tile = (2, rows, 128)
    return pl.pallas_call(
        functools.partial(backward_kernel, count=count),
        grid_spec=pltpu.PrefetchScalarGridSpec(
            num_scalar_prefetch=1,
            grid=(pairs + 1,),
            in_specs=[
                row_spec,
                key_spec,
                key_spec,
                row_spec,
                row_spec,
                pl.BlockSpec((1, 2, rows), lambda pair, *_: (jnp.minimum(pair, pairs - 1), 0, 0)),
                ANY,
                ANY,
            ],
            out_specs=[row_spec, sum_spec, sum_spec, ANY, ANY],
            scratch_shapes=[
                pltpu.VMEM((128, rows), jnp.float32),
                pltpu.VMEM((2,) + tile, jnp.bfloat16),
                pltpu.VMEM((2, 2) + tile, jnp.bfloat16),
                pltpu.VMEM((2,) + tile, jnp.bfloat16),
                pltpu.VMEM((2,) + tile, jnp.bfloat16),
                pltpu.VMEM((2,) + tile, jnp.bfloat16),
                DMA((2,)),
                DMA((2, 2)),
                DMA((2,)),
                DMA((2,)),
            ]
            + LateSum.scratch(count, shard, width) * 2,
        ),
        out_shape=[jax.ShapeDtypeStruct((rows, width), jnp.bfloat16)] * 3
        + [jax.ShapeDtypeStruct((4, shard, width), jnp.bfloat16)] * 2,
        compiler_params=pltpu.CompilerParams(
            collective_id=2, has_side_effects=True, vmem_limit_bytes=VMEM_BYTES
        ),
        cost_estimate=pl.CostEstimate(
            flops=40 * rows * full * width, bytes_accessed=40_000_000, transcendentals=0
        ),
        name="attend_backward",
    )(limit, queries, keys, values, grad_rows, attended, lse, inner_part, outer_part)


def on_device(
    hidden_in,
    lengths,
    seq_order,
    query_weight,
    query_bias,
    key_weight,
    value_weight,
    value_bias,
    output_weight,
    output_bias,
    norm1_gain,
    norm1_shift,
    inner_weight,
    inner_bias,
    outer_weight,
    outer_bias,
    norm2_gain,
    norm2_shift,
    cotangent,
):
    width = hidden_in.shape[2]
    count = lax.axis_size("fsdp")
    group = lax.axis_index("fsdp")
    shard = query_bias.shape[0]
    low = jnp.bfloat16
    placed = jnp.swapaxes(jnp.take(hidden_in, seq_order, axis=1), 0, 1)
    vectors = jnp.concatenate(
        (
            jnp.stack(
                (
                    query_bias,
                    value_bias,
                    output_bias,
                    norm1_gain,
                    norm1_shift,
                    outer_bias,
                    norm2_gain,
                    norm2_shift,
                )
            ),
            inner_bias.reshape(4, shard),
        )
    )
    vectors = jnp.pad(vectors, ((0, 4), (0, 128 - shard)))
    weights = jnp.stack((query_weight, key_weight, value_weight, output_weight))
    tokens, weights, vectors = bring_in(placed, weights, vectors)
    w_query, w_key, w_value, w_output = (weights[i].reshape(width, width) for i in range(4))
    vectors = vectors[:, :12, :shard].astype(jnp.float32)
    b_query, b_value, b_output, gain_one, shift_one, b_outer, gain_two, shift_two = (
        vectors[:, i].reshape(width) for i in range(8)
    )
    b_inner = vectors[:, 8:].reshape(-1)
    limits = jnp.take(lengths, jnp.take(seq_order, group[None]))
    all_rows = tokens.reshape(-1, width)
    local_len = all_rows.shape[0] // 4
    token_rows = lax.dynamic_index_in_dim(tokens, lax.axis_index("ctx"), 0, False)
    token_rows = token_rows.reshape(local_len, width)
    queries = (product(token_rows, w_query, ((1,), (0,))) + b_query).astype(low)
    keys = product(all_rows, w_key, ((1,), (0,))).astype(low)
    values = (product(all_rows, w_value, ((1,), (0,))) + b_value).astype(low)
    attended, lse, w_inner, w_outer = attend_forward(
        queries,
        keys,
        values,
        limits,
        inner_weight,
        outer_weight.reshape(4, shard, width),
        count,
    )
    w_inner = w_inner.reshape(width, 4 * width)
    w_outer = w_outer.reshape(4 * width, width)
    mixed_low = attended.astype(low)
    branch = product(mixed_low, w_output, ((1,), (0,))) + b_output
    normed, unit_one, scale_one = norm_forward(
        token_rows.astype(jnp.float32) + branch, gain_one, shift_one
    )
    normed_low = normed.astype(low)
    inner_pre = product(normed_low, w_inner, ((1,), (0,))) + b_inner
    activated = gelu_exact(inner_pre).astype(low)
    outer_out = product(activated, w_outer, ((1,), (0,))) + b_outer
    second, unit_two, scale_two = norm_forward(normed + outer_out, gain_two, shift_two)
    layer_out = second.astype(low).reshape(local_len, 1, width)
    upstream = cotangent.reshape(local_len, width).astype(jnp.float32)
    d_second, grad_gain_two, grad_shift_two = norm_backward(upstream, unit_two, scale_two, gain_two)
    d_outer = d_second.astype(low)
    grad_outer_w = product(activated, d_outer, ((0,), (0,))).astype(low)
    grad_outer_b = jnp.sum(d_outer.astype(jnp.float32), axis=0)
    inner_grad = product(d_outer, w_outer, ((1,), (1,)))
    d_inner = (inner_grad * gelu_slope(inner_pre)).astype(low)
    grad_inner_w = product(normed_low, d_inner, ((0,), (0,))).astype(low)
    grad_inner_b = jnp.sum(d_inner.astype(jnp.float32), axis=0)
    d_normed = d_second + product(d_inner, w_inner, ((1,), (1,)))
    d_res, grad_gain_one, grad_shift_one = norm_backward(d_normed, unit_one, scale_one, gain_one)
    d_branch = d_res.astype(low)
    grad_output_w = product(mixed_low, d_branch, ((0,), (0,))).astype(low)
    grad_output_b = jnp.sum(d_branch.astype(jnp.float32), axis=0)
    d_mixed = product(d_branch, w_output, ((1,), (1,))).astype(low)
    d_query, d_keys, d_values, inner_w, outer_w = attend_backward(
        queries,
        keys,
        values,
        limits,
        d_mixed,
        attended,
        lse,
        grad_inner_w.reshape(count, shard, 4 * width),
        grad_outer_w.reshape(count, 4, shard, width),
    )
    grad_query_w = product(token_rows, d_query, ((0,), (0,))).astype(low)
    grad_query_b = jnp.sum(d_query.astype(jnp.float32), axis=0)
    grad_key_w = product(token_rows, d_keys, ((0,), (0,))).astype(low)
    grad_value_w = product(token_rows, d_values, ((0,), (0,))).astype(low)
    grad_value_b = jnp.sum(d_values.astype(jnp.float32), axis=0)
    d_placed = d_res + product(d_query, w_query, ((1,), (1,)))
    d_placed = d_placed + product(d_keys, w_key, ((1,), (1,)))
    d_placed = d_placed + product(d_values, w_value, ((1,), (1,)))
    back_rows = d_placed.astype(low).reshape(count, local_len // count, width)
    returned = lax.all_to_all(back_rows, "fsdp", split_axis=0, concat_axis=0, tiled=True)
    inverse = jnp.argmax(seq_order[:, None] == jnp.arange(count), axis=0)
    grad_in = jnp.take(jnp.swapaxes(returned, 0, 1), inverse, axis=1)
    attention_w = jnp.stack((grad_query_w, grad_key_w, grad_value_w, grad_output_w))
    small_sums = jnp.concatenate(
        (
            jnp.stack(
                (
                    grad_query_b,
                    grad_value_b,
                    grad_output_b,
                    grad_gain_one,
                    grad_shift_one,
                    grad_outer_b,
                    grad_gain_two,
                    grad_shift_two,
                )
            ),
            grad_inner_b.reshape(4, width),
            jnp.zeros((4, width), jnp.float32),
        )
    )
    attention_w, small_sums = sum_gradients(
        (attention_w.reshape(4, count, shard, width),),
        (0,),
        small_sums,
        shard,
        width,
        count,
    )
    attention_w = attention_w.astype(jnp.float32)
    inner_w = jnp.swapaxes(inner_w, 0, 1).reshape(shard, 4 * width).astype(jnp.float32)
    outer_w = outer_w.reshape(4 * shard, width).astype(jnp.float32)
    small = lax.dynamic_slice_in_dim(small_sums[:8], group * shard, shard, axis=1)
    inner_b = lax.dynamic_slice_in_dim(
        small_sums[8:12].reshape(-1), group * 4 * shard, 4 * shard, axis=0
    )
    return (
        layer_out,
        grad_in,
        attention_w[0],
        small[0],
        attention_w[1],
        attention_w[2],
        small[1],
        attention_w[3],
        small[2],
        small[3],
        small[4],
        inner_w,
        inner_b,
        outer_w,
        small[5],
        small[6],
        small[7],
    )


def solution(mesh):
    placed = (
        P(("ctx", "fsdp"), None, None),
        P(),
        P(),
        P("fsdp", None),
        P("fsdp"),
        P("fsdp", None),
        P("fsdp", None),
        P("fsdp"),
        P("fsdp", None),
        P("fsdp"),
        P("fsdp"),
        P("fsdp"),
        P("fsdp", None),
        P("fsdp"),
        P("fsdp", None),
        P("fsdp"),
        P("fsdp"),
        P("fsdp"),
        P("ctx", "fsdp", None),
    )
    return jax.shard_map(
        on_device,
        mesh=mesh,
        in_specs=placed,
        out_specs=(
            P("ctx", "fsdp", None),
            P(("ctx", "fsdp"), None, None),
            P("fsdp", None),
            P("fsdp"),
            P("fsdp", None),
            P("fsdp", None),
            P("fsdp"),
            P("fsdp", None),
            P("fsdp"),
            P("fsdp"),
            P("fsdp"),
            P("fsdp", None),
            P("fsdp"),
            P("fsdp", None),
            P("fsdp"),
            P("fsdp"),
            P("fsdp"),
        ),
        check_vma=False,
    )
```

```python
import functools

import jax
import jax.numpy as jnp
from jax import lax
from jax.experimental import pallas as pl
from jax.experimental.pallas import tpu as pltpu
from jax.sharding import PartitionSpec as P

SCALE = 64 ** (-0.5)
LOG2E = 1.4426950408889634
LAST_SLOT = 12
VMEM_BYTES = 60 * 2**20

NORM_EPSILON = 1e-12
NEG_BIG = -1e30
ROOT_HALF = 0.7071067811865476
ROOT_TWO_PI = 2.5066282746310002


def norm_forward(source, gain_vec, shift_vec):
    centre = source - jnp.mean(source, axis=-1, keepdims=True)
    inv_scale = lax.rsqrt(jnp.mean(centre * centre, axis=-1, keepdims=True) + NORM_EPSILON)
    unit_rows = centre * inv_scale
    return (unit_rows * gain_vec + shift_vec, unit_rows, inv_scale)


def norm_backward(upstream, unit_rows, inv_scale, gain_vec):
    scaled = upstream * gain_vec
    plain_mean = jnp.mean(scaled, axis=-1, keepdims=True)
    cross_mean = jnp.mean(scaled * unit_rows, axis=-1, keepdims=True)
    d_source = inv_scale * (scaled - plain_mean - unit_rows * cross_mean)
    return (d_source, jnp.sum(upstream * unit_rows, axis=0), jnp.sum(upstream, axis=0))


def gelu_exact(source):
    return 0.5 * source * (1.0 + jax.scipy.special.erf(source * ROOT_HALF))


def gelu_slope(source):
    return (
        0.5 * (1.0 + jax.scipy.special.erf(source * ROOT_HALF))
        + source * jnp.exp(-0.5 * source * source) / ROOT_TWO_PI
    )


def product(left, right, dims):
    return lax.dot_general(left, right, (dims, ((), ())), preferred_element_type=jnp.float32)


def lane_is_low():
    return lax.broadcasted_iota(jnp.int32, (1, 128), 1) < 64


def split_query(query_pair, low_half):
    scaled = query_pair * (SCALE * LOG2E)
    high = scaled.astype(jnp.bfloat16).astype(jnp.float32)
    rest = pltpu.roll(scaled - high, 64, 1)
    return (
        jnp.where(low_half, high, rest).astype(jnp.bfloat16),
        jnp.where(low_half, rest, high).astype(jnp.bfloat16),
    )


def twice(pair, low_half):
    other = pltpu.roll(pair, 64, 1)
    return (
        jnp.where(low_half, pair, other).astype(jnp.bfloat16),
        jnp.where(low_half, other, pair).astype(jnp.bfloat16),
    )


MESH = pl.DeviceIdType.MESH
DMA = pltpu.SemaphoreType.DMA
ANY = pl.BlockSpec(memory_space=pl.ANY)
STAGES = ("start", "after_core", "after_across", "after_group", "finish")


def places():
    ctx, group = lax.axis_index("ctx"), lax.axis_index("fsdp")
    return ctx, group, lax.rem(ctx + 2, 4), ctx + 1 - 2 * lax.rem(ctx, 2)


def remote(source, target, send_sem, recv_sem, where):
    return pltpu.make_async_remote_copy(
        src_ref=source,
        dst_ref=target,
        send_sem=send_sem,
        recv_sem=recv_sem,
        device_id=where,
        device_id_type=MESH,
    )


def greet(count):
    ctx, group, _, _ = places()
    barrier = pltpu.get_barrier_semaphore()

    def one(step, carry):
        pl.semaphore_signal(
            barrier,
            inc=1,
            device_id={"fsdp": lax.rem(group + step, count)},
            device_id_type=MESH,
        )
        return carry

    lax.fori_loop(1, count, one, 0)
    for other in range(1, 4):
        pl.semaphore_signal(
            barrier, inc=1, device_id={"ctx": lax.rem(ctx + other, 4)}, device_id_type=MESH
        )
    pl.semaphore_wait(barrier, count - 1 + 3)


class Gather:
    SCRATCH = 11

    def __init__(self, kinds, sems, count):
        self.kinds, self.count = kinds, count
        self.right_send, self.left_send, self.line_recv = sems[:3]
        self.y_send, self.y_recv, self.x_send, self.x_recv = sems[3:7]
        self.s_send, self.s_recv, self.r_send, self.r_recv = sems[7:11]
        self.ctx, self.group, self.across, self.sibling = places()
        self.line, self.side, self.length = self.group // 2, lax.rem(self.group, 2), count // 2

    @staticmethod
    def scratch(kinds, count):
        return [DMA((kinds, count))] * Gather.SCRATCH

    def copy(self, kind, block, quarter, send, recv, where, own=False):
        mine, place = self.kinds[kind]
        target = place(block, quarter)
        source = mine(quarter) if own else target
        return remote(source, target, send.at[kind, block], recv.at[kind, block], where)

    def right(self, kind, block, own=False):
        there = {"fsdp": lax.rem(self.group + 2, self.count)}
        return self.copy(kind, block, self.ctx, self.right_send, self.line_recv, there, own)

    def left(self, kind, block, own=False):
        there = {"fsdp": lax.rem(self.group - 2 + self.count, self.count)}
        return self.copy(kind, block, self.ctx, self.left_send, self.line_recv, there, own)

    def pair(self, kind, block, own=False):
        there = {"fsdp": self.group + 1 - 2 * self.side}
        return self.copy(kind, block, self.ctx, self.y_send, self.y_recv, there, own)

    def cross(self, kind, block):
        return self.copy(kind, block, self.ctx, self.x_send, self.x_recv, {"ctx": self.across})

    def share(self, kind, block):
        return self.copy(kind, block, self.ctx, self.s_send, self.s_recv, {"ctx": self.sibling})

    def relay(self, kind, block):
        return self.copy(kind, block, self.across, self.r_send, self.r_recv, {"ctx": self.sibling})

    def at(self, line, side):
        return 2 * line + side

    def every(self, body):
        for kind in range(len(self.kinds)):
            body(kind)

    def before(self, distance, body):
        @pl.when(self.line - distance >= 0)
        def _():
            body(self.line - distance)

    def after(self, distance, body):
        @pl.when(self.line + distance < self.length)
        def _():
            body(self.line + distance)

    def start(self):
        block = self.group

        def body(kind):
            self.after(1, lambda _: self.right(kind, block, True).start())
            self.before(1, lambda _: self.left(kind, block, True).start())
            self.pair(kind, block, True).start()

        self.every(body)

    def along(self, distance):
        def from_left(line):
            block = self.at(line, self.side)

            def body(kind):
                self.right(kind, block).wait_recv()
                self.after(1, lambda _: self.right(kind, block).start())
                self.pair(kind, block).start()
                self.cross(kind, block).start()
                self.share(kind, block).start()

            self.every(body)

        def from_right(line):
            block = self.at(line, self.side)

            def body(kind):
                self.left(kind, block).wait_recv()
                self.before(1, lambda _: self.left(kind, block).start())
                self.pair(kind, block).start()
                self.cross(kind, block).start()
                self.share(kind, block).start()

            self.every(body)

        self.before(distance, from_left)
        self.after(distance, from_right)

    def both(self, distance, side, body):
        if isinstance(distance, int) and distance == 0:
            body(self.at(self.line, side))
        else:
            self.before(distance, lambda line: body(self.at(line, side)))
            self.after(distance, lambda line: body(self.at(line, side)))

    def beside(self, distance):
        def one(block):
            def body(kind):
                self.pair(kind, block).wait_recv()
                self.cross(kind, block).start()
                self.share(kind, block).start()

            self.every(body)

        self.both(distance, 1 - self.side, one)

    def crossed(self, distance, side):
        def one(block):
            def body(kind):
                self.cross(kind, block).wait_recv()
                self.relay(kind, block).start()

            self.every(body)

        self.both(distance, self.side if side == 0 else 1 - self.side, one)

    def finish(self):
        def passed(block):
            def body(kind):
                self.cross(kind, block).wait_send()
                self.share(kind, block).wait()
                self.relay(kind, block).wait()

            self.every(body)

        def own(kind):
            self.after(1, lambda _: self.right(kind, self.group).wait_send())
            self.before(1, lambda _: self.left(kind, self.group).wait_send())
            self.pair(kind, self.group).wait_send()

        self.every(own)

        def one(distance, carry):
            def lefts(line):
                block = self.at(line, self.side)

                def body(kind):
                    self.after(1, lambda _: self.right(kind, block).wait_send())
                    self.pair(kind, block).wait_send()

                self.every(body)
                passed(block)

            def rights(line):
                block = self.at(line, self.side)

                def body(kind):
                    self.before(1, lambda _: self.left(kind, block).wait_send())
                    self.pair(kind, block).wait_send()

                self.every(body)
                passed(block)

            self.before(distance, lefts)
            self.after(distance, rights)
            self.both(distance, 1 - self.side, passed)
            return carry

        lax.fori_loop(1, self.length, one, 0)
        passed(self.at(self.line, 1 - self.side))


def arrival_kernel(
    placed,
    weights,
    small,
    tokens,
    gathered,
    small_all,
    tok_stage,
    w_stage,
    small_stage,
    local_sem,
    tok_send,
    tok_recv,
    small_send,
    small_recv,
    x_send,
    x_recv,
    s_send,
    s_recv,
    r_send,
    r_recv,
    *sems,
    count,
):
    ctx, group, across, sibling = places()
    gather = Gather(((lambda q: weights.at[q], lambda b, q: gathered.at[q, b]),), sems, count)
    own_tok = pltpu.make_async_copy(placed.at[group], tok_stage, local_sem.at[0])
    own_w = pltpu.make_async_copy(weights, w_stage, local_sem.at[1])
    own_small = pltpu.make_async_copy(small, small_stage, local_sem.at[2])
    own_tok.start()
    own_w.start()
    own_small.start()
    greet(count)

    def tok_copy(peer, step):
        return remote(
            placed.at[peer],
            tokens.at[ctx, group],
            tok_send.at[step],
            tok_recv.at[step],
            {"fsdp": peer},
        )

    def small_copy(peer, step):
        return remote(
            small, small_all.at[group], small_send.at[step], small_recv.at[step], {"fsdp": peer}
        )

    def pass_on(block, quarter, send, recv, target):
        place = tokens.at[quarter, block]
        return remote(place, place, send.at[block], recv.at[block], {"ctx": target})

    def across_copy(block):
        return pass_on(block, ctx, x_send, x_recv, across)

    def sibling_copy(block):
        return pass_on(block, ctx, s_send, s_recv, sibling)

    def relay_copy(block):
        return pass_on(block, across, r_send, r_recv, sibling)

    def send(step, carry):
        peer = lax.rem(group + step, count)
        tok_copy(peer, step).start()
        small_copy(peer, step).start()
        return carry

    gather.start()
    lax.fori_loop(1, count, send, 0)
    own_tok.wait()
    own_w.wait()
    own_small.wait()
    put_tok = pltpu.make_async_copy(tok_stage, tokens.at[ctx, group], local_sem.at[0])
    put_w = pltpu.make_async_copy(w_stage, gathered.at[:, group], local_sem.at[1])
    put_small = pltpu.make_async_copy(small_stage, small_all.at[group], local_sem.at[2])
    put_tok.start()
    put_w.start()
    put_small.start()
    put_tok.wait()
    across_copy(group).start()
    sibling_copy(group).start()
    put_w.wait()
    put_small.wait()

    def arrive(step, carry):
        origin = lax.rem(group - step + count, count)
        tok_copy(origin, step).wait_recv()
        across_copy(origin).start()
        sibling_copy(origin).start()
        return carry

    length = count // 2
    gather.along(1)
    gather.beside(0)
    lax.fori_loop(1, 3, arrive, 0)

    def advance(distance, carry):
        gather.along(distance)
        gather.beside(distance - 1)
        lax.fori_loop(2 * distance - 1, 2 * distance + 1, arrive, 0)
        return carry

    lax.fori_loop(2, length, advance, 0)
    gather.beside(length - 1)
    lax.fori_loop(2 * length - 1, count, arrive, 0)

    def crossed(distance, carry):
        gather.crossed(distance, 0)
        gather.crossed(distance, 1)
        return carry

    gather.crossed(0, 1)
    lax.fori_loop(1, length, crossed, 0)

    def passed(step, carry):
        origin = lax.rem(group - step + count, count)
        across_copy(origin).wait_recv()
        relay_copy(origin).start()
        return carry

    lax.fori_loop(0, count, passed, 0)
    gather.finish()

    def finish(step, carry):
        origin = lax.rem(group - step + count, count)
        across_copy(origin).wait_send()
        sibling_copy(origin).wait()
        relay_copy(origin).wait()
        return carry

    lax.fori_loop(0, count, finish, 0)

    def sent(step, carry):
        peer = lax.rem(group + step, count)
        tok_copy(peer, step).wait_send()
        small_copy(peer, step).wait()
        return carry

    lax.fori_loop(1, count, sent, 0)


def bring_in(placed, weights, small):
    count, rows, width = placed.shape
    return pl.pallas_call(
        functools.partial(arrival_kernel, count=count),
        in_specs=[ANY] * 3,
        out_specs=[ANY] * 3,
        out_shape=[
            jax.ShapeDtypeStruct((4, count, rows, width), jnp.bfloat16),
            jax.ShapeDtypeStruct((4, count) + weights.shape[1:], jnp.bfloat16),
            jax.ShapeDtypeStruct((count,) + small.shape, jnp.bfloat16),
        ],
        scratch_shapes=[
            pltpu.VMEM((rows, width), jnp.bfloat16),
            pltpu.VMEM((4,) + weights.shape[1:], jnp.bfloat16),
            pltpu.VMEM(small.shape, jnp.bfloat16),
            DMA((3,)),
        ]
        + [DMA((count,))] * 10
        + Gather.scratch(1, count),
        compiler_params=pltpu.CompilerParams(
            collective_id=0, has_side_effects=True, vmem_limit_bytes=8 * 2**20
        ),
        name="bring_in",
    )(placed, weights, small)


class Sum:
    SCRATCH = 16

    def __init__(self, kind, ref, out, scratch, count):
        self.kind, self.ref, self.out, self.count = kind, ref, out, count
        self.near, self.far, self.got_near, self.got_far = scratch[:4]
        self.got_across, self.got_group, self.done = scratch[4:7]
        self.load, self.c_send, self.c_recv, self.x_send, self.x_recv = scratch[7:12]
        self.g_send, self.g_recv, self.o_send, self.o_recv = scratch[12:16]
        self.ctx, self.group, self.across, self.sibling = places()
        self.width = self.near.shape[-1]

    @staticmethod
    def scratch(count, rows, width):
        return (
            [pltpu.VMEM((count, rows, width), jnp.bfloat16)] * 6
            + [pltpu.VMEM((rows, width), jnp.bfloat16)]
            + [DMA((2,))] * 3
            + [DMA((count,))] * 4
            + [DMA((4,))] * 2
        )

    def quarter(self, index):
        if self.kind == 0:
            return self.ref.at[index]
        if self.kind == 1:
            start = pl.multiple_of(index * self.width, self.width)
            return self.ref.at[:, :, pl.ds(start, self.width)]
        return self.ref.at[:, index]

    def loads(self):
        return (
            pltpu.make_async_copy(self.quarter(self.across), self.far, self.load.at[0]),
            pltpu.make_async_copy(self.quarter(self.ctx), self.near, self.load.at[1]),
        )

    def cores(self):
        beyond = lax.rem(self.sibling + 2, 4)
        there = {"ctx": self.sibling}
        return (
            remote(self.quarter(beyond), self.got_far, self.c_send.at[0], self.c_recv.at[0], there),
            remote(
                self.quarter(self.sibling),
                self.got_near,
                self.c_send.at[1],
                self.c_recv.at[1],
                there,
            ),
        )

    def x_copy(self, block):
        return remote(
            self.far.at[block],
            self.got_across.at[block],
            self.x_send.at[block],
            self.x_recv.at[block],
            {"ctx": self.across},
        )

    def g_copy(self, peer, step):
        return remote(
            self.near.at[peer],
            self.got_group.at[step],
            self.g_send.at[step],
            self.g_recv.at[step],
            {"fsdp": peer},
        )

    def o_copy(self, other):
        return remote(
            self.done,
            self.out.at[self.ctx],
            self.o_send.at[other],
            self.o_recv.at[other],
            {"ctx": lax.rem(self.ctx + other, 4)},
        )

    def own_out(self):
        return pltpu.make_async_copy(self.done, self.out.at[self.ctx], self.load.at[0])

    def add(self, total, other):
        def one(block, carry):
            both = total[block].astype(jnp.float32) + other[block].astype(jnp.float32)
            total[block] = both.astype(jnp.bfloat16)
            return carry

        lax.fori_loop(0, self.count, one, 0)

    def start(self):
        for copy in self.loads() + self.cores():
            copy.start()

    def after_core(self):
        loads, cores = self.loads(), self.cores()
        loads[0].wait()
        cores[0].wait_recv()
        self.add(self.far, self.got_far)

        def send(step, carry):
            self.x_copy(lax.rem(self.group + 1 + step, self.count)).start()
            return carry

        lax.fori_loop(0, self.count, send, 0)
        loads[1].wait()
        cores[1].wait_recv()
        self.add(self.near, self.got_near)
        cores[0].wait_send()
        cores[1].wait_send()

    def after_across(self):
        def one(step, carry):
            block = lax.rem(self.group + step, self.count)
            self.x_copy(block).wait()
            both = self.near[block].astype(jnp.float32) + self.got_across[block].astype(jnp.float32)
            self.near[block] = both.astype(jnp.bfloat16)
            self.g_copy(block, step).start()
            return carry

        lax.fori_loop(1, self.count, one, 0)
        self.x_copy(self.group).wait()

    def after_group(self):
        group = self.group
        total = self.near[group].astype(jnp.float32) + self.got_across[group].astype(jnp.float32)

        def one(step, total):
            self.g_copy(lax.rem(group + step, self.count), step).wait()
            return total + self.got_group[step].astype(jnp.float32)

        self.done[...] = lax.fori_loop(1, self.count, one, total).astype(jnp.bfloat16)
        self.own_out().start()
        for other in range(1, 4):
            self.o_copy(other).start()

    def finish(self):
        self.own_out().wait()
        for other in range(1, 4):
            self.o_copy(other).wait()


class VectorSum:
    SCRATCH = 9

    def __init__(self, ref, out, scratch, count):
        self.ref, self.out, self.count = ref, out, count
        self.total, self.got_ctx, self.got_group = scratch[:3]
        self.load, self.c_send, self.c_recv, self.g_send, self.g_recv = scratch[3:8]
        self.result = scratch[8]
        self.ctx, self.group, _, _ = places()

    @staticmethod
    def scratch(count, rows, width):
        return [
            pltpu.VMEM((rows, width), jnp.float32),
            pltpu.VMEM((4, rows, width), jnp.float32),
            pltpu.VMEM((count, rows, width), jnp.float32),
            DMA((2,)),
            DMA((4,)),
            DMA((4,)),
            DMA((count,)),
            DMA((count,)),
            pltpu.VMEM((rows, width), jnp.float32),
        ]

    def own(self):
        return pltpu.make_async_copy(self.ref, self.total, self.load.at[0])

    def own_out(self):
        return pltpu.make_async_copy(self.result, self.out, self.load.at[1])

    def c_copy(self, other):
        return remote(
            self.ref,
            self.got_ctx.at[other],
            self.c_send.at[other],
            self.c_recv.at[other],
            {"ctx": lax.rem(self.ctx + other, 4)},
        )

    def g_copy(self, step):
        return remote(
            self.total,
            self.got_group.at[step],
            self.g_send.at[step],
            self.g_recv.at[step],
            {"fsdp": lax.rem(self.group + step, self.count)},
        )

    def start(self):
        self.own().start()
        for other in range(1, 4):
            self.c_copy(other).start()

    def after_core(self):
        self.own().wait()
        total = self.total[...]
        for other in range(1, 4):
            self.c_copy(other).wait()
            total = total + self.got_ctx[other]
        self.total[...] = total

        def one(step, carry):
            self.g_copy(step).start()
            return carry

        lax.fori_loop(1, self.count, one, 0)

    def after_across(self):
        pass

    def after_group(self):
        def one(step, total):
            self.g_copy(step).wait()
            return total + self.got_group[step]

        self.result[...] = lax.fori_loop(1, self.count, one, self.total[...])
        self.own_out().start()

    def finish(self):
        self.own_out().wait()


class LateSum:
    SCRATCH = 16

    def __init__(self, kind, ref, out, scratch, count):
        self.kind, self.ref, self.out, self.count = kind, ref, out, count
        self.near, self.got, self.got_group, self.half, self.got_across, self.done = scratch[:6]
        self.load, self.c_send, self.c_recv, self.g_send, self.g_recv = scratch[6:11]
        self.x_send, self.x_recv, self.o_send, self.o_recv, self.put = scratch[11:16]
        self.ctx, self.group, self.across, self.sibling = places()
        self.core = lax.rem(self.ctx, 2)
        self.width = self.near.shape[-1]

    @staticmethod
    def scratch(count, rows, width):
        return (
            [pltpu.VMEM((count, 2, rows, width), jnp.bfloat16)] * 3
            + [pltpu.VMEM((2, rows, width), jnp.bfloat16)] * 3
            + [DMA((2,))] * 3
            + [DMA((count,))] * 2
            + [DMA((2,))] * 5
        )

    def quarter(self, index):
        if self.kind == 1:
            start = pl.multiple_of(index * self.width, self.width)
            return self.ref.at[:, :, pl.ds(start, self.width)]
        return self.ref.at[:, index]

    def load_copy(self, half):
        return pltpu.make_async_copy(
            self.quarter(2 * half + self.core), self.near.at[:, half], self.load.at[half]
        )

    def core_copy(self, half):
        return remote(
            self.quarter(2 * half + 1 - self.core),
            self.got.at[:, half],
            self.c_send.at[half],
            self.c_recv.at[half],
            {"ctx": self.sibling},
        )

    def group_copy(self, step):
        peer = lax.rem(self.group + step, self.count)
        return remote(
            self.near.at[peer],
            self.got_group.at[step],
            self.g_send.at[step],
            self.g_recv.at[step],
            {"fsdp": peer},
        )

    def x_copy(self):
        return remote(
            self.half, self.got_across, self.x_send.at[0], self.x_recv.at[0], {"ctx": self.across}
        )

    def out_copy(self, half):
        return remote(
            self.done.at[half],
            self.out.at[2 * half + self.core],
            self.o_send.at[half],
            self.o_recv.at[half],
            {"ctx": self.sibling},
        )

    def own_out(self, half):
        return pltpu.make_async_copy(
            self.done.at[half], self.out.at[2 * half + self.core], self.put.at[half]
        )

    def start(self):
        for half in range(2):
            self.load_copy(half).start()
            self.core_copy(half).start()

    def after_core(self):
        for half in range(2):
            self.load_copy(half).wait()
            self.core_copy(half).wait()

        def one(step, carry):
            block = lax.rem(self.group + step, self.count)
            both = self.near[block].astype(jnp.float32) + self.got[block].astype(jnp.float32)
            self.near[block] = both.astype(jnp.bfloat16)
            return carry

        lax.fori_loop(0, self.count, one, 0)

        def send(step, carry):
            self.group_copy(step).start()
            return carry

        lax.fori_loop(1, self.count, send, 0)

    def after_group(self):
        def one(step, total):
            self.group_copy(step).wait()
            return total + self.got_group[step].astype(jnp.float32)

        total = lax.fori_loop(1, self.count, one, self.near[self.group].astype(jnp.float32))
        self.half[...] = total.astype(jnp.bfloat16)
        self.x_copy().start()

    def after_across(self):
        self.x_copy().wait()
        both = self.half[...].astype(jnp.float32) + self.got_across[...].astype(jnp.float32)
        self.done[...] = both.astype(jnp.bfloat16)
        for half in range(2):
            self.own_out(half).start()
            self.out_copy(half).start()

    def finish(self):
        for half in range(2):
            self.own_out(half).wait()
            self.out_copy(half).wait()


def sums_kernel(*refs, kinds, count):
    parts = len(kinds)
    ins, outs, rest = refs[: parts + 1], refs[parts + 1 : 2 * parts + 2], refs[2 * parts + 2 :]
    jobs = [VectorSum(ins[parts], outs[parts], rest[: VectorSum.SCRATCH], count)]
    rest = rest[VectorSum.SCRATCH :]
    for index, kind in enumerate(kinds):
        own = rest[index * Sum.SCRATCH : (index + 1) * Sum.SCRATCH]
        jobs.append(Sum(kind, ins[index], outs[index], own, count))
    greet(count)
    for stage in STAGES:
        for job in jobs:
            getattr(job, stage)()


def sum_gradients(parts, kinds, vectors, rows, width, count):
    scratch = VectorSum.scratch(count, *vectors.shape)
    for _ in kinds:
        scratch += Sum.scratch(count, rows, width)
    return pl.pallas_call(
        functools.partial(sums_kernel, kinds=kinds, count=count),
        in_specs=[ANY] * (len(kinds) + 1),
        out_specs=[ANY] * (len(kinds) + 1),
        out_shape=[jax.ShapeDtypeStruct((4, rows, width), jnp.bfloat16)] * len(kinds)
        + [jax.ShapeDtypeStruct(vectors.shape, jnp.float32)],
        scratch_shapes=scratch,
        compiler_params=pltpu.CompilerParams(
            collective_id=1, has_side_effects=True, vmem_limit_bytes=VMEM_BYTES
        ),
        name="sum_gradients",
    )(*parts, vectors)


def gather_plan(length):
    stretch = max(length - 2, 1)
    slots = [[] for _ in range(LAST_SLOT + 1)]

    def put(name, at, over, first):
        for distance in range(1, length):
            slot = min(at + (distance - 1) * over // stretch, LAST_SLOT)
            events = slots[slot]
            if events and events[-1][0] == name:
                events[-1] = (name, events[-1][1], distance + 1)
            else:
                events.append((name, distance, distance + 1))
        if first:
            slots[first].append((name, 0, 1))

    put("along", 2, 4, 0)
    put("beside", 5, 3, 2)
    put("line", 6, 4, 0)
    put("pair", 8, 4, 6)
    return slots


def forward_kernel(
    limit_ref,
    query_ref,
    key_ref,
    value_ref,
    inner_ref,
    outer_ref,
    attended_ref,
    lse_ref,
    inner_all,
    outer_all,
    *scratch,
    key_rows,
    count,
):
    pair = pl.program_id(0)
    pairs = pl.num_programs(0) - 1
    inner_stage, outer_stage, local, *sems = scratch
    width = outer_ref.shape[-1]

    def columns(quarter):
        return pl.ds(pl.multiple_of(quarter * width, width), width)

    kinds = (
        (lambda q: inner_ref.at[:, columns(q)], lambda b, q: inner_all.at[b, :, columns(q)]),
        (lambda q: outer_ref.at[q], lambda b, q: outer_all.at[b, q]),
    )
    gather = Gather(kinds, sems, count)
    loads = (
        pltpu.make_async_copy(inner_ref, inner_stage, local.at[0]),
        pltpu.make_async_copy(outer_ref, outer_stage, local.at[1]),
    )
    puts = (
        pltpu.make_async_copy(inner_stage, inner_all.at[gather.group], local.at[2]),
        pltpu.make_async_copy(outer_stage, outer_all.at[gather.group], local.at[3]),
    )
    plan = gather_plan(count // 2)

    def communicate(events):
        for name, first, last in events:
            act = {
                "along": gather.along,
                "beside": gather.beside,
                "line": lambda distance: gather.crossed(distance, 0),
                "pair": lambda distance: gather.crossed(distance, 1),
            }[name]
            if last - first == 1:
                act(first)
            else:

                def one(distance, carry, act=act):
                    act(distance)
                    return carry

                lax.fori_loop(first, last, one, 0)

    @pl.when(pair == 0)
    def _():
        greet(count)
        for load in loads:
            load.start()
        gather.start()
        for load, put in zip(loads, puts):
            load.wait()
            put.start()

    @pl.when(pair == pairs)
    def _():
        communicate(plan[LAST_SLOT])
        gather.finish()
        for put in puts:
            put.wait()

    @pl.when(pair < pairs)
    def _():
        low_half = lane_is_low()
        limit = limit_ref[0]
        queries = split_query(query_ref[...].astype(jnp.float32), low_half)
        query_rows = query_ref.shape[0]

        def step(tile, state):
            for slot in range(1, LAST_SLOT):
                if plan[slot]:

                    @pl.when(2 * pair + tile == slot)
                    def _(slot=slot):
                        communicate(plan[slot])

            start = pl.multiple_of(tile * key_rows, key_rows)
            usable = start + lax.broadcasted_iota(jnp.int32, (key_rows, 1), 0) < limit
            key_tile = key_ref[pl.ds(start, key_rows), :].astype(jnp.float32)
            keys = twice(jnp.where(usable, key_tile, key_ref[0:1, :].astype(jnp.float32)), low_half)
            value_tile = value_ref[pl.ds(start, key_rows), :].astype(jnp.float32)
            value_tile = jnp.where(usable, value_tile, 0.0)
            count = jnp.where(usable, 1.0, 0.0)
            values = (
                jnp.where(low_half, value_tile, count).astype(jnp.bfloat16),
                jnp.where(low_half, count, value_tile).astype(jnp.bfloat16),
            )
            fresh = []
            for head in range(2):
                top, total = state[head]
                scores = product(queries[head], keys[head], ((1,), (1,)))
                new_top = jnp.maximum(top, jnp.max(scores, axis=1, keepdims=True))
                weights = jnp.exp2(scores - new_top).astype(jnp.bfloat16)
                total = total * jnp.exp2(top - new_top) + product(weights, values[head], ((1,), (0,)))
                fresh.append((new_top, total))
            return tuple(fresh)

        empty = (
            jnp.full((query_rows, 1), NEG_BIG, jnp.float32),
            jnp.zeros((query_rows, 128), jnp.float32),
        )
        (top_a, total_a), (top_b, total_b) = lax.fori_loop(
            0, key_ref.shape[0] // key_rows, step, (empty, empty)
        )
        mass_a, mass_b = total_a[:, 64:65], total_b[:, 0:1]
        attended_ref[...] = jnp.where(low_half, total_a / mass_a, total_b / mass_b)
        lse = jnp.where(low_half, top_a + jnp.log2(mass_a), top_b + jnp.log2(mass_b)).T
        lse_ref[0, 0:1, :] = lse[0:1, :]
        lse_ref[0, 1:2, :] = lse[64:65, :]


def attend_forward(queries, keys, values, limit, inner, outer, count):
    rows, width = queries.shape
    full = keys.shape[0]
    pairs = width // 128
    shard = inner.shape[0]
    now = lambda pair, *_: (0, jnp.minimum(pair, pairs - 1))
    row_spec = pl.BlockSpec((rows, 128), now)
    key_spec = pl.BlockSpec((full, 128), now)
    return pl.pallas_call(
        functools.partial(forward_kernel, key_rows=full // 2, count=count),
        grid_spec=pltpu.PrefetchScalarGridSpec(
            num_scalar_prefetch=1,
            grid=(pairs + 1,),
            in_specs=[row_spec, key_spec, key_spec, ANY, ANY],
            out_specs=[
                row_spec,
                pl.BlockSpec((1, 2, rows), lambda pair, *_: (jnp.minimum(pair, pairs - 1), 0, 0)),
                ANY,
                ANY,
            ],
            scratch_shapes=[
                pltpu.VMEM((shard, 4 * width), jnp.bfloat16),
                pltpu.VMEM((4, shard, width), jnp.bfloat16),
                DMA((4,)),
            ]
            + Gather.scratch(2, count),
        ),
        out_shape=[
            jax.ShapeDtypeStruct((rows, width), jnp.float32),
            jax.ShapeDtypeStruct((pairs, 2, rows), jnp.float32),
            jax.ShapeDtypeStruct((count, shard, 4 * width), jnp.bfloat16),
            jax.ShapeDtypeStruct((count, 4, shard, width), jnp.bfloat16),
        ],
        compiler_params=pltpu.CompilerParams(
            collective_id=3, has_side_effects=True, vmem_limit_bytes=VMEM_BYTES
        ),
        cost_estimate=pl.CostEstimate(
            flops=16 * rows * full * width, bytes_accessed=20_000_000, transcendentals=0
        ),
        name="attend_forward",
    )(limit, queries, keys, values, inner, outer)


def backward_kernel(
    limit_ref,
    query_ref,
    key_ref,
    value_ref,
    grad_ref,
    attended_ref,
    lse_ref,
    inner_ref,
    outer_ref,
    d_query_ref,
    d_key_ref,
    d_value_ref,
    inner_out,
    outer_out,
    query_sum,
    part,
    got_core,
    far,
    near,
    got_x,
    core_send,
    core_recv,
    x_send,
    x_recv,
    *rest,
    count,
):
    pair = pl.program_id(0)
    pairs = pl.num_programs(0) - 1
    slot = lax.rem(pair, 2)
    ctx, _, across, sibling = places()
    key_rows = query_ref.shape[0]
    jobs = [
        LateSum(1, inner_ref, inner_out, rest[: LateSum.SCRATCH], count),
        LateSum(2, outer_ref, outer_out, rest[LateSum.SCRATCH :], count),
    ]

    def core_copy(which):
        return remote(
            part.at[which],
            got_core.at[slot, which],
            core_send.at[which],
            core_recv.at[slot, which],
            {"ctx": sibling},
        )

    def x_copy(where):
        return remote(
            far.at[where], got_x.at[where], x_send.at[where], x_recv.at[where], {"ctx": across}
        )

    def settle():
        where = 1 - slot
        x_copy(where).wait()
        for kind, ref in enumerate((d_key_ref, d_value_ref)):
            both = near[where, kind].astype(jnp.float32) + got_x[where, kind].astype(jnp.float32)
            ref[...] = both.astype(jnp.bfloat16)

    @pl.when(pair == 0)
    def _():
        greet(count)
        for job in jobs:
            job.start()

    @pl.when(pair == 1)
    def _():
        for job in jobs:
            job.after_core()

    @pl.when(pair < pairs)
    def _():
        low_half = lane_is_low()
        high_half = jnp.logical_not(low_half)
        lane = lax.broadcasted_iota(jnp.int32, (1, 128), 1)
        limit = limit_ref[0]
        query_pair = query_ref[...].astype(jnp.float32)
        queries = split_query(query_pair, low_half)
        scaled = query_pair * SCALE
        grad_pair = grad_ref[...].astype(jnp.float32)
        overlap = grad_pair * attended_ref[...]
        own_query, own_grad, joined_grad = [], [], []
        for head in range(2):
            mine = low_half if head == 0 else high_half
            own_query.append(jnp.where(mine, scaled, 0.0).astype(jnp.bfloat16))
            own_grad.append(jnp.where(mine, grad_pair, 0.0).astype(jnp.bfloat16))
            delta = -jnp.sum(jnp.where(mine, overlap, 0.0), axis=1, keepdims=True)
            first = delta.astype(jnp.bfloat16).astype(jnp.float32)
            second = (delta - first).astype(jnp.bfloat16).astype(jnp.float32)
            third = delta - first - second
            spare = 64 * (1 - head)
            joined = jnp.where(lane == spare + 2, third, 0.0)
            joined = jnp.where(lane == spare + 1, second, joined)
            joined = jnp.where(lane == spare, first, joined)
            joined_grad.append(jnp.where(mine, grad_pair, joined).astype(jnp.bfloat16))
        query_sum[...] = jnp.zeros_like(query_sum)

        def step(tile, carry):
            odd = lax.rem(tile, 2)
            quarter = lax.rem(sibling + odd * (ctx - sibling) + 2 * (1 - tile // 2), 4)
            start = pl.multiple_of(quarter * key_rows, key_rows)
            usable = start + lax.broadcasted_iota(jnp.int32, (key_rows, 1), 0) < limit
            key_tile = key_ref[pl.ds(start, key_rows), :].astype(jnp.float32)
            value_tile = value_ref[pl.ds(start, key_rows), :].astype(jnp.float32)
            keys = twice(jnp.where(usable, key_tile, key_ref[0:1, :].astype(jnp.float32)), low_half)
            own_tile = jnp.where(usable, key_tile * SCALE, 0.0)
            key_piece = value_piece = None
            for head in range(2):
                mine = low_half if head == 0 else high_half
                values = jnp.where(mine, value_tile, 1.0).astype(jnp.bfloat16)
                own_key = jnp.where(mine, own_tile, 0.0).astype(jnp.bfloat16)
                scores = product(keys[head], queries[head], ((1,), (1,)))
                probs = jnp.exp2(scores - lse_ref[0, head : head + 1, :])
                slopes = product(values, joined_grad[head], ((1,), (1,)))
                score_grads = (probs * slopes).astype(jnp.bfloat16)
                value_term = product(probs.astype(jnp.bfloat16), own_grad[head], ((1,), (0,)))
                key_term = product(score_grads, own_query[head], ((1,), (0,)))
                value_piece = value_term if value_piece is None else value_piece + value_term
                key_piece = key_term if key_piece is None else key_piece + key_term
                query_sum[...] += product(own_key, score_grads, ((0,), (0,)))
            pieces = (jnp.where(usable, key_piece, 0.0), jnp.where(usable, value_piece, 0.0))

            @pl.when(odd == 0)
            def _():
                which = tile // 2
                for kind in range(2):
                    part[which, kind] = pieces[kind].astype(jnp.bfloat16)
                core_copy(which).start()

            @pl.when(tile == 1)
            def _():
                @pl.when(pair > 0)
                def _():
                    settle()

                core_copy(0).wait_recv()
                for kind in range(2):
                    both = pieces[kind] + got_core[slot, 0, kind].astype(jnp.float32)
                    far[slot, kind] = both.astype(jnp.bfloat16)
                x_copy(slot).start()

            @pl.when(tile == 3)
            def _():
                core_copy(1).wait_recv()
                for kind in range(2):
                    both = pieces[kind] + got_core[slot, 1, kind].astype(jnp.float32)
                    near[slot, kind] = both.astype(jnp.bfloat16)
                core_copy(0).wait_send()
                core_copy(1).wait_send()

            return carry

        lax.fori_loop(0, 4, step, 0)
        d_query_ref[...] = query_sum[...].T.astype(jnp.bfloat16)

    @pl.when(pair == pairs)
    def _():
        for job in jobs:
            job.after_group()
        settle()
        for job in jobs:
            job.after_across()
        for job in jobs:
            job.finish()


def attend_backward(queries, keys, values, limit, grad_rows, attended, lse, inner_part, outer_part):
    rows, width = queries.shape
    full = keys.shape[0]
    pairs = width // 128
    count, shard = inner_part.shape[:2]
    now = lambda pair, *_: (0, jnp.minimum(pair, pairs - 1))
    before = lambda pair, *_: (0, jnp.maximum(pair - 1, 0))
    row_spec = pl.BlockSpec((rows, 128), now)
    key_spec = pl.BlockSpec((full, 128), now)
    sum_spec = pl.BlockSpec((rows, 128), before)
    tile = (2, rows, 128)
    return pl.pallas_call(
        functools.partial(backward_kernel, count=count),
        grid_spec=pltpu.PrefetchScalarGridSpec(
            num_scalar_prefetch=1,
            grid=(pairs + 1,),
            in_specs=[
                row_spec,
                key_spec,
                key_spec,
                row_spec,
                row_spec,
                pl.BlockSpec((1, 2, rows), lambda pair, *_: (jnp.minimum(pair, pairs - 1), 0, 0)),
                ANY,
                ANY,
            ],
            out_specs=[row_spec, sum_spec, sum_spec, ANY, ANY],
            scratch_shapes=[
                pltpu.VMEM((128, rows), jnp.float32),
                pltpu.VMEM((2,) + tile, jnp.bfloat16),
                pltpu.VMEM((2, 2) + tile, jnp.bfloat16),
                pltpu.VMEM((2,) + tile, jnp.bfloat16),
                pltpu.VMEM((2,) + tile, jnp.bfloat16),
                pltpu.VMEM((2,) + tile, jnp.bfloat16),
                DMA((2,)),
                DMA((2, 2)),
                DMA((2,)),
                DMA((2,)),
            ]
            + LateSum.scratch(count, shard, width) * 2,
        ),
        out_shape=[jax.ShapeDtypeStruct((rows, width), jnp.bfloat16)] * 3
        + [jax.ShapeDtypeStruct((4, shard, width), jnp.bfloat16)] * 2,
        compiler_params=pltpu.CompilerParams(
            collective_id=2, has_side_effects=True, vmem_limit_bytes=VMEM_BYTES
        ),
        cost_estimate=pl.CostEstimate(
            flops=40 * rows * full * width, bytes_accessed=40_000_000, transcendentals=0
        ),
        name="attend_backward",
    )(limit, queries, keys, values, grad_rows, attended, lse, inner_part, outer_part)


def on_device(
    hidden_in,
    lengths,
    seq_order,
    query_weight,
    query_bias,
    key_weight,
    value_weight,
    value_bias,
    output_weight,
    output_bias,
    norm1_gain,
    norm1_shift,
    inner_weight,
    inner_bias,
    outer_weight,
    outer_bias,
    norm2_gain,
    norm2_shift,
    cotangent,
):
    width = hidden_in.shape[2]
    count = lax.axis_size("fsdp")
    group = lax.axis_index("fsdp")
    shard = query_bias.shape[0]
    low = jnp.bfloat16
    placed = jnp.swapaxes(jnp.take(hidden_in, seq_order, axis=1), 0, 1)
    vectors = jnp.concatenate(
        (
            jnp.stack(
                (
                    query_bias,
                    value_bias,
                    output_bias,
                    norm1_gain,
                    norm1_shift,
                    outer_bias,
                    norm2_gain,
                    norm2_shift,
                )
            ),
            inner_bias.reshape(4, shard),
        )
    )
    vectors = jnp.pad(vectors, ((0, 4), (0, 128 - shard)))
    weights = jnp.stack((query_weight, key_weight, value_weight, output_weight))
    tokens, weights, vectors = bring_in(placed, weights, vectors)
    w_query, w_key, w_value, w_output = (weights[i].reshape(width, width) for i in range(4))
    vectors = vectors[:, :12, :shard].astype(jnp.float32)
    b_query, b_value, b_output, gain_one, shift_one, b_outer, gain_two, shift_two = (
        vectors[:, i].reshape(width) for i in range(8)
    )
    b_inner = vectors[:, 8:].reshape(-1)
    limits = jnp.take(lengths, jnp.take(seq_order, group[None]))
    all_rows = tokens.reshape(-1, width)
    local_len = all_rows.shape[0] // 4
    token_rows = lax.dynamic_index_in_dim(tokens, lax.axis_index("ctx"), 0, False)
    token_rows = token_rows.reshape(local_len, width)
    queries = (product(token_rows, w_query, ((1,), (0,))) + b_query).astype(low)
    keys = product(all_rows, w_key, ((1,), (0,))).astype(low)
    values = (product(all_rows, w_value, ((1,), (0,))) + b_value).astype(low)
    attended, lse, w_inner, w_outer = attend_forward(
        queries,
        keys,
        values,
        limits,
        inner_weight,
        outer_weight.reshape(4, shard, width),
        count,
    )
    w_inner = w_inner.reshape(width, 4 * width)
    w_outer = w_outer.reshape(4 * width, width)
    mixed_low = attended.astype(low)
    branch = product(mixed_low, w_output, ((1,), (0,))) + b_output
    normed, unit_one, scale_one = norm_forward(
        token_rows.astype(jnp.float32) + branch, gain_one, shift_one
    )
    normed_low = normed.astype(low)
    inner_pre = product(normed_low, w_inner, ((1,), (0,))) + b_inner
    activated = gelu_exact(inner_pre).astype(low)
    outer_out = product(activated, w_outer, ((1,), (0,))) + b_outer
    second, unit_two, scale_two = norm_forward(normed + outer_out, gain_two, shift_two)
    layer_out = second.astype(low).reshape(local_len, 1, width)
    upstream = cotangent.reshape(local_len, width).astype(jnp.float32)
    d_second, grad_gain_two, grad_shift_two = norm_backward(upstream, unit_two, scale_two, gain_two)
    d_outer = d_second.astype(low)
    grad_outer_w = product(activated, d_outer, ((0,), (0,))).astype(low)
    grad_outer_b = jnp.sum(d_outer.astype(jnp.float32), axis=0)
    inner_grad = product(d_outer, w_outer, ((1,), (1,)))
    d_inner = (inner_grad * gelu_slope(inner_pre)).astype(low)
    grad_inner_w = product(normed_low, d_inner, ((0,), (0,))).astype(low)
    grad_inner_b = jnp.sum(d_inner.astype(jnp.float32), axis=0)
    d_normed = d_second + product(d_inner, w_inner, ((1,), (1,)))
    d_res, grad_gain_one, grad_shift_one = norm_backward(d_normed, unit_one, scale_one, gain_one)
    d_branch = d_res.astype(low)
    grad_output_w = product(mixed_low, d_branch, ((0,), (0,))).astype(low)
    grad_output_b = jnp.sum(d_branch.astype(jnp.float32), axis=0)
    d_mixed = product(d_branch, w_output, ((1,), (1,))).astype(low)
    d_query, d_keys, d_values, inner_w, outer_w = attend_backward(
        queries,
        keys,
        values,
        limits,
        d_mixed,
        attended,
        lse,
        grad_inner_w.reshape(count, shard, 4 * width),
        grad_outer_w.reshape(count, 4, shard, width),
    )
    grad_query_w = product(token_rows, d_query, ((0,), (0,))).astype(low)
    grad_query_b = jnp.sum(d_query.astype(jnp.float32), axis=0)
    grad_key_w = product(token_rows, d_keys, ((0,), (0,))).astype(low)
    grad_value_w = product(token_rows, d_values, ((0,), (0,))).astype(low)
    grad_value_b = jnp.sum(d_values.astype(jnp.float32), axis=0)
    d_placed = d_res + product(d_query, w_query, ((1,), (1,)))
    d_placed = d_placed + product(d_keys, w_key, ((1,), (1,)))
    d_placed = d_placed + product(d_values, w_value, ((1,), (1,)))
    back_rows = d_placed.astype(low).reshape(count, local_len // count, width)
    returned = lax.all_to_all(back_rows, "fsdp", split_axis=0, concat_axis=0, tiled=True)
    inverse = jnp.argmax(seq_order[:, None] == jnp.arange(count), axis=0)
    grad_in = jnp.take(jnp.swapaxes(returned, 0, 1), inverse, axis=1)
    attention_w = jnp.stack((grad_query_w, grad_key_w, grad_value_w, grad_output_w))
    small_sums = jnp.concatenate(
        (
            jnp.stack(
                (
                    grad_query_b,
                    grad_value_b,
                    grad_output_b,
                    grad_gain_one,
                    grad_shift_one,
                    grad_outer_b,
                    grad_gain_two,
                    grad_shift_two,
                )
            ),
            grad_inner_b.reshape(4, width),
            jnp.zeros((4, width), jnp.float32),
        )
    )
    attention_w, small_sums = sum_gradients(
        (attention_w.reshape(4, count, shard, width),),
        (0,),
        small_sums,
        shard,
        width,
        count,
    )
    attention_w = attention_w.astype(jnp.float32)
    inner_w = jnp.swapaxes(inner_w, 0, 1).reshape(shard, 4 * width).astype(jnp.float32)
    outer_w = outer_w.reshape(4 * shard, width).astype(jnp.float32)
    small = lax.dynamic_slice_in_dim(small_sums[:8], group * shard, shard, axis=1)
    inner_b = lax.dynamic_slice_in_dim(
        small_sums[8:12].reshape(-1), group * 4 * shard, 4 * shard, axis=0
    )
    return (
        layer_out,
        grad_in,
        attention_w[0],
        small[0],
        attention_w[1],
        attention_w[2],
        small[1],
        attention_w[3],
        small[2],
        small[3],
        small[4],
        inner_w,
        inner_b,
        outer_w,
        small[5],
        small[6],
        small[7],
    )


def solution(mesh):
    placed = (
        P(("ctx", "fsdp"), None, None),
        P(),
        P(),
        P("fsdp", None),
        P("fsdp"),
        P("fsdp", None),
        P("fsdp", None),
        P("fsdp"),
        P("fsdp", None),
        P("fsdp"),
        P("fsdp"),
        P("fsdp"),
        P("fsdp", None),
        P("fsdp"),
        P("fsdp", None),
        P("fsdp"),
        P("fsdp"),
        P("fsdp"),
        P("ctx", "fsdp", None),
    )
    return jax.shard_map(
        on_device,
        mesh=mesh,
        in_specs=placed,
        out_specs=(
            P("ctx", "fsdp", None),
            P(("ctx", "fsdp"), None, None),
            P("fsdp", None),
            P("fsdp"),
            P("fsdp", None),
            P("fsdp", None),
            P("fsdp"),
            P("fsdp", None),
            P("fsdp"),
            P("fsdp"),
            P("fsdp"),
            P("fsdp", None),
            P("fsdp"),
            P("fsdp", None),
            P("fsdp"),
            P("fsdp"),
            P("fsdp"),
        ),
        check_vma=False,
    )
```

```python
import functools

import jax
import jax.numpy as jnp
from jax import lax
from jax.experimental import pallas as pl
from jax.experimental.pallas import tpu as pltpu
from jax.sharding import PartitionSpec as P

SCALE = 64 ** (-0.5)
LOG2E = 1.4426950408889634
LAST_SLOT = 12
VMEM_BYTES = 60 * 2**20

NORM_EPSILON = 1e-12
NEG_BIG = -1e30
ROOT_HALF = 0.7071067811865476
ROOT_TWO_PI = 2.5066282746310002


def norm_forward(source, gain_vec, shift_vec):
    centre = source - jnp.mean(source, axis=-1, keepdims=True)
    inv_scale = lax.rsqrt(jnp.mean(centre * centre, axis=-1, keepdims=True) + NORM_EPSILON)
    unit_rows = centre * inv_scale
    return (unit_rows * gain_vec + shift_vec, unit_rows, inv_scale)


def norm_backward(upstream, unit_rows, inv_scale, gain_vec):
    scaled = upstream * gain_vec
    plain_mean = jnp.mean(scaled, axis=-1, keepdims=True)
    cross_mean = jnp.mean(scaled * unit_rows, axis=-1, keepdims=True)
    d_source = inv_scale * (scaled - plain_mean - unit_rows * cross_mean)
    return (d_source, jnp.sum(upstream * unit_rows, axis=0), jnp.sum(upstream, axis=0))


def gelu_exact(source):
    return 0.5 * source * (1.0 + jax.scipy.special.erf(source * ROOT_HALF))


def gelu_slope(source):
    return (
        0.5 * (1.0 + jax.scipy.special.erf(source * ROOT_HALF))
        + source * jnp.exp(-0.5 * source * source) / ROOT_TWO_PI
    )


def product(left, right, dims):
    return lax.dot_general(left, right, (dims, ((), ())), preferred_element_type=jnp.float32)


def lane_is_low():
    return lax.broadcasted_iota(jnp.int32, (1, 128), 1) < 64


def split_query(query_pair, low_half):
    scaled = query_pair * (SCALE * LOG2E)
    high = scaled.astype(jnp.bfloat16).astype(jnp.float32)
    rest = pltpu.roll(scaled - high, 64, 1)
    return (
        jnp.where(low_half, high, rest).astype(jnp.bfloat16),
        jnp.where(low_half, rest, high).astype(jnp.bfloat16),
    )


def twice(pair, low_half):
    other = pltpu.roll(pair, 64, 1)
    return (
        jnp.where(low_half, pair, other).astype(jnp.bfloat16),
        jnp.where(low_half, other, pair).astype(jnp.bfloat16),
    )


MESH = pl.DeviceIdType.MESH
DMA = pltpu.SemaphoreType.DMA
ANY = pl.BlockSpec(memory_space=pl.ANY)
SUM_PLAN = {
    3: ((0, "after_core"),),
    4: ((1, "after_core"), (2, "after_core")),
    8: ((0, "after_pair"),),
    12: ((1, "after_pair"),),
    13: ((2, "after_pair"),),
    15: ((0, "after_line"),),
    18: ((0, "after_across"),),
    19: ((1, "after_line"),),
    20: ((2, "after_line"),),
    22: ((1, "after_across"),),
    23: ((2, "after_across"),),
}
STAGES = ("start", "after_core", "after_across", "after_group", "finish")


def places():
    ctx, group = lax.axis_index("ctx"), lax.axis_index("fsdp")
    return ctx, group, lax.rem(ctx + 2, 4), ctx + 1 - 2 * lax.rem(ctx, 2)


def remote(source, target, send_sem, recv_sem, where):
    return pltpu.make_async_remote_copy(
        src_ref=source,
        dst_ref=target,
        send_sem=send_sem,
        recv_sem=recv_sem,
        device_id=where,
        device_id_type=MESH,
    )


def greet(count):
    ctx, group, _, _ = places()
    barrier = pltpu.get_barrier_semaphore()

    def one(step, carry):
        pl.semaphore_signal(
            barrier,
            inc=1,
            device_id={"fsdp": lax.rem(group + step, count)},
            device_id_type=MESH,
        )
        return carry

    lax.fori_loop(1, count, one, 0)
    for other in range(1, 4):
        pl.semaphore_signal(
            barrier, inc=1, device_id={"ctx": lax.rem(ctx + other, 4)}, device_id_type=MESH
        )
    pl.semaphore_wait(barrier, count - 1 + 3)


class Gather:
    SCRATCH = 11

    def __init__(self, kinds, sems, count):
        self.kinds, self.count = kinds, count
        self.right_send, self.left_send, self.line_recv = sems[:3]
        self.y_send, self.y_recv, self.x_send, self.x_recv = sems[3:7]
        self.s_send, self.s_recv, self.r_send, self.r_recv = sems[7:11]
        self.ctx, self.group, self.across, self.sibling = places()
        self.line, self.side, self.length = self.group // 2, lax.rem(self.group, 2), count // 2

    @staticmethod
    def scratch(kinds, count):
        return [DMA((kinds, count))] * Gather.SCRATCH

    def copy(self, kind, block, quarter, send, recv, where, own=False):
        mine, place = self.kinds[kind]
        target = place(block, quarter)
        source = mine(quarter) if own else target
        return remote(source, target, send.at[kind, block], recv.at[kind, block], where)

    def right(self, kind, block, own=False):
        there = {"fsdp": lax.rem(self.group + 2, self.count)}
        return self.copy(kind, block, self.ctx, self.right_send, self.line_recv, there, own)

    def left(self, kind, block, own=False):
        there = {"fsdp": lax.rem(self.group - 2 + self.count, self.count)}
        return self.copy(kind, block, self.ctx, self.left_send, self.line_recv, there, own)

    def pair(self, kind, block, own=False):
        there = {"fsdp": self.group + 1 - 2 * self.side}
        return self.copy(kind, block, self.ctx, self.y_send, self.y_recv, there, own)

    def cross(self, kind, block):
        return self.copy(kind, block, self.ctx, self.x_send, self.x_recv, {"ctx": self.across})

    def share(self, kind, block):
        return self.copy(kind, block, self.ctx, self.s_send, self.s_recv, {"ctx": self.sibling})

    def relay(self, kind, block):
        return self.copy(kind, block, self.across, self.r_send, self.r_recv, {"ctx": self.sibling})

    def at(self, line, side):
        return 2 * line + side

    def every(self, body):
        for kind in range(len(self.kinds)):
            body(kind)

    def before(self, distance, body):
        @pl.when(self.line - distance >= 0)
        def _():
            body(self.line - distance)

    def after(self, distance, body):
        @pl.when(self.line + distance < self.length)
        def _():
            body(self.line + distance)

    def start(self):
        block = self.group

        def body(kind):
            self.after(1, lambda _: self.right(kind, block, True).start())
            self.before(1, lambda _: self.left(kind, block, True).start())
            self.pair(kind, block, True).start()

        self.every(body)

    def along(self, distance):
        def from_left(line):
            block = self.at(line, self.side)

            def body(kind):
                self.right(kind, block).wait_recv()
                self.after(1, lambda _: self.right(kind, block).start())
                self.pair(kind, block).start()
                self.cross(kind, block).start()
                self.share(kind, block).start()

            self.every(body)

        def from_right(line):
            block = self.at(line, self.side)

            def body(kind):
                self.left(kind, block).wait_recv()
                self.before(1, lambda _: self.left(kind, block).start())
                self.pair(kind, block).start()
                self.cross(kind, block).start()
                self.share(kind, block).start()

            self.every(body)

        self.before(distance, from_left)
        self.after(distance, from_right)

    def both(self, distance, side, body):
        if isinstance(distance, int) and distance == 0:
            body(self.at(self.line, side))
        else:
            self.before(distance, lambda line: body(self.at(line, side)))
            self.after(distance, lambda line: body(self.at(line, side)))

    def beside(self, distance):
        def one(block):
            def body(kind):
                self.pair(kind, block).wait_recv()
                self.cross(kind, block).start()
                self.share(kind, block).start()

            self.every(body)

        self.both(distance, 1 - self.side, one)

    def crossed(self, distance, side):
        def one(block):
            def body(kind):
                self.cross(kind, block).wait_recv()
                self.relay(kind, block).start()

            self.every(body)

        self.both(distance, self.side if side == 0 else 1 - self.side, one)

    def finish(self):
        def passed(block):
            def body(kind):
                self.cross(kind, block).wait_send()
                self.share(kind, block).wait()
                self.relay(kind, block).wait()

            self.every(body)

        def own(kind):
            self.after(1, lambda _: self.right(kind, self.group).wait_send())
            self.before(1, lambda _: self.left(kind, self.group).wait_send())
            self.pair(kind, self.group).wait_send()

        self.every(own)

        def one(distance, carry):
            def lefts(line):
                block = self.at(line, self.side)

                def body(kind):
                    self.after(1, lambda _: self.right(kind, block).wait_send())
                    self.pair(kind, block).wait_send()

                self.every(body)
                passed(block)

            def rights(line):
                block = self.at(line, self.side)

                def body(kind):
                    self.before(1, lambda _: self.left(kind, block).wait_send())
                    self.pair(kind, block).wait_send()

                self.every(body)
                passed(block)

            self.before(distance, lefts)
            self.after(distance, rights)
            self.both(distance, 1 - self.side, passed)
            return carry

        lax.fori_loop(1, self.length, one, 0)
        passed(self.at(self.line, 1 - self.side))


def arrival_kernel(
    placed,
    weights,
    small,
    tokens,
    gathered,
    small_all,
    tok_stage,
    w_stage,
    small_stage,
    local_sem,
    tok_send,
    tok_recv,
    small_send,
    small_recv,
    x_send,
    x_recv,
    s_send,
    s_recv,
    r_send,
    r_recv,
    *sems,
    count,
):
    ctx, group, across, sibling = places()
    gather = Gather(((lambda q: weights.at[q], lambda b, q: gathered.at[q, b]),), sems, count)
    own_tok = pltpu.make_async_copy(placed.at[group], tok_stage, local_sem.at[0])
    own_w = pltpu.make_async_copy(weights, w_stage, local_sem.at[1])
    own_small = pltpu.make_async_copy(small, small_stage, local_sem.at[2])
    own_tok.start()
    own_w.start()
    own_small.start()
    greet(count)

    def tok_copy(peer, step):
        return remote(
            placed.at[peer],
            tokens.at[ctx, group],
            tok_send.at[step],
            tok_recv.at[step],
            {"fsdp": peer},
        )

    def small_copy(peer, step):
        return remote(
            small, small_all.at[group], small_send.at[step], small_recv.at[step], {"fsdp": peer}
        )

    def pass_on(block, quarter, send, recv, target):
        place = tokens.at[quarter, block]
        return remote(place, place, send.at[block], recv.at[block], {"ctx": target})

    def across_copy(block):
        return pass_on(block, ctx, x_send, x_recv, across)

    def sibling_copy(block):
        return pass_on(block, ctx, s_send, s_recv, sibling)

    def relay_copy(block):
        return pass_on(block, across, r_send, r_recv, sibling)

    def send(step, carry):
        peer = lax.rem(group + step, count)
        tok_copy(peer, step).start()
        small_copy(peer, step).start()
        return carry

    gather.start()
    lax.fori_loop(1, count, send, 0)
    own_tok.wait()
    own_w.wait()
    own_small.wait()
    put_tok = pltpu.make_async_copy(tok_stage, tokens.at[ctx, group], local_sem.at[0])
    put_w = pltpu.make_async_copy(w_stage, gathered.at[:, group], local_sem.at[1])
    put_small = pltpu.make_async_copy(small_stage, small_all.at[group], local_sem.at[2])
    put_tok.start()
    put_w.start()
    put_small.start()
    put_tok.wait()
    across_copy(group).start()
    sibling_copy(group).start()
    put_w.wait()
    put_small.wait()

    def arrive(step, carry):
        origin = lax.rem(group - step + count, count)
        tok_copy(origin, step).wait_recv()
        across_copy(origin).start()
        sibling_copy(origin).start()
        return carry

    length = count // 2
    gather.along(1)
    gather.beside(0)
    lax.fori_loop(1, 3, arrive, 0)

    def advance(distance, carry):
        gather.along(distance)
        gather.beside(distance - 1)
        lax.fori_loop(2 * distance - 1, 2 * distance + 1, arrive, 0)
        return carry

    lax.fori_loop(2, length, advance, 0)
    gather.beside(length - 1)
    lax.fori_loop(2 * length - 1, count, arrive, 0)

    def crossed(distance, carry):
        gather.crossed(distance, 0)
        gather.crossed(distance, 1)
        return carry

    gather.crossed(0, 1)
    lax.fori_loop(1, length, crossed, 0)

    def passed(step, carry):
        origin = lax.rem(group - step + count, count)
        across_copy(origin).wait_recv()
        relay_copy(origin).start()
        return carry

    lax.fori_loop(0, count, passed, 0)
    gather.finish()

    def finish(step, carry):
        origin = lax.rem(group - step + count, count)
        across_copy(origin).wait_send()
        sibling_copy(origin).wait()
        relay_copy(origin).wait()
        return carry

    lax.fori_loop(0, count, finish, 0)

    def sent(step, carry):
        peer = lax.rem(group + step, count)
        tok_copy(peer, step).wait_send()
        small_copy(peer, step).wait()
        return carry

    lax.fori_loop(1, count, sent, 0)


def bring_in(placed, weights, small):
    count, rows, width = placed.shape
    return pl.pallas_call(
        functools.partial(arrival_kernel, count=count),
        in_specs=[ANY] * 3,
        out_specs=[ANY] * 3,
        out_shape=[
            jax.ShapeDtypeStruct((4, count, rows, width), jnp.bfloat16),
            jax.ShapeDtypeStruct((4, count) + weights.shape[1:], jnp.bfloat16),
            jax.ShapeDtypeStruct((count,) + small.shape, jnp.bfloat16),
        ],
        scratch_shapes=[
            pltpu.VMEM((rows, width), jnp.bfloat16),
            pltpu.VMEM((4,) + weights.shape[1:], jnp.bfloat16),
            pltpu.VMEM(small.shape, jnp.bfloat16),
            DMA((3,)),
        ]
        + [DMA((count,))] * 10
        + Gather.scratch(1, count),
        compiler_params=pltpu.CompilerParams(
            collective_id=0, has_side_effects=True, vmem_limit_bytes=8 * 2**20
        ),
        name="bring_in",
    )(placed, weights, small)


class Sum:
    SCRATCH = 16

    def __init__(self, ref, out, scratch, count):
        self.ref, self.out, self.count = ref, out, count
        self.near, self.far, self.got_near, self.got_far = scratch[:4]
        self.got_across, self.got_group, self.done = scratch[4:7]
        self.load, self.c_send, self.c_recv, self.x_send, self.x_recv = scratch[7:12]
        self.g_send, self.g_recv, self.o_send, self.o_recv = scratch[12:16]
        self.ctx, self.group, self.across, self.sibling = places()
        self.width = self.near.shape[-1]

    @staticmethod
    def scratch(count, rows, width):
        return (
            [pltpu.VMEM((count, rows, width), jnp.bfloat16)] * 6
            + [pltpu.VMEM((rows, width), jnp.bfloat16)]
            + [DMA((2,))] * 3
            + [DMA((count,))] * 4
            + [DMA((4,))] * 2
        )

    def quarter(self, index):
        start = pl.multiple_of(lax.rem(index, 2) * self.width, self.width)
        return self.ref.at[:, index // 2, :, pl.ds(start, self.width)]

    def loads(self):
        return (
            pltpu.make_async_copy(self.quarter(self.across), self.far, self.load.at[0]),
            pltpu.make_async_copy(self.quarter(self.ctx), self.near, self.load.at[1]),
        )

    def cores(self):
        beyond = lax.rem(self.sibling + 2, 4)
        there = {"ctx": self.sibling}
        return (
            remote(self.quarter(beyond), self.got_far, self.c_send.at[0], self.c_recv.at[0], there),
            remote(
                self.quarter(self.sibling),
                self.got_near,
                self.c_send.at[1],
                self.c_recv.at[1],
                there,
            ),
        )

    def x_copy(self, block):
        return remote(
            self.far.at[block],
            self.got_across.at[block],
            self.x_send.at[block],
            self.x_recv.at[block],
            {"ctx": self.across},
        )

    def g_copy(self, peer, step):
        return remote(
            self.near.at[peer],
            self.got_group.at[step],
            self.g_send.at[step],
            self.g_recv.at[step],
            {"fsdp": peer},
        )

    def o_copy(self, other):
        return remote(
            self.done,
            self.out.at[self.ctx],
            self.o_send.at[other],
            self.o_recv.at[other],
            {"ctx": lax.rem(self.ctx + other, 4)},
        )

    def own_out(self):
        return pltpu.make_async_copy(self.done, self.out.at[self.ctx], self.load.at[0])

    def add(self, total, other):
        def one(block, carry):
            both = total[block].astype(jnp.float32) + other[block].astype(jnp.float32)
            total[block] = both.astype(jnp.bfloat16)
            return carry

        lax.fori_loop(0, self.count, one, 0)

    def start(self):
        for copy in self.loads() + self.cores():
            copy.start()

    def after_core(self):
        loads, cores = self.loads(), self.cores()
        loads[0].wait()
        cores[0].wait_recv()
        self.add(self.far, self.got_far)

        def send(step, carry):
            self.x_copy(lax.rem(self.group + 1 + step, self.count)).start()
            return carry

        lax.fori_loop(0, self.count, send, 0)
        loads[1].wait()
        cores[1].wait_recv()
        self.add(self.near, self.got_near)
        cores[0].wait_send()
        cores[1].wait_send()

    def after_across(self):
        def one(step, carry):
            block = lax.rem(self.group + step, self.count)
            self.x_copy(block).wait()
            both = self.near[block].astype(jnp.float32) + self.got_across[block].astype(jnp.float32)
            self.near[block] = both.astype(jnp.bfloat16)
            self.g_copy(block, step).start()
            return carry

        lax.fori_loop(1, self.count, one, 0)
        self.x_copy(self.group).wait()

    def after_group(self):
        group = self.group
        total = self.near[group].astype(jnp.float32) + self.got_across[group].astype(jnp.float32)

        def one(step, total):
            self.g_copy(lax.rem(group + step, self.count), step).wait()
            return total + self.got_group[step].astype(jnp.float32)

        self.done[...] = lax.fori_loop(1, self.count, one, total).astype(jnp.bfloat16)
        self.own_out().start()
        for other in range(1, 4):
            self.o_copy(other).start()

    def finish(self):
        self.own_out().wait()
        for other in range(1, 4):
            self.o_copy(other).wait()


class VectorSum:
    SCRATCH = 9

    def __init__(self, ref, out, scratch, count):
        self.ref, self.out, self.count = ref, out, count
        self.total, self.got_ctx, self.got_group = scratch[:3]
        self.load, self.c_send, self.c_recv, self.g_send, self.g_recv = scratch[3:8]
        self.result = scratch[8]
        self.ctx, self.group, _, _ = places()

    @staticmethod
    def scratch(count, rows, width):
        return [
            pltpu.VMEM((rows, width), jnp.float32),
            pltpu.VMEM((4, rows, width), jnp.float32),
            pltpu.VMEM((count, rows, width), jnp.float32),
            DMA((2,)),
            DMA((4,)),
            DMA((4,)),
            DMA((count,)),
            DMA((count,)),
            pltpu.VMEM((rows, width), jnp.float32),
        ]

    def own(self):
        return pltpu.make_async_copy(self.ref, self.total, self.load.at[0])

    def own_out(self):
        return pltpu.make_async_copy(self.result, self.out, self.load.at[1])

    def c_copy(self, other):
        return remote(
            self.ref,
            self.got_ctx.at[other],
            self.c_send.at[other],
            self.c_recv.at[other],
            {"ctx": lax.rem(self.ctx + other, 4)},
        )

    def g_copy(self, step):
        return remote(
            self.total,
            self.got_group.at[step],
            self.g_send.at[step],
            self.g_recv.at[step],
            {"fsdp": lax.rem(self.group + step, self.count)},
        )

    def start(self):
        self.own().start()
        for other in range(1, 4):
            self.c_copy(other).start()

    def after_core(self):
        self.own().wait()
        total = self.total[...]
        for other in range(1, 4):
            self.c_copy(other).wait()
            total = total + self.got_ctx[other]
        self.total[...] = total

        def one(step, carry):
            self.g_copy(step).start()
            return carry

        lax.fori_loop(1, self.count, one, 0)

    def after_across(self):
        pass

    def after_group(self):
        def one(step, total):
            self.g_copy(step).wait()
            return total + self.got_group[step]

        self.result[...] = lax.fori_loop(1, self.count, one, self.total[...])
        self.own_out().start()

    def finish(self):
        self.own_out().wait()


class LateSum:
    SCRATCH = 19

    def __init__(self, view, out, scratch, count):
        self.view, self.out, self.count = view, out, count
        self.near, self.got, self.got_pair, self.got_line = scratch[:4]
        self.half, self.got_across, self.done = scratch[4:7]
        self.load, self.c_send, self.c_recv, self.p_send, self.p_recv = scratch[7:12]
        self.l_send, self.l_recv, self.x_send, self.x_recv = scratch[12:16]
        self.o_send, self.o_recv, self.put = scratch[16:19]
        self.ctx, self.group, self.across, self.sibling = places()
        self.core = lax.rem(self.ctx, 2)
        self.line, self.side, self.length = self.group // 2, lax.rem(self.group, 2), count // 2
        self.halves = self.half.shape[0]

    @staticmethod
    def scratch(count, halves, rows, width):
        def block(*lead):
            return pltpu.VMEM(lead + (halves, rows, width), jnp.bfloat16)

        return (
            [block(count), block(count), block(count // 2), block(count // 2)]
            + [block(), block(), block()]
            + [DMA((halves,))] * 3
            + [DMA((count // 2,))] * 4
            + [DMA((1,))] * 2
            + [DMA((halves,))] * 3
        )

    def load_copy(self, half):
        return pltpu.make_async_copy(
            self.view(2 * half + self.core), self.near.at[:, half], self.load.at[half]
        )

    def core_copy(self, half):
        return remote(
            self.view(2 * half + 1 - self.core),
            self.got.at[:, half],
            self.c_send.at[half],
            self.c_recv.at[half],
            {"ctx": self.sibling},
        )

    def pair_copy(self, line):
        return remote(
            self.near.at[2 * line + 1 - self.side],
            self.got_pair.at[line],
            self.p_send.at[line],
            self.p_recv.at[line],
            {"fsdp": self.group + 1 - 2 * self.side},
        )

    def line_copy(self, step):
        peer = 2 * lax.rem(self.line + step, self.length) + self.side
        return remote(
            self.near.at[peer],
            self.got_line.at[step],
            self.l_send.at[step],
            self.l_recv.at[step],
            {"fsdp": peer},
        )

    def x_copy(self):
        return remote(
            self.half, self.got_across, self.x_send.at[0], self.x_recv.at[0], {"ctx": self.across}
        )

    def out_copy(self, half):
        return remote(
            self.done.at[half],
            self.out.at[2 * half + self.core],
            self.o_send.at[half],
            self.o_recv.at[half],
            {"ctx": self.sibling},
        )

    def own_out(self, half):
        return pltpu.make_async_copy(
            self.done.at[half], self.out.at[2 * half + self.core], self.put.at[half]
        )

    def add(self, block, other):
        both = self.near[block].astype(jnp.float32) + other.astype(jnp.float32)
        self.near[block] = both.astype(jnp.bfloat16)

    def start(self):
        for half in range(self.halves):
            self.load_copy(half).start()
            self.core_copy(half).start()

    def after_core(self):
        for half in range(self.halves):
            self.load_copy(half).wait()
            self.core_copy(half).wait()

        def theirs(step, carry):
            line = lax.rem(self.line + step, self.length)
            block = 2 * line + 1 - self.side
            self.add(block, self.got[block])
            self.pair_copy(line).start()
            return carry

        lax.fori_loop(0, self.length, theirs, 0)

        def mine(line, carry):
            block = 2 * line + self.side
            self.add(block, self.got[block])
            return carry

        lax.fori_loop(0, self.length, mine, 0)

    def after_pair(self):
        def one(step, carry):
            line = lax.rem(self.line + step, self.length)
            self.pair_copy(line).wait()
            self.add(2 * line + self.side, self.got_pair[line])
            self.line_copy(step).start()
            return carry

        lax.fori_loop(1, self.length, one, 0)
        self.pair_copy(self.line).wait()
        self.add(self.group, self.got_pair[self.line])

    def after_line(self):
        def one(step, total):
            self.line_copy(step).wait()
            return total + self.got_line[step].astype(jnp.float32)

        total = lax.fori_loop(1, self.length, one, self.near[self.group].astype(jnp.float32))
        self.half[...] = total.astype(jnp.bfloat16)
        self.x_copy().start()

    def after_across(self):
        self.x_copy().wait()
        both = self.half[...].astype(jnp.float32) + self.got_across[...].astype(jnp.float32)
        self.done[...] = both.astype(jnp.bfloat16)
        for half in range(self.halves):
            self.own_out(half).start()
            self.out_copy(half).start()

    def finish(self):
        for half in range(self.halves):
            self.own_out(half).wait()
            self.out_copy(half).wait()


def sums_kernel(*refs, parts, count):
    ins, outs, rest = refs[: parts + 1], refs[parts + 1 : 2 * parts + 2], refs[2 * parts + 2 :]
    jobs = [VectorSum(ins[parts], outs[parts], rest[: VectorSum.SCRATCH], count)]
    rest = rest[VectorSum.SCRATCH :]
    for index in range(parts):
        own = rest[index * Sum.SCRATCH : (index + 1) * Sum.SCRATCH]
        jobs.append(Sum(ins[index], outs[index], own, count))
    greet(count)
    for stage in STAGES:
        for job in jobs:
            getattr(job, stage)()


def sum_gradients(parts, vectors):
    count, _, rows, width = parts[0].shape
    width = width // 2
    scratch = VectorSum.scratch(count, *vectors.shape)
    for _ in parts:
        scratch += Sum.scratch(count, rows, width)
    return pl.pallas_call(
        functools.partial(sums_kernel, parts=len(parts), count=count),
        in_specs=[ANY] * (len(parts) + 1),
        out_specs=[ANY] * (len(parts) + 1),
        out_shape=[jax.ShapeDtypeStruct((4, rows, width), jnp.bfloat16)] * len(parts)
        + [jax.ShapeDtypeStruct(vectors.shape, jnp.float32)],
        scratch_shapes=scratch,
        compiler_params=pltpu.CompilerParams(
            collective_id=1, has_side_effects=True, vmem_limit_bytes=VMEM_BYTES
        ),
        name="sum_gradients",
    )(*parts, vectors)


def gather_plan(length):
    stretch = max(length - 2, 1)
    slots = [[] for _ in range(LAST_SLOT + 1)]

    def put(name, at, over, first):
        for distance in range(1, length):
            slot = min(at + (distance - 1) * over // stretch, LAST_SLOT)
            events = slots[slot]
            if events and events[-1][0] == name:
                events[-1] = (name, events[-1][1], distance + 1)
            else:
                events.append((name, distance, distance + 1))
        if first:
            slots[first].append((name, 0, 1))

    put("along", 2, 4, 0)
    put("beside", 5, 3, 2)
    put("line", 6, 4, 0)
    put("pair", 8, 4, 6)
    return slots


def forward_kernel(
    limit_ref,
    query_ref,
    key_ref,
    value_ref,
    inner_ref,
    outer_ref,
    attended_ref,
    lse_ref,
    inner_all,
    outer_all,
    *scratch,
    key_rows,
    count,
):
    pair = pl.program_id(0)
    pairs = pl.num_programs(0) - 1
    inner_stage, outer_stage, local, *sems = scratch
    width = outer_ref.shape[-1]

    def columns(quarter):
        return pl.ds(pl.multiple_of(quarter * width, width), width)

    kinds = (
        (lambda q: inner_ref.at[:, columns(q)], lambda b, q: inner_all.at[b, :, columns(q)]),
        (lambda q: outer_ref.at[q], lambda b, q: outer_all.at[b, q]),
    )
    gather = Gather(kinds, sems, count)
    loads = (
        pltpu.make_async_copy(inner_ref, inner_stage, local.at[0]),
        pltpu.make_async_copy(outer_ref, outer_stage, local.at[1]),
    )
    puts = (
        pltpu.make_async_copy(inner_stage, inner_all.at[gather.group], local.at[2]),
        pltpu.make_async_copy(outer_stage, outer_all.at[gather.group], local.at[3]),
    )
    plan = gather_plan(count // 2)

    def communicate(events):
        for name, first, last in events:
            act = {
                "along": gather.along,
                "beside": gather.beside,
                "line": lambda distance: gather.crossed(distance, 0),
                "pair": lambda distance: gather.crossed(distance, 1),
            }[name]
            if last - first == 1:
                act(first)
            else:

                def one(distance, carry, act=act):
                    act(distance)
                    return carry

                lax.fori_loop(first, last, one, 0)

    @pl.when(pair == 0)
    def _():
        greet(count)
        for load in loads:
            load.start()
        gather.start()
        for load, put in zip(loads, puts):
            load.wait()
            put.start()

    @pl.when(pair == pairs)
    def _():
        communicate(plan[LAST_SLOT])
        gather.finish()
        for put in puts:
            put.wait()

    @pl.when(pair < pairs)
    def _():
        low_half = lane_is_low()
        limit = limit_ref[0]
        queries = split_query(query_ref[...].astype(jnp.float32), low_half)
        query_rows = query_ref.shape[0]

        def step(tile, state):
            for slot in range(1, LAST_SLOT):
                if plan[slot]:

                    @pl.when(2 * pair + tile == slot)
                    def _(slot=slot):
                        communicate(plan[slot])

            start = pl.multiple_of(tile * key_rows, key_rows)
            usable = start + lax.broadcasted_iota(jnp.int32, (key_rows, 1), 0) < limit
            key_tile = key_ref[pl.ds(start, key_rows), :].astype(jnp.float32)
            keys = twice(jnp.where(usable, key_tile, key_ref[0:1, :].astype(jnp.float32)), low_half)
            value_tile = value_ref[pl.ds(start, key_rows), :].astype(jnp.float32)
            value_tile = jnp.where(usable, value_tile, 0.0)
            count = jnp.where(usable, 1.0, 0.0)
            values = (
                jnp.where(low_half, value_tile, count).astype(jnp.bfloat16),
                jnp.where(low_half, count, value_tile).astype(jnp.bfloat16),
            )
            fresh = []
            for head in range(2):
                top, total = state[head]
                scores = product(queries[head], keys[head], ((1,), (1,)))
                new_top = jnp.maximum(top, jnp.max(scores, axis=1, keepdims=True))
                weights = jnp.exp2(scores - new_top).astype(jnp.bfloat16)
                total = total * jnp.exp2(top - new_top) + product(weights, values[head], ((1,), (0,)))
                fresh.append((new_top, total))
            return tuple(fresh)

        empty = (
            jnp.full((query_rows, 1), NEG_BIG, jnp.float32),
            jnp.zeros((query_rows, 128), jnp.float32),
        )
        (top_a, total_a), (top_b, total_b) = lax.fori_loop(
            0, key_ref.shape[0] // key_rows, step, (empty, empty)
        )
        mass_a, mass_b = total_a[:, 64:65], total_b[:, 0:1]
        attended_ref[...] = jnp.where(low_half, total_a / mass_a, total_b / mass_b)
        lse = jnp.where(low_half, top_a + jnp.log2(mass_a), top_b + jnp.log2(mass_b)).T
        lse_ref[0, 0:1, :] = lse[0:1, :]
        lse_ref[0, 1:2, :] = lse[64:65, :]


def attend_forward(queries, keys, values, limit, inner, outer, count):
    rows, width = queries.shape
    full = keys.shape[0]
    pairs = width // 128
    shard = inner.shape[0]
    now = lambda pair, *_: (0, jnp.minimum(pair, pairs - 1))
    row_spec = pl.BlockSpec((rows, 128), now)
    key_spec = pl.BlockSpec((full, 128), now)
    return pl.pallas_call(
        functools.partial(forward_kernel, key_rows=full // 2, count=count),
        grid_spec=pltpu.PrefetchScalarGridSpec(
            num_scalar_prefetch=1,
            grid=(pairs + 1,),
            in_specs=[row_spec, key_spec, key_spec, ANY, ANY],
            out_specs=[
                row_spec,
                pl.BlockSpec((1, 2, rows), lambda pair, *_: (jnp.minimum(pair, pairs - 1), 0, 0)),
                ANY,
                ANY,
            ],
            scratch_shapes=[
                pltpu.VMEM((shard, 4 * width), jnp.bfloat16),
                pltpu.VMEM((4, shard, width), jnp.bfloat16),
                DMA((4,)),
            ]
            + Gather.scratch(2, count),
        ),
        out_shape=[
            jax.ShapeDtypeStruct((rows, width), jnp.float32),
            jax.ShapeDtypeStruct((pairs, 2, rows), jnp.float32),
            jax.ShapeDtypeStruct((count, shard, 4 * width), jnp.bfloat16),
            jax.ShapeDtypeStruct((count, 4, shard, width), jnp.bfloat16),
        ],
        compiler_params=pltpu.CompilerParams(
            collective_id=3, has_side_effects=True, vmem_limit_bytes=VMEM_BYTES
        ),
        cost_estimate=pl.CostEstimate(
            flops=16 * rows * full * width, bytes_accessed=20_000_000, transcendentals=0
        ),
        name="attend_forward",
    )(limit, queries, keys, values, inner, outer)


def backward_kernel(
    limit_ref,
    query_ref,
    key_ref,
    value_ref,
    grad_ref,
    attended_ref,
    lse_ref,
    inner_ref,
    outer_ref,
    output_ref,
    d_query_ref,
    d_key_ref,
    d_value_ref,
    inner_out,
    outer_out,
    output_out,
    query_sum,
    part,
    got_core,
    far,
    near,
    got_x,
    core_send,
    core_recv,
    x_send,
    x_recv,
    *rest,
    count,
):
    pair = pl.program_id(0)
    pairs = pl.num_programs(0) - 1
    slot = lax.rem(pair, 2)
    ctx, _, across, sibling = places()
    key_rows = query_ref.shape[0]
    def columns(ref, parts):
        size = ref.shape[2] // parts
        return lambda index: ref.at[:, :, pl.ds(pl.multiple_of(index * size, size), size)]

    views = (columns(inner_ref, 4), lambda index: outer_ref.at[:, index], columns(output_ref, 2))
    jobs = [
        LateSum(
            view, out, rest[index * LateSum.SCRATCH : (index + 1) * LateSum.SCRATCH], count
        )
        for index, (view, out) in enumerate(zip(views, (inner_out, outer_out, output_out)))
    ]

    def core_copy(which):
        return remote(
            part.at[which],
            got_core.at[slot, which],
            core_send.at[which],
            core_recv.at[slot, which],
            {"ctx": sibling},
        )

    def x_copy(where):
        return remote(
            far.at[where], got_x.at[where], x_send.at[where], x_recv.at[where], {"ctx": across}
        )

    def settle():
        where = 1 - slot
        x_copy(where).wait()
        for kind, ref in enumerate((d_key_ref, d_value_ref)):
            both = near[where, kind].astype(jnp.float32) + got_x[where, kind].astype(jnp.float32)
            ref[...] = both.astype(jnp.bfloat16)

    @pl.when(pair == 0)
    def _():
        greet(count)
        for job in jobs:
            job.start()

    @pl.when(pair < pairs)
    def _():
        low_half = lane_is_low()
        high_half = jnp.logical_not(low_half)
        lane = lax.broadcasted_iota(jnp.int32, (1, 128), 1)
        limit = limit_ref[0]
        query_pair = query_ref[...].astype(jnp.float32)
        queries = split_query(query_pair, low_half)
        scaled = query_pair * SCALE
        grad_pair = grad_ref[...].astype(jnp.float32)
        overlap = grad_pair * attended_ref[...]
        own_query, own_grad, joined_grad = [], [], []
        for head in range(2):
            mine = low_half if head == 0 else high_half
            own_query.append(jnp.where(mine, scaled, 0.0).astype(jnp.bfloat16))
            own_grad.append(jnp.where(mine, grad_pair, 0.0).astype(jnp.bfloat16))
            delta = -jnp.sum(jnp.where(mine, overlap, 0.0), axis=1, keepdims=True)
            first = delta.astype(jnp.bfloat16).astype(jnp.float32)
            second = (delta - first).astype(jnp.bfloat16).astype(jnp.float32)
            third = delta - first - second
            spare = 64 * (1 - head)
            joined = jnp.where(lane == spare + 2, third, 0.0)
            joined = jnp.where(lane == spare + 1, second, joined)
            joined = jnp.where(lane == spare, first, joined)
            joined_grad.append(jnp.where(mine, grad_pair, joined).astype(jnp.bfloat16))
        query_sum[...] = jnp.zeros_like(query_sum)

        def step(tile, carry):
            for at, stages in SUM_PLAN.items():

                @pl.when(4 * pair + tile == at)
                def _(stages=stages):
                    for index, stage in stages:
                        getattr(jobs[index], stage)()

            odd = lax.rem(tile, 2)
            quarter = lax.rem(sibling + odd * (ctx - sibling) + 2 * (1 - tile // 2), 4)
            start = pl.multiple_of(quarter * key_rows, key_rows)
            usable = start + lax.broadcasted_iota(jnp.int32, (key_rows, 1), 0) < limit
            key_tile = key_ref[pl.ds(start, key_rows), :].astype(jnp.float32)
            value_tile = value_ref[pl.ds(start, key_rows), :].astype(jnp.float32)
            keys = twice(jnp.where(usable, key_tile, key_ref[0:1, :].astype(jnp.float32)), low_half)
            own_tile = jnp.where(usable, key_tile * SCALE, 0.0)
            key_piece = value_piece = None
            for head in range(2):
                mine = low_half if head == 0 else high_half
                values = jnp.where(mine, value_tile, 1.0).astype(jnp.bfloat16)
                own_key = jnp.where(mine, own_tile, 0.0).astype(jnp.bfloat16)
                scores = product(keys[head], queries[head], ((1,), (1,)))
                probs = jnp.exp2(scores - lse_ref[0, head : head + 1, :])
                slopes = product(values, joined_grad[head], ((1,), (1,)))
                score_grads = (probs * slopes).astype(jnp.bfloat16)
                value_term = product(probs.astype(jnp.bfloat16), own_grad[head], ((1,), (0,)))
                key_term = product(score_grads, own_query[head], ((1,), (0,)))
                value_piece = value_term if value_piece is None else value_piece + value_term
                key_piece = key_term if key_piece is None else key_piece + key_term
                query_sum[...] += product(own_key, score_grads, ((0,), (0,)))
            pieces = (jnp.where(usable, key_piece, 0.0), jnp.where(usable, value_piece, 0.0))

            @pl.when(odd == 0)
            def _():
                which = tile // 2
                for kind in range(2):
                    part[which, kind] = pieces[kind].astype(jnp.bfloat16)
                core_copy(which).start()

            @pl.when(tile == 1)
            def _():
                @pl.when(pair > 0)
                def _():
                    settle()

                core_copy(0).wait_recv()
                for kind in range(2):
                    both = pieces[kind] + got_core[slot, 0, kind].astype(jnp.float32)
                    far[slot, kind] = both.astype(jnp.bfloat16)
                x_copy(slot).start()

            @pl.when(tile == 3)
            def _():
                core_copy(1).wait_recv()
                for kind in range(2):
                    both = pieces[kind] + got_core[slot, 1, kind].astype(jnp.float32)
                    near[slot, kind] = both.astype(jnp.bfloat16)
                core_copy(0).wait_send()
                core_copy(1).wait_send()

            return carry

        lax.fori_loop(0, 4, step, 0)
        d_query_ref[...] = query_sum[...].T.astype(jnp.bfloat16)

    @pl.when(pair == pairs)
    def _():
        settle()
        for job in jobs:
            job.finish()


def attend_backward(queries, keys, values, limit, grad_rows, attended, lse, parts):
    rows, width = queries.shape
    full = keys.shape[0]
    pairs = width // 128
    count, shard = parts[0].shape[:2]
    now = lambda pair, *_: (0, jnp.minimum(pair, pairs - 1))
    before = lambda pair, *_: (0, jnp.maximum(pair - 1, 0))
    row_spec = pl.BlockSpec((rows, 128), now)
    key_spec = pl.BlockSpec((full, 128), now)
    sum_spec = pl.BlockSpec((rows, 128), before)
    tile = (2, rows, 128)
    return pl.pallas_call(
        functools.partial(backward_kernel, count=count),
        grid_spec=pltpu.PrefetchScalarGridSpec(
            num_scalar_prefetch=1,
            grid=(pairs + 1,),
            in_specs=[
                row_spec,
                key_spec,
                key_spec,
                row_spec,
                row_spec,
                pl.BlockSpec((1, 2, rows), lambda pair, *_: (jnp.minimum(pair, pairs - 1), 0, 0)),
                ANY,
                ANY,
                ANY,
            ],
            out_specs=[row_spec, sum_spec, sum_spec, ANY, ANY, ANY],
            scratch_shapes=[
                pltpu.VMEM((128, rows), jnp.float32),
                pltpu.VMEM((2,) + tile, jnp.bfloat16),
                pltpu.VMEM((2, 2) + tile, jnp.bfloat16),
                pltpu.VMEM((2,) + tile, jnp.bfloat16),
                pltpu.VMEM((2,) + tile, jnp.bfloat16),
                pltpu.VMEM((2,) + tile, jnp.bfloat16),
                DMA((2,)),
                DMA((2, 2)),
                DMA((2,)),
                DMA((2,)),
            ]
            + LateSum.scratch(count, 2, shard, width) * 2
            + LateSum.scratch(count, 1, shard, width // 2),
        ),
        out_shape=[jax.ShapeDtypeStruct((rows, width), jnp.bfloat16)] * 3
        + [jax.ShapeDtypeStruct((4, shard, width), jnp.bfloat16)] * 2
        + [jax.ShapeDtypeStruct((2, shard, width // 2), jnp.bfloat16)],
        compiler_params=pltpu.CompilerParams(
            collective_id=2, has_side_effects=True, vmem_limit_bytes=VMEM_BYTES
        ),
        cost_estimate=pl.CostEstimate(
            flops=40 * rows * full * width, bytes_accessed=40_000_000, transcendentals=0
        ),
        name="attend_backward",
    )(limit, queries, keys, values, grad_rows, attended, lse, *parts)


def on_device(
    hidden_in,
    lengths,
    seq_order,
    query_weight,
    query_bias,
    key_weight,
    value_weight,
    value_bias,
    output_weight,
    output_bias,
    norm1_gain,
    norm1_shift,
    inner_weight,
    inner_bias,
    outer_weight,
    outer_bias,
    norm2_gain,
    norm2_shift,
    cotangent,
):
    width = hidden_in.shape[2]
    count = lax.axis_size("fsdp")
    group = lax.axis_index("fsdp")
    shard = query_bias.shape[0]
    low = jnp.bfloat16
    placed = jnp.swapaxes(hidden_in.at[:, seq_order].get(mode="promise_in_bounds"), 0, 1)
    vectors = jnp.concatenate(
        (
            jnp.stack(
                (
                    query_bias,
                    value_bias,
                    output_bias,
                    norm1_gain,
                    norm1_shift,
                    outer_bias,
                    norm2_gain,
                    norm2_shift,
                )
            ),
            inner_bias.reshape(4, shard),
        )
    )
    vectors = jnp.pad(vectors, ((0, 4), (0, 128 - shard)))
    weights = jnp.stack((query_weight, key_weight, value_weight, output_weight))
    tokens, weights, vectors = bring_in(placed, weights, vectors)
    w_query, w_key, w_value, w_output = (weights[i].reshape(width, width) for i in range(4))
    vectors = vectors[:, :12, :shard].astype(jnp.float32)
    b_query, b_value, b_output, gain_one, shift_one, b_outer, gain_two, shift_two = (
        vectors[:, i].reshape(width) for i in range(8)
    )
    b_inner = vectors[:, 8:].reshape(-1)
    limits = jnp.take(lengths, jnp.take(seq_order, group[None]))
    all_rows = tokens.reshape(-1, width)
    local_len = all_rows.shape[0] // 4
    token_rows = lax.dynamic_index_in_dim(tokens, lax.axis_index("ctx"), 0, False)
    token_rows = token_rows.reshape(local_len, width)
    queries = (product(token_rows, w_query, ((1,), (0,))) + b_query).astype(low)
    keys = product(all_rows, w_key, ((1,), (0,))).astype(low)
    values = (product(all_rows, w_value, ((1,), (0,))) + b_value).astype(low)
    attended, lse, w_inner, w_outer = attend_forward(
        queries,
        keys,
        values,
        limits,
        inner_weight,
        outer_weight.reshape(4, shard, width),
        count,
    )
    w_inner = w_inner.reshape(width, 4 * width)
    w_outer = w_outer.reshape(4 * width, width)
    mixed_low = attended.astype(low)
    branch = product(mixed_low, w_output, ((1,), (0,))) + b_output
    normed, unit_one, scale_one = norm_forward(
        token_rows.astype(jnp.float32) + branch, gain_one, shift_one
    )
    normed_low = normed.astype(low)
    inner_pre = product(normed_low, w_inner, ((1,), (0,))) + b_inner
    activated = gelu_exact(inner_pre).astype(low)
    outer_out = product(activated, w_outer, ((1,), (0,))) + b_outer
    second, unit_two, scale_two = norm_forward(normed + outer_out, gain_two, shift_two)
    layer_out = second.astype(low).reshape(local_len, 1, width)
    upstream = cotangent.reshape(local_len, width).astype(jnp.float32)
    d_second, grad_gain_two, grad_shift_two = norm_backward(upstream, unit_two, scale_two, gain_two)
    d_outer = d_second.astype(low)
    grad_outer_w = product(activated, d_outer, ((0,), (0,))).astype(low)
    grad_outer_b = jnp.sum(d_outer.astype(jnp.float32), axis=0)
    inner_grad = product(d_outer, w_outer, ((1,), (1,)))
    d_inner = (inner_grad * gelu_slope(inner_pre)).astype(low)
    grad_inner_w = product(normed_low, d_inner, ((0,), (0,))).astype(low)
    grad_inner_b = jnp.sum(d_inner.astype(jnp.float32), axis=0)
    d_normed = d_second + product(d_inner, w_inner, ((1,), (1,)))
    d_res, grad_gain_one, grad_shift_one = norm_backward(d_normed, unit_one, scale_one, gain_one)
    d_branch = d_res.astype(low)
    grad_output_w = product(mixed_low, d_branch, ((0,), (0,))).astype(low)
    grad_output_b = jnp.sum(d_branch.astype(jnp.float32), axis=0)
    d_mixed = product(d_branch, w_output, ((1,), (1,))).astype(low)
    d_query, d_keys, d_values, inner_w, outer_w, output_w = attend_backward(
        queries,
        keys,
        values,
        limits,
        d_mixed,
        attended,
        lse,
        (
            grad_inner_w.reshape(count, shard, 4 * width),
            grad_outer_w.reshape(count, 4, shard, width),
            grad_output_w.reshape(count, shard, width),
        ),
    )
    grad_query_w = product(token_rows, d_query, ((0,), (0,))).astype(low)
    grad_query_b = jnp.sum(d_query.astype(jnp.float32), axis=0)
    grad_key_w = product(token_rows, d_keys, ((0,), (0,))).astype(low)
    grad_value_w = product(token_rows, d_values, ((0,), (0,))).astype(low)
    grad_value_b = jnp.sum(d_values.astype(jnp.float32), axis=0)
    d_placed = d_res + product(d_query, w_query, ((1,), (1,)))
    d_placed = d_placed + product(d_keys, w_key, ((1,), (1,)))
    d_placed = d_placed + product(d_values, w_value, ((1,), (1,)))
    back_rows = d_placed.astype(low).reshape(count, local_len // count, width)
    returned = lax.all_to_all(back_rows, "fsdp", split_axis=0, concat_axis=0, tiled=True)
    inverse = jnp.argmax(seq_order[:, None] == jnp.arange(count), axis=0)
    grad_in = jnp.swapaxes(returned, 0, 1).at[:, inverse].get(mode="promise_in_bounds")
    small_sums = jnp.concatenate(
        (
            jnp.stack(
                (
                    grad_query_b,
                    grad_value_b,
                    grad_output_b,
                    grad_gain_one,
                    grad_shift_one,
                    grad_outer_b,
                    grad_gain_two,
                    grad_shift_two,
                )
            ),
            grad_inner_b.reshape(4, width),
            jnp.zeros((4, width), jnp.float32),
        )
    )
    *attention_w, small_sums = sum_gradients(
        [
            part.reshape(count, 2, shard // 2, width)
            for part in (grad_query_w, grad_key_w, grad_value_w)
        ],
        small_sums,
    )
    attention_w = [
        jnp.swapaxes(part.reshape(2, 2, shard // 2, width // 2), 1, 2)
        .reshape(shard, width)
        .astype(jnp.float32)
        for part in attention_w
    ]
    output_w = jnp.swapaxes(output_w, 0, 1).reshape(shard, width).astype(jnp.float32)
    inner_w = jnp.swapaxes(inner_w, 0, 1).reshape(shard, 4 * width).astype(jnp.float32)
    outer_w = outer_w.reshape(4 * shard, width).astype(jnp.float32)
    small = lax.dynamic_slice_in_dim(small_sums[:8], group * shard, shard, axis=1)
    inner_b = lax.dynamic_slice_in_dim(
        small_sums[8:12].reshape(-1), group * 4 * shard, 4 * shard, axis=0
    )
    return (
        layer_out,
        grad_in,
        attention_w[0],
        small[0],
        attention_w[1],
        attention_w[2],
        small[1],
        output_w,
        small[2],
        small[3],
        small[4],
        inner_w,
        inner_b,
        outer_w,
        small[5],
        small[6],
        small[7],
    )


def solution(mesh):
    placed = (
        P(("ctx", "fsdp"), None, None),
        P(),
        P(),
        P("fsdp", None),
        P("fsdp"),
        P("fsdp", None),
        P("fsdp", None),
        P("fsdp"),
        P("fsdp", None),
        P("fsdp"),
        P("fsdp"),
        P("fsdp"),
        P("fsdp", None),
        P("fsdp"),
        P("fsdp", None),
        P("fsdp"),
        P("fsdp"),
        P("fsdp"),
        P("ctx", "fsdp", None),
    )
    return jax.shard_map(
        on_device,
        mesh=mesh,
        in_specs=placed,
        out_specs=(
            P("ctx", "fsdp", None),
            P(("ctx", "fsdp"), None, None),
            P("fsdp", None),
            P("fsdp"),
            P("fsdp", None),
            P("fsdp", None),
            P("fsdp"),
            P("fsdp", None),
            P("fsdp"),
            P("fsdp"),
            P("fsdp"),
            P("fsdp", None),
            P("fsdp"),
            P("fsdp", None),
            P("fsdp"),
            P("fsdp"),
            P("fsdp"),
        ),
        check_vma=False,
    )
```

```python
import functools

import jax
import jax.numpy as jnp
from jax import lax
from jax.experimental import pallas as pl
from jax.experimental.pallas import tpu as pltpu
from jax.sharding import PartitionSpec as P

SCALE = 64 ** (-0.5)
LOG2E = 1.4426950408889634
LAST_SLOT = 12
VMEM_BYTES = 60 * 2**20

NORM_EPSILON = 1e-12
NEG_BIG = -1e30
ROOT_HALF = 0.7071067811865476
ROOT_TWO_PI = 2.5066282746310002


def norm_forward(source, gain_vec, shift_vec):
    centre = source - jnp.mean(source, axis=-1, keepdims=True)
    inv_scale = lax.rsqrt(jnp.mean(centre * centre, axis=-1, keepdims=True) + NORM_EPSILON)
    unit_rows = centre * inv_scale
    return (unit_rows * gain_vec + shift_vec, unit_rows, inv_scale)


def norm_backward(upstream, unit_rows, inv_scale, gain_vec):
    scaled = upstream * gain_vec
    plain_mean = jnp.mean(scaled, axis=-1, keepdims=True)
    cross_mean = jnp.mean(scaled * unit_rows, axis=-1, keepdims=True)
    d_source = inv_scale * (scaled - plain_mean - unit_rows * cross_mean)
    return (d_source, jnp.sum(upstream * unit_rows, axis=0), jnp.sum(upstream, axis=0))


def gelu_exact(source):
    return 0.5 * source * (1.0 + jax.scipy.special.erf(source * ROOT_HALF))


def gelu_slope(source):
    return (
        0.5 * (1.0 + jax.scipy.special.erf(source * ROOT_HALF))
        + source * jnp.exp(-0.5 * source * source) / ROOT_TWO_PI
    )


def product(left, right, dims):
    return lax.dot_general(left, right, (dims, ((), ())), preferred_element_type=jnp.float32)


def lane_is_low():
    return lax.broadcasted_iota(jnp.int32, (1, 128), 1) < 64


def split_query(query_pair, low_half):
    scaled = query_pair * (SCALE * LOG2E)
    high = scaled.astype(jnp.bfloat16).astype(jnp.float32)
    rest = pltpu.roll(scaled - high, 64, 1)
    return (
        jnp.where(low_half, high, rest).astype(jnp.bfloat16),
        jnp.where(low_half, rest, high).astype(jnp.bfloat16),
    )


def twice(pair, low_half):
    other = pltpu.roll(pair, 64, 1)
    return (
        jnp.where(low_half, pair, other).astype(jnp.bfloat16),
        jnp.where(low_half, other, pair).astype(jnp.bfloat16),
    )


MESH = pl.DeviceIdType.MESH
DMA = pltpu.SemaphoreType.DMA
ANY = pl.BlockSpec(memory_space=pl.ANY)
SUM_PLAN = {
    3: ((0, "after_core"),),
    4: ((1, "after_core"), (2, "after_core")),
    8: ((0, "after_pair"),),
    12: ((1, "after_pair"),),
    13: ((2, "after_pair"),),
    15: ((0, "after_line"),),
    18: ((0, "after_across"),),
    19: ((1, "after_line"),),
    20: ((2, "after_line"),),
    22: ((1, "after_across"),),
    23: ((2, "after_across"),),
}
STAGES = ("start", "after_core", "after_across", "after_group", "finish")


def places():
    ctx, group = lax.axis_index("ctx"), lax.axis_index("fsdp")
    return ctx, group, lax.rem(ctx + 2, 4), ctx + 1 - 2 * lax.rem(ctx, 2)


def remote(source, target, send_sem, recv_sem, where):
    return pltpu.make_async_remote_copy(
        src_ref=source,
        dst_ref=target,
        send_sem=send_sem,
        recv_sem=recv_sem,
        device_id=where,
        device_id_type=MESH,
    )


def greet(count):
    ctx, group, _, _ = places()
    barrier = pltpu.get_barrier_semaphore()

    def one(step, carry):
        pl.semaphore_signal(
            barrier,
            inc=1,
            device_id={"fsdp": lax.rem(group + step, count)},
            device_id_type=MESH,
        )
        return carry

    lax.fori_loop(1, count, one, 0)
    for other in range(1, 4):
        pl.semaphore_signal(
            barrier, inc=1, device_id={"ctx": lax.rem(ctx + other, 4)}, device_id_type=MESH
        )
    pl.semaphore_wait(barrier, count - 1 + 3)


class Gather:
    SCRATCH = 11

    def __init__(self, kinds, sems, count, over_x=True):
        self.kinds, self.count, self.over_x = kinds, count, over_x
        self.right_send, self.left_send, self.line_recv = sems[:3]
        self.y_send, self.y_recv, self.x_send, self.x_recv = sems[3:7]
        self.s_send, self.s_recv, self.r_send, self.r_recv = sems[7:11]
        self.ctx, self.group, self.across, self.sibling = places()
        self.line, self.side, self.length = self.group // 2, lax.rem(self.group, 2), count // 2

    @staticmethod
    def scratch(kinds, count):
        return [DMA((kinds, count))] * Gather.SCRATCH

    def copy(self, kind, block, quarter, send, recv, where, own=False):
        mine, place = self.kinds[kind]
        target = place(block, quarter)
        source = mine(quarter) if own else target
        return remote(source, target, send.at[kind, block], recv.at[kind, block], where)

    def right(self, kind, block, own=False):
        there = {"fsdp": lax.rem(self.group + 2, self.count)}
        return self.copy(kind, block, self.ctx, self.right_send, self.line_recv, there, own)

    def left(self, kind, block, own=False):
        there = {"fsdp": lax.rem(self.group - 2 + self.count, self.count)}
        return self.copy(kind, block, self.ctx, self.left_send, self.line_recv, there, own)

    def pair(self, kind, block, own=False):
        there = {"fsdp": self.group + 1 - 2 * self.side}
        return self.copy(kind, block, self.ctx, self.y_send, self.y_recv, there, own)

    def cross(self, kind, block):
        return self.copy(kind, block, self.ctx, self.x_send, self.x_recv, {"ctx": self.across})

    def share(self, kind, block):
        return self.copy(kind, block, self.ctx, self.s_send, self.s_recv, {"ctx": self.sibling})

    def relay(self, kind, block):
        return self.copy(kind, block, self.across, self.r_send, self.r_recv, {"ctx": self.sibling})

    def hand_over(self, kind, block):
        if self.over_x:
            self.cross(kind, block).start()
        self.share(kind, block).start()

    def at(self, line, side):
        return 2 * line + side

    def every(self, body):
        for kind in range(len(self.kinds)):
            body(kind)

    def before(self, distance, body):
        @pl.when(self.line - distance >= 0)
        def _():
            body(self.line - distance)

    def after(self, distance, body):
        @pl.when(self.line + distance < self.length)
        def _():
            body(self.line + distance)

    def start(self):
        block = self.group

        def body(kind):
            self.after(1, lambda _: self.right(kind, block, True).start())
            self.before(1, lambda _: self.left(kind, block, True).start())
            self.pair(kind, block, True).start()

        self.every(body)

    def along(self, distance):
        def from_left(line):
            block = self.at(line, self.side)

            def body(kind):
                self.right(kind, block).wait_recv()
                self.after(1, lambda _: self.right(kind, block).start())
                self.pair(kind, block).start()
                self.hand_over(kind, block)

            self.every(body)

        def from_right(line):
            block = self.at(line, self.side)

            def body(kind):
                self.left(kind, block).wait_recv()
                self.before(1, lambda _: self.left(kind, block).start())
                self.pair(kind, block).start()
                self.hand_over(kind, block)

            self.every(body)

        self.before(distance, from_left)
        self.after(distance, from_right)

    def both(self, distance, side, body):
        if isinstance(distance, int) and distance == 0:
            body(self.at(self.line, side))
        else:
            self.before(distance, lambda line: body(self.at(line, side)))
            self.after(distance, lambda line: body(self.at(line, side)))

    def beside(self, distance):
        def one(block):
            def body(kind):
                self.pair(kind, block).wait_recv()
                self.hand_over(kind, block)

            self.every(body)

        self.both(distance, 1 - self.side, one)

    def crossed(self, distance, side):
        def one(block):
            def body(kind):
                self.cross(kind, block).wait_recv()
                self.relay(kind, block).start()

            self.every(body)

        self.both(distance, self.side if side == 0 else 1 - self.side, one)

    def finish(self):
        def passed(block):
            def body(kind):
                self.share(kind, block).wait()
                if self.over_x:
                    self.cross(kind, block).wait_send()
                    self.relay(kind, block).wait()

            self.every(body)

        def own(kind):
            self.after(1, lambda _: self.right(kind, self.group).wait_send())
            self.before(1, lambda _: self.left(kind, self.group).wait_send())
            self.pair(kind, self.group).wait_send()

        self.every(own)

        def one(distance, carry):
            def lefts(line):
                block = self.at(line, self.side)

                def body(kind):
                    self.after(1, lambda _: self.right(kind, block).wait_send())
                    self.pair(kind, block).wait_send()

                self.every(body)
                passed(block)

            def rights(line):
                block = self.at(line, self.side)

                def body(kind):
                    self.before(1, lambda _: self.left(kind, block).wait_send())
                    self.pair(kind, block).wait_send()

                self.every(body)
                passed(block)

            self.before(distance, lefts)
            self.after(distance, rights)
            self.both(distance, 1 - self.side, passed)
            return carry

        lax.fori_loop(1, self.length, one, 0)
        passed(self.at(self.line, 1 - self.side))


def arrival_kernel(
    placed,
    weights,
    small,
    tokens,
    gathered,
    small_all,
    tok_stage,
    w_stage,
    small_stage,
    local_sem,
    tok_send,
    tok_recv,
    small_send,
    small_recv,
    x_send,
    x_recv,
    s_send,
    s_recv,
    r_send,
    r_recv,
    *sems,
    count,
):
    ctx, group, across, sibling = places()
    half = pl.ds(2 * lax.rem(ctx, 2), 2)
    kind = (lambda q: weights.at[half], lambda b, q: gathered.at[half, b])
    gather = Gather((kind,), sems, count, over_x=False)
    own_tok = pltpu.make_async_copy(placed.at[group], tok_stage, local_sem.at[0])
    own_w = pltpu.make_async_copy(weights, w_stage, local_sem.at[1])
    own_small = pltpu.make_async_copy(small, small_stage, local_sem.at[2])
    own_tok.start()
    own_w.start()
    own_small.start()
    greet(count)

    def tok_copy(peer, step):
        return remote(
            placed.at[peer],
            tokens.at[ctx, group],
            tok_send.at[step],
            tok_recv.at[step],
            {"fsdp": peer},
        )

    def small_copy(peer, step):
        return remote(
            small, small_all.at[group], small_send.at[step], small_recv.at[step], {"fsdp": peer}
        )

    def pass_on(block, quarter, send, recv, target):
        place = tokens.at[quarter, block]
        return remote(place, place, send.at[block], recv.at[block], {"ctx": target})

    def across_copy(block):
        return pass_on(block, ctx, x_send, x_recv, across)

    def sibling_copy(block):
        return pass_on(block, ctx, s_send, s_recv, sibling)

    def relay_copy(block):
        return pass_on(block, across, r_send, r_recv, sibling)

    def send(step, carry):
        peer = lax.rem(group + step, count)
        tok_copy(peer, step).start()
        small_copy(peer, step).start()
        return carry

    gather.start()
    lax.fori_loop(1, count, send, 0)
    own_tok.wait()
    own_w.wait()
    own_small.wait()
    put_tok = pltpu.make_async_copy(tok_stage, tokens.at[ctx, group], local_sem.at[0])
    put_w = pltpu.make_async_copy(w_stage, gathered.at[:, group], local_sem.at[1])
    put_small = pltpu.make_async_copy(small_stage, small_all.at[group], local_sem.at[2])
    put_tok.start()
    put_w.start()
    put_small.start()
    put_tok.wait()
    across_copy(group).start()
    sibling_copy(group).start()
    put_w.wait()
    put_small.wait()

    def arrive(step, carry):
        origin = lax.rem(group - step + count, count)
        tok_copy(origin, step).wait_recv()
        across_copy(origin).start()
        sibling_copy(origin).start()
        return carry

    length = count // 2
    gather.along(1)
    gather.beside(0)
    lax.fori_loop(1, 3, arrive, 0)

    def advance(distance, carry):
        gather.along(distance)
        gather.beside(distance - 1)
        lax.fori_loop(2 * distance - 1, 2 * distance + 1, arrive, 0)
        return carry

    lax.fori_loop(2, length, advance, 0)
    gather.beside(length - 1)
    lax.fori_loop(2 * length - 1, count, arrive, 0)

    def passed(step, carry):
        origin = lax.rem(group - step + count, count)
        across_copy(origin).wait_recv()
        relay_copy(origin).start()
        return carry

    lax.fori_loop(0, count, passed, 0)
    gather.finish()

    def finish(step, carry):
        origin = lax.rem(group - step + count, count)
        across_copy(origin).wait_send()
        sibling_copy(origin).wait()
        relay_copy(origin).wait()
        return carry

    lax.fori_loop(0, count, finish, 0)

    def sent(step, carry):
        peer = lax.rem(group + step, count)
        tok_copy(peer, step).wait_send()
        small_copy(peer, step).wait()
        return carry

    lax.fori_loop(1, count, sent, 0)


def bring_in(placed, weights, small):
    count, rows, width = placed.shape
    return pl.pallas_call(
        functools.partial(arrival_kernel, count=count),
        in_specs=[ANY] * 3,
        out_specs=[ANY] * 3,
        out_shape=[
            jax.ShapeDtypeStruct((4, count, rows, width), jnp.bfloat16),
            jax.ShapeDtypeStruct((4, count) + weights.shape[1:], jnp.bfloat16),
            jax.ShapeDtypeStruct((count,) + small.shape, jnp.bfloat16),
        ],
        scratch_shapes=[
            pltpu.VMEM((rows, width), jnp.bfloat16),
            pltpu.VMEM((4,) + weights.shape[1:], jnp.bfloat16),
            pltpu.VMEM(small.shape, jnp.bfloat16),
            DMA((3,)),
        ]
        + [DMA((count,))] * 10
        + Gather.scratch(1, count),
        compiler_params=pltpu.CompilerParams(
            collective_id=0, has_side_effects=True, vmem_limit_bytes=8 * 2**20
        ),
        name="bring_in",
    )(placed, weights, small)


class Sum:
    SCRATCH = 16

    def __init__(self, ref, out, scratch, count):
        self.ref, self.out, self.count = ref, out, count
        self.near, self.far, self.got_near, self.got_far = scratch[:4]
        self.got_across, self.got_group, self.done = scratch[4:7]
        self.load, self.c_send, self.c_recv, self.x_send, self.x_recv = scratch[7:12]
        self.g_send, self.g_recv, self.o_send, self.o_recv = scratch[12:16]
        self.ctx, self.group, self.across, self.sibling = places()
        self.width = self.near.shape[-1]

    @staticmethod
    def scratch(count, rows, width):
        return (
            [pltpu.VMEM((count, rows, width), jnp.bfloat16)] * 6
            + [pltpu.VMEM((rows, width), jnp.bfloat16)]
            + [DMA((2,))] * 3
            + [DMA((count,))] * 4
            + [DMA((4,))] * 2
        )

    def quarter(self, index):
        start = pl.multiple_of(lax.rem(index, 2) * self.width, self.width)
        return self.ref.at[:, index // 2, :, pl.ds(start, self.width)]

    def loads(self):
        return (
            pltpu.make_async_copy(self.quarter(self.across), self.far, self.load.at[0]),
            pltpu.make_async_copy(self.quarter(self.ctx), self.near, self.load.at[1]),
        )

    def cores(self):
        beyond = lax.rem(self.sibling + 2, 4)
        there = {"ctx": self.sibling}
        return (
            remote(self.quarter(beyond), self.got_far, self.c_send.at[0], self.c_recv.at[0], there),
            remote(
                self.quarter(self.sibling),
                self.got_near,
                self.c_send.at[1],
                self.c_recv.at[1],
                there,
            ),
        )

    def x_copy(self, block):
        return remote(
            self.far.at[block],
            self.got_across.at[block],
            self.x_send.at[block],
            self.x_recv.at[block],
            {"ctx": self.across},
        )

    def g_copy(self, peer, step):
        return remote(
            self.near.at[peer],
            self.got_group.at[step],
            self.g_send.at[step],
            self.g_recv.at[step],
            {"fsdp": peer},
        )

    def o_copy(self, other):
        return remote(
            self.done,
            self.out.at[self.ctx],
            self.o_send.at[other],
            self.o_recv.at[other],
            {"ctx": lax.rem(self.ctx + other, 4)},
        )

    def own_out(self):
        return pltpu.make_async_copy(self.done, self.out.at[self.ctx], self.load.at[0])

    def add(self, total, other):
        def one(block, carry):
            both = total[block].astype(jnp.float32) + other[block].astype(jnp.float32)
            total[block] = both.astype(jnp.bfloat16)
            return carry

        lax.fori_loop(0, self.count, one, 0)

    def start(self):
        for copy in self.loads() + self.cores():
            copy.start()

    def after_core(self):
        loads, cores = self.loads(), self.cores()
        loads[0].wait()
        cores[0].wait_recv()
        self.add(self.far, self.got_far)

        def send(step, carry):
            self.x_copy(lax.rem(self.group + 1 + step, self.count)).start()
            return carry

        lax.fori_loop(0, self.count, send, 0)
        loads[1].wait()
        cores[1].wait_recv()
        self.add(self.near, self.got_near)
        cores[0].wait_send()
        cores[1].wait_send()

    def after_across(self):
        def one(step, carry):
            block = lax.rem(self.group + step, self.count)
            self.x_copy(block).wait()
            both = self.near[block].astype(jnp.float32) + self.got_across[block].astype(jnp.float32)
            self.near[block] = both.astype(jnp.bfloat16)
            self.g_copy(block, step).start()
            return carry

        lax.fori_loop(1, self.count, one, 0)
        self.x_copy(self.group).wait()

    def after_group(self):
        group = self.group
        total = self.near[group].astype(jnp.float32) + self.got_across[group].astype(jnp.float32)

        def one(step, total):
            self.g_copy(lax.rem(group + step, self.count), step).wait()
            return total + self.got_group[step].astype(jnp.float32)

        self.done[...] = lax.fori_loop(1, self.count, one, total).astype(jnp.bfloat16)
        self.own_out().start()
        for other in range(1, 4):
            self.o_copy(other).start()

    def finish(self):
        self.own_out().wait()
        for other in range(1, 4):
            self.o_copy(other).wait()


class VectorSum:
    SCRATCH = 9

    def __init__(self, ref, out, scratch, count):
        self.ref, self.out, self.count = ref, out, count
        self.total, self.got_ctx, self.got_group = scratch[:3]
        self.load, self.c_send, self.c_recv, self.g_send, self.g_recv = scratch[3:8]
        self.result = scratch[8]
        self.ctx, self.group, _, _ = places()

    @staticmethod
    def scratch(count, rows, width):
        return [
            pltpu.VMEM((rows, width), jnp.float32),
            pltpu.VMEM((4, rows, width), jnp.float32),
            pltpu.VMEM((count, rows, width), jnp.float32),
            DMA((2,)),
            DMA((4,)),
            DMA((4,)),
            DMA((count,)),
            DMA((count,)),
            pltpu.VMEM((rows, width), jnp.float32),
        ]

    def own(self):
        return pltpu.make_async_copy(self.ref, self.total, self.load.at[0])

    def own_out(self):
        return pltpu.make_async_copy(self.result, self.out, self.load.at[1])

    def c_copy(self, other):
        return remote(
            self.ref,
            self.got_ctx.at[other],
            self.c_send.at[other],
            self.c_recv.at[other],
            {"ctx": lax.rem(self.ctx + other, 4)},
        )

    def g_copy(self, step):
        return remote(
            self.total,
            self.got_group.at[step],
            self.g_send.at[step],
            self.g_recv.at[step],
            {"fsdp": lax.rem(self.group + step, self.count)},
        )

    def start(self):
        self.own().start()
        for other in range(1, 4):
            self.c_copy(other).start()

    def after_core(self):
        self.own().wait()
        total = self.total[...]
        for other in range(1, 4):
            self.c_copy(other).wait()
            total = total + self.got_ctx[other]
        self.total[...] = total

        def one(step, carry):
            self.g_copy(step).start()
            return carry

        lax.fori_loop(1, self.count, one, 0)

    def after_across(self):
        pass

    def after_group(self):
        def one(step, total):
            self.g_copy(step).wait()
            return total + self.got_group[step]

        self.result[...] = lax.fori_loop(1, self.count, one, self.total[...])
        self.own_out().start()

    def finish(self):
        self.own_out().wait()


class LateSum:
    SCRATCH = 19

    def __init__(self, view, out, scratch, count):
        self.view, self.out, self.count = view, out, count
        self.near, self.got, self.got_pair, self.got_line = scratch[:4]
        self.half, self.got_across, self.done = scratch[4:7]
        self.load, self.c_send, self.c_recv, self.p_send, self.p_recv = scratch[7:12]
        self.l_send, self.l_recv, self.x_send, self.x_recv = scratch[12:16]
        self.o_send, self.o_recv, self.put = scratch[16:19]
        self.ctx, self.group, self.across, self.sibling = places()
        self.core = lax.rem(self.ctx, 2)
        self.line, self.side, self.length = self.group // 2, lax.rem(self.group, 2), count // 2
        self.halves = self.half.shape[0]

    @staticmethod
    def scratch(count, halves, rows, width):
        def block(*lead):
            return pltpu.VMEM(lead + (halves, rows, width), jnp.bfloat16)

        return (
            [block(count), block(count), block(count // 2), block(count // 2)]
            + [block(), block(), block()]
            + [DMA((halves,))] * 3
            + [DMA((count // 2,))] * 4
            + [DMA((1,))] * 2
            + [DMA((halves,))] * 3
        )

    def load_copy(self, half):
        return pltpu.make_async_copy(
            self.view(2 * half + self.core), self.near.at[:, half], self.load.at[half]
        )

    def core_copy(self, half):
        return remote(
            self.view(2 * half + 1 - self.core),
            self.got.at[:, half],
            self.c_send.at[half],
            self.c_recv.at[half],
            {"ctx": self.sibling},
        )

    def pair_copy(self, line):
        return remote(
            self.near.at[2 * line + 1 - self.side],
            self.got_pair.at[line],
            self.p_send.at[line],
            self.p_recv.at[line],
            {"fsdp": self.group + 1 - 2 * self.side},
        )

    def line_copy(self, step):
        peer = 2 * lax.rem(self.line + step, self.length) + self.side
        return remote(
            self.near.at[peer],
            self.got_line.at[step],
            self.l_send.at[step],
            self.l_recv.at[step],
            {"fsdp": peer},
        )

    def x_copy(self):
        return remote(
            self.half, self.got_across, self.x_send.at[0], self.x_recv.at[0], {"ctx": self.across}
        )

    def out_copy(self, half):
        return remote(
            self.done.at[half],
            self.out.at[2 * half + self.core],
            self.o_send.at[half],
            self.o_recv.at[half],
            {"ctx": self.sibling},
        )

    def own_out(self, half):
        return pltpu.make_async_copy(
            self.done.at[half], self.out.at[2 * half + self.core], self.put.at[half]
        )

    def add(self, block, other):
        both = self.near[block].astype(jnp.float32) + other.astype(jnp.float32)
        self.near[block] = both.astype(jnp.bfloat16)

    def start(self):
        for half in range(self.halves):
            self.load_copy(half).start()
            self.core_copy(half).start()

    def after_core(self):
        for half in range(self.halves):
            self.load_copy(half).wait()
            self.core_copy(half).wait()

        def theirs(step, carry):
            line = lax.rem(self.line + step, self.length)
            block = 2 * line + 1 - self.side
            self.add(block, self.got[block])
            self.pair_copy(line).start()
            return carry

        lax.fori_loop(0, self.length, theirs, 0)

        def mine(line, carry):
            block = 2 * line + self.side
            self.add(block, self.got[block])
            return carry

        lax.fori_loop(0, self.length, mine, 0)

    def after_pair(self):
        def one(step, carry):
            line = lax.rem(self.line + step, self.length)
            self.pair_copy(line).wait()
            self.add(2 * line + self.side, self.got_pair[line])
            self.line_copy(step).start()
            return carry

        lax.fori_loop(1, self.length, one, 0)
        self.pair_copy(self.line).wait()
        self.add(self.group, self.got_pair[self.line])

    def after_line(self):
        def one(step, total):
            self.line_copy(step).wait()
            return total + self.got_line[step].astype(jnp.float32)

        total = lax.fori_loop(1, self.length, one, self.near[self.group].astype(jnp.float32))
        self.half[...] = total.astype(jnp.bfloat16)
        self.x_copy().start()

    def after_across(self):
        self.x_copy().wait()
        both = self.half[...].astype(jnp.float32) + self.got_across[...].astype(jnp.float32)
        self.done[...] = both.astype(jnp.bfloat16)
        for half in range(self.halves):
            self.own_out(half).start()
            self.out_copy(half).start()

    def finish(self):
        for half in range(self.halves):
            self.own_out(half).wait()
            self.out_copy(half).wait()


def sums_kernel(*refs, parts, count):
    ins, outs, rest = refs[: parts + 1], refs[parts + 1 : 2 * parts + 2], refs[2 * parts + 2 :]
    jobs = [VectorSum(ins[parts], outs[parts], rest[: VectorSum.SCRATCH], count)]
    rest = rest[VectorSum.SCRATCH :]
    for index in range(parts):
        own = rest[index * Sum.SCRATCH : (index + 1) * Sum.SCRATCH]
        jobs.append(Sum(ins[index], outs[index], own, count))
    greet(count)
    for stage in STAGES:
        for job in jobs:
            getattr(job, stage)()


def sum_gradients(parts, vectors):
    count, _, rows, width = parts[0].shape
    width = width // 2
    scratch = VectorSum.scratch(count, *vectors.shape)
    for _ in parts:
        scratch += Sum.scratch(count, rows, width)
    return pl.pallas_call(
        functools.partial(sums_kernel, parts=len(parts), count=count),
        in_specs=[ANY] * (len(parts) + 1),
        out_specs=[ANY] * (len(parts) + 1),
        out_shape=[jax.ShapeDtypeStruct((4, rows, width), jnp.bfloat16)] * len(parts)
        + [jax.ShapeDtypeStruct(vectors.shape, jnp.float32)],
        scratch_shapes=scratch,
        compiler_params=pltpu.CompilerParams(
            collective_id=1, has_side_effects=True, vmem_limit_bytes=VMEM_BYTES
        ),
        name="sum_gradients",
    )(*parts, vectors)


def gather_plan(length):
    stretch = max(length - 2, 1)
    slots = [[] for _ in range(LAST_SLOT + 1)]

    def put(name, at, over, first):
        for distance in range(1, length):
            slot = min(at + (distance - 1) * over // stretch, LAST_SLOT)
            events = slots[slot]
            if events and events[-1][0] == name:
                events[-1] = (name, events[-1][1], distance + 1)
            else:
                events.append((name, distance, distance + 1))
        if first:
            slots[first].append((name, 0, 1))

    put("along", 2, 4, 0)
    put("beside", 5, 4, 2)
    put("line", 7, 4, 0)
    put("pair", 9, 3, 7)
    return slots


def forward_kernel(
    limit_ref,
    query_ref,
    key_ref,
    value_ref,
    inner_ref,
    outer_ref,
    attended_ref,
    lse_ref,
    inner_all,
    outer_all,
    *scratch,
    key_rows,
    count,
):
    pair = pl.program_id(0)
    pairs = pl.num_programs(0) - 1
    inner_stage, outer_stage, local, *sems = scratch
    width = outer_ref.shape[-1]

    def columns(quarter):
        return pl.ds(pl.multiple_of(quarter * width, width), width)

    kinds = (
        (lambda q: inner_ref.at[:, columns(q)], lambda b, q: inner_all.at[b, :, columns(q)]),
        (lambda q: outer_ref.at[q], lambda b, q: outer_all.at[b, q]),
    )
    gather = Gather(kinds, sems, count)
    loads = (
        pltpu.make_async_copy(inner_ref, inner_stage, local.at[0]),
        pltpu.make_async_copy(outer_ref, outer_stage, local.at[1]),
    )
    puts = (
        pltpu.make_async_copy(inner_stage, inner_all.at[gather.group], local.at[2]),
        pltpu.make_async_copy(outer_stage, outer_all.at[gather.group], local.at[3]),
    )
    plan = gather_plan(count // 2)

    def communicate(events):
        for name, first, last in events:
            act = {
                "along": gather.along,
                "beside": gather.beside,
                "line": lambda distance: gather.crossed(distance, 0),
                "pair": lambda distance: gather.crossed(distance, 1),
            }[name]
            if last - first == 1:
                act(first)
            else:

                def one(distance, carry, act=act):
                    act(distance)
                    return carry

                lax.fori_loop(first, last, one, 0)

    @pl.when(pair == 0)
    def _():
        greet(count)
        for load in loads:
            load.start()
        gather.start()
        for load, put in zip(loads, puts):
            load.wait()
            put.start()

    @pl.when(pair == pairs)
    def _():
        communicate(plan[LAST_SLOT])
        gather.finish()
        for put in puts:
            put.wait()

    @pl.when(pair < pairs)
    def _():
        low_half = lane_is_low()
        limit = limit_ref[0]
        queries = split_query(query_ref[...].astype(jnp.float32), low_half)
        query_rows = query_ref.shape[0]

        def step(tile, state):
            for slot in range(1, LAST_SLOT):
                if plan[slot]:

                    @pl.when(2 * pair + tile == slot)
                    def _(slot=slot):
                        communicate(plan[slot])

            start = pl.multiple_of(tile * key_rows, key_rows)
            usable = start + lax.broadcasted_iota(jnp.int32, (key_rows, 1), 0) < limit
            key_tile = key_ref[pl.ds(start, key_rows), :].astype(jnp.float32)
            keys = twice(jnp.where(usable, key_tile, key_ref[0:1, :].astype(jnp.float32)), low_half)
            value_tile = value_ref[pl.ds(start, key_rows), :].astype(jnp.float32)
            value_tile = jnp.where(usable, value_tile, 0.0)
            count = jnp.where(usable, 1.0, 0.0)
            values = (
                jnp.where(low_half, value_tile, count).astype(jnp.bfloat16),
                jnp.where(low_half, count, value_tile).astype(jnp.bfloat16),
            )
            fresh = []
            for head in range(2):
                top, total = state[head]
                scores = product(queries[head], keys[head], ((1,), (1,)))
                new_top = jnp.maximum(top, jnp.max(scores, axis=1, keepdims=True))
                weights = jnp.exp2(scores - new_top).astype(jnp.bfloat16)
                total = total * jnp.exp2(top - new_top) + product(weights, values[head], ((1,), (0,)))
                fresh.append((new_top, total))
            return tuple(fresh)

        empty = (
            jnp.full((query_rows, 1), NEG_BIG, jnp.float32),
            jnp.zeros((query_rows, 128), jnp.float32),
        )
        (top_a, total_a), (top_b, total_b) = lax.fori_loop(
            0, key_ref.shape[0] // key_rows, step, (empty, empty)
        )
        mass_a, mass_b = total_a[:, 64:65], total_b[:, 0:1]
        attended_ref[...] = jnp.where(low_half, total_a / mass_a, total_b / mass_b)
        lse = jnp.where(low_half, top_a + jnp.log2(mass_a), top_b + jnp.log2(mass_b)).T
        lse_ref[0, 0:1, :] = lse[0:1, :]
        lse_ref[0, 1:2, :] = lse[64:65, :]


def attend_forward(queries, keys, values, limit, inner, outer, count):
    rows, width = queries.shape
    full = keys.shape[0]
    pairs = width // 128
    shard = inner.shape[0]
    now = lambda pair, *_: (0, jnp.minimum(pair, pairs - 1))
    row_spec = pl.BlockSpec((rows, 128), now)
    key_spec = pl.BlockSpec((full, 128), now)
    return pl.pallas_call(
        functools.partial(forward_kernel, key_rows=full // 2, count=count),
        grid_spec=pltpu.PrefetchScalarGridSpec(
            num_scalar_prefetch=1,
            grid=(pairs + 1,),
            in_specs=[row_spec, key_spec, key_spec, ANY, ANY],
            out_specs=[
                row_spec,
                pl.BlockSpec((1, 2, rows), lambda pair, *_: (jnp.minimum(pair, pairs - 1), 0, 0)),
                ANY,
                ANY,
            ],
            scratch_shapes=[
                pltpu.VMEM((shard, 4 * width), jnp.bfloat16),
                pltpu.VMEM((4, shard, width), jnp.bfloat16),
                DMA((4,)),
            ]
            + Gather.scratch(2, count),
        ),
        out_shape=[
            jax.ShapeDtypeStruct((rows, width), jnp.float32),
            jax.ShapeDtypeStruct((pairs, 2, rows), jnp.float32),
            jax.ShapeDtypeStruct((count, shard, 4 * width), jnp.bfloat16),
            jax.ShapeDtypeStruct((count, 4, shard, width), jnp.bfloat16),
        ],
        compiler_params=pltpu.CompilerParams(
            collective_id=3, has_side_effects=True, vmem_limit_bytes=VMEM_BYTES
        ),
        cost_estimate=pl.CostEstimate(
            flops=16 * rows * full * width, bytes_accessed=20_000_000, transcendentals=0
        ),
        name="attend_forward",
    )(limit, queries, keys, values, inner, outer)


def backward_kernel(
    limit_ref,
    query_ref,
    key_ref,
    value_ref,
    grad_ref,
    attended_ref,
    lse_ref,
    inner_ref,
    outer_ref,
    output_ref,
    d_query_ref,
    d_key_ref,
    d_value_ref,
    inner_out,
    outer_out,
    output_out,
    query_sum,
    part,
    got_core,
    far,
    near,
    got_x,
    core_send,
    core_recv,
    x_send,
    x_recv,
    *rest,
    count,
):
    pair = pl.program_id(0)
    pairs = pl.num_programs(0) - 1
    slot = lax.rem(pair, 2)
    ctx, _, across, sibling = places()
    key_rows = query_ref.shape[0]
    def columns(ref, parts):
        size = ref.shape[2] // parts
        return lambda index: ref.at[:, :, pl.ds(pl.multiple_of(index * size, size), size)]

    views = (columns(inner_ref, 4), lambda index: outer_ref.at[:, index], columns(output_ref, 2))
    jobs = [
        LateSum(
            view, out, rest[index * LateSum.SCRATCH : (index + 1) * LateSum.SCRATCH], count
        )
        for index, (view, out) in enumerate(zip(views, (inner_out, outer_out, output_out)))
    ]

    def core_copy(which):
        return remote(
            part.at[which],
            got_core.at[slot, which],
            core_send.at[which],
            core_recv.at[slot, which],
            {"ctx": sibling},
        )

    def x_copy(where):
        return remote(
            far.at[where], got_x.at[where], x_send.at[where], x_recv.at[where], {"ctx": across}
        )

    def settle():
        where = 1 - slot
        x_copy(where).wait()
        for kind, ref in enumerate((d_key_ref, d_value_ref)):
            both = near[where, kind].astype(jnp.float32) + got_x[where, kind].astype(jnp.float32)
            ref[...] = both.astype(jnp.bfloat16)

    @pl.when(pair == 0)
    def _():
        greet(count)
        for job in jobs:
            job.start()

    @pl.when(pair < pairs)
    def _():
        low_half = lane_is_low()
        high_half = jnp.logical_not(low_half)
        lane = lax.broadcasted_iota(jnp.int32, (1, 128), 1)
        limit = limit_ref[0]
        query_pair = query_ref[...].astype(jnp.float32)
        queries = split_query(query_pair, low_half)
        scaled = query_pair * SCALE
        grad_pair = grad_ref[...].astype(jnp.float32)
        overlap = grad_pair * attended_ref[...]
        own_query, own_grad, joined_grad = [], [], []
        for head in range(2):
            mine = low_half if head == 0 else high_half
            own_query.append(jnp.where(mine, scaled, 0.0).astype(jnp.bfloat16))
            own_grad.append(jnp.where(mine, grad_pair, 0.0).astype(jnp.bfloat16))
            delta = -jnp.sum(jnp.where(mine, overlap, 0.0), axis=1, keepdims=True)
            first = delta.astype(jnp.bfloat16).astype(jnp.float32)
            second = (delta - first).astype(jnp.bfloat16).astype(jnp.float32)
            third = delta - first - second
            spare = 64 * (1 - head)
            joined = jnp.where(lane == spare + 2, third, 0.0)
            joined = jnp.where(lane == spare + 1, second, joined)
            joined = jnp.where(lane == spare, first, joined)
            joined_grad.append(jnp.where(mine, grad_pair, joined).astype(jnp.bfloat16))
        query_sum[...] = jnp.zeros_like(query_sum)

        def step(tile, carry):
            for at, stages in SUM_PLAN.items():

                @pl.when(4 * pair + tile == at)
                def _(stages=stages):
                    for index, stage in stages:
                        getattr(jobs[index], stage)()

            odd = lax.rem(tile, 2)
            quarter = lax.rem(sibling + odd * (ctx - sibling) + 2 * (1 - tile // 2), 4)
            start = pl.multiple_of(quarter * key_rows, key_rows)
            usable = start + lax.broadcasted_iota(jnp.int32, (key_rows, 1), 0) < limit
            key_tile = key_ref[pl.ds(start, key_rows), :].astype(jnp.float32)
            value_tile = value_ref[pl.ds(start, key_rows), :].astype(jnp.float32)
            keys = twice(jnp.where(usable, key_tile, key_ref[0:1, :].astype(jnp.float32)), low_half)
            own_tile = jnp.where(usable, key_tile * SCALE, 0.0)
            key_piece = value_piece = None
            for head in range(2):
                mine = low_half if head == 0 else high_half
                values = jnp.where(mine, value_tile, 1.0).astype(jnp.bfloat16)
                own_key = jnp.where(mine, own_tile, 0.0).astype(jnp.bfloat16)
                scores = product(keys[head], queries[head], ((1,), (1,)))
                probs = jnp.exp2(scores - lse_ref[0, head : head + 1, :])
                slopes = product(values, joined_grad[head], ((1,), (1,)))
                score_grads = (probs * slopes).astype(jnp.bfloat16)
                value_term = product(probs.astype(jnp.bfloat16), own_grad[head], ((1,), (0,)))
                key_term = product(score_grads, own_query[head], ((1,), (0,)))
                value_piece = value_term if value_piece is None else value_piece + value_term
                key_piece = key_term if key_piece is None else key_piece + key_term
                query_sum[...] += product(own_key, score_grads, ((0,), (0,)))
            pieces = (jnp.where(usable, key_piece, 0.0), jnp.where(usable, value_piece, 0.0))

            @pl.when(odd == 0)
            def _():
                which = tile // 2
                for kind in range(2):
                    part[which, kind] = pieces[kind].astype(jnp.bfloat16)
                core_copy(which).start()

            @pl.when(tile == 1)
            def _():
                @pl.when(pair > 0)
                def _():
                    settle()

                core_copy(0).wait_recv()
                for kind in range(2):
                    both = pieces[kind] + got_core[slot, 0, kind].astype(jnp.float32)
                    far[slot, kind] = both.astype(jnp.bfloat16)
                x_copy(slot).start()

            @pl.when(tile == 3)
            def _():
                core_copy(1).wait_recv()
                for kind in range(2):
                    both = pieces[kind] + got_core[slot, 1, kind].astype(jnp.float32)
                    near[slot, kind] = both.astype(jnp.bfloat16)
                core_copy(0).wait_send()
                core_copy(1).wait_send()

            return carry

        lax.fori_loop(0, 4, step, 0)
        d_query_ref[...] = query_sum[...].T.astype(jnp.bfloat16)

    @pl.when(pair == pairs)
    def _():
        settle()
        for job in jobs:
            job.finish()


def attend_backward(queries, keys, values, limit, grad_rows, attended, lse, parts):
    rows, width = queries.shape
    full = keys.shape[0]
    pairs = width // 128
    count, shard = parts[0].shape[:2]
    now = lambda pair, *_: (0, jnp.minimum(pair, pairs - 1))
    before = lambda pair, *_: (0, jnp.maximum(pair - 1, 0))
    row_spec = pl.BlockSpec((rows, 128), now)
    key_spec = pl.BlockSpec((full, 128), now)
    sum_spec = pl.BlockSpec((rows, 128), before)
    tile = (2, rows, 128)
    return pl.pallas_call(
        functools.partial(backward_kernel, count=count),
        grid_spec=pltpu.PrefetchScalarGridSpec(
            num_scalar_prefetch=1,
            grid=(pairs + 1,),
            in_specs=[
                row_spec,
                key_spec,
                key_spec,
                row_spec,
                row_spec,
                pl.BlockSpec((1, 2, rows), lambda pair, *_: (jnp.minimum(pair, pairs - 1), 0, 0)),
                ANY,
                ANY,
                ANY,
            ],
            out_specs=[row_spec, sum_spec, sum_spec, ANY, ANY, ANY],
            scratch_shapes=[
                pltpu.VMEM((128, rows), jnp.float32),
                pltpu.VMEM((2,) + tile, jnp.bfloat16),
                pltpu.VMEM((2, 2) + tile, jnp.bfloat16),
                pltpu.VMEM((2,) + tile, jnp.bfloat16),
                pltpu.VMEM((2,) + tile, jnp.bfloat16),
                pltpu.VMEM((2,) + tile, jnp.bfloat16),
                DMA((2,)),
                DMA((2, 2)),
                DMA((2,)),
                DMA((2,)),
            ]
            + LateSum.scratch(count, 2, shard, width) * 2
            + LateSum.scratch(count, 1, shard, width // 2),
        ),
        out_shape=[jax.ShapeDtypeStruct((rows, width), jnp.bfloat16)] * 3
        + [jax.ShapeDtypeStruct((4, shard, width), jnp.bfloat16)] * 2
        + [jax.ShapeDtypeStruct((2, shard, width // 2), jnp.bfloat16)],
        compiler_params=pltpu.CompilerParams(
            collective_id=2, has_side_effects=True, vmem_limit_bytes=VMEM_BYTES
        ),
        cost_estimate=pl.CostEstimate(
            flops=40 * rows * full * width, bytes_accessed=40_000_000, transcendentals=0
        ),
        name="attend_backward",
    )(limit, queries, keys, values, grad_rows, attended, lse, *parts)


def on_device(
    hidden_in,
    lengths,
    seq_order,
    query_weight,
    query_bias,
    key_weight,
    value_weight,
    value_bias,
    output_weight,
    output_bias,
    norm1_gain,
    norm1_shift,
    inner_weight,
    inner_bias,
    outer_weight,
    outer_bias,
    norm2_gain,
    norm2_shift,
    cotangent,
):
    width = hidden_in.shape[2]
    count = lax.axis_size("fsdp")
    group = lax.axis_index("fsdp")
    shard = query_bias.shape[0]
    low = jnp.bfloat16
    placed = jnp.swapaxes(hidden_in.at[:, seq_order].get(mode="promise_in_bounds"), 0, 1)
    vectors = jnp.concatenate(
        (
            jnp.stack(
                (
                    query_bias,
                    value_bias,
                    output_bias,
                    norm1_gain,
                    norm1_shift,
                    outer_bias,
                    norm2_gain,
                    norm2_shift,
                )
            ),
            inner_bias.reshape(4, shard),
        )
    )
    vectors = jnp.pad(vectors, ((0, 4), (0, 128 - shard)))
    weights = jnp.stack((query_weight, key_weight, value_weight, output_weight))
    tokens, weights, vectors = bring_in(placed, weights, vectors)
    w_query, w_key, w_value, w_output = (weights[i].reshape(width, width) for i in range(4))
    vectors = vectors[:, :12, :shard].astype(jnp.float32)
    b_query, b_value, b_output, gain_one, shift_one, b_outer, gain_two, shift_two = (
        vectors[:, i].reshape(width) for i in range(8)
    )
    b_inner = vectors[:, 8:].reshape(-1)
    limits = jnp.take(lengths, jnp.take(seq_order, group[None]))
    all_rows = tokens.reshape(-1, width)
    local_len = all_rows.shape[0] // 4
    token_rows = lax.dynamic_index_in_dim(tokens, lax.axis_index("ctx"), 0, False)
    token_rows = token_rows.reshape(local_len, width)
    queries = (product(token_rows, w_query, ((1,), (0,))) + b_query).astype(low)
    keys = product(all_rows, w_key, ((1,), (0,))).astype(low)
    values = (product(all_rows, w_value, ((1,), (0,))) + b_value).astype(low)
    attended, lse, w_inner, w_outer = attend_forward(
        queries,
        keys,
        values,
        limits,
        inner_weight,
        outer_weight.reshape(4, shard, width),
        count,
    )
    w_inner = w_inner.reshape(width, 4 * width)
    w_outer = w_outer.reshape(4 * width, width)
    mixed_low = attended.astype(low)
    branch = product(mixed_low, w_output, ((1,), (0,))) + b_output
    normed, unit_one, scale_one = norm_forward(
        token_rows.astype(jnp.float32) + branch, gain_one, shift_one
    )
    normed_low = normed.astype(low)
    inner_pre = product(normed_low, w_inner, ((1,), (0,))) + b_inner
    activated = gelu_exact(inner_pre).astype(low)
    outer_out = product(activated, w_outer, ((1,), (0,))) + b_outer
    second, unit_two, scale_two = norm_forward(normed + outer_out, gain_two, shift_two)
    layer_out = second.astype(low).reshape(local_len, 1, width)
    upstream = cotangent.reshape(local_len, width).astype(jnp.float32)
    d_second, grad_gain_two, grad_shift_two = norm_backward(upstream, unit_two, scale_two, gain_two)
    d_outer = d_second.astype(low)
    grad_outer_w = product(activated, d_outer, ((0,), (0,))).astype(low)
    grad_outer_b = jnp.sum(d_outer.astype(jnp.float32), axis=0)
    inner_grad = product(d_outer, w_outer, ((1,), (1,)))
    d_inner = (inner_grad * gelu_slope(inner_pre)).astype(low)
    grad_inner_w = product(normed_low, d_inner, ((0,), (0,))).astype(low)
    grad_inner_b = jnp.sum(d_inner.astype(jnp.float32), axis=0)
    d_normed = d_second + product(d_inner, w_inner, ((1,), (1,)))
    d_res, grad_gain_one, grad_shift_one = norm_backward(d_normed, unit_one, scale_one, gain_one)
    d_branch = d_res.astype(low)
    grad_output_w = product(mixed_low, d_branch, ((0,), (0,))).astype(low)
    grad_output_b = jnp.sum(d_branch.astype(jnp.float32), axis=0)
    d_mixed = product(d_branch, w_output, ((1,), (1,))).astype(low)
    d_query, d_keys, d_values, inner_w, outer_w, output_w = attend_backward(
        queries,
        keys,
        values,
        limits,
        d_mixed,
        attended,
        lse,
        (
            grad_inner_w.reshape(count, shard, 4 * width),
            grad_outer_w.reshape(count, 4, shard, width),
            grad_output_w.reshape(count, shard, width),
        ),
    )
    grad_query_w = product(token_rows, d_query, ((0,), (0,))).astype(low)
    grad_query_b = jnp.sum(d_query.astype(jnp.float32), axis=0)
    grad_key_w = product(token_rows, d_keys, ((0,), (0,))).astype(low)
    grad_value_w = product(token_rows, d_values, ((0,), (0,))).astype(low)
    grad_value_b = jnp.sum(d_values.astype(jnp.float32), axis=0)
    d_placed = d_res + product(d_query, w_query, ((1,), (1,)))
    d_placed = d_placed + product(d_keys, w_key, ((1,), (1,)))
    d_placed = d_placed + product(d_values, w_value, ((1,), (1,)))
    back_rows = d_placed.astype(low).reshape(count, local_len // count, width)
    returned = lax.all_to_all(back_rows, "fsdp", split_axis=0, concat_axis=0, tiled=True)
    inverse = jnp.argmax(seq_order[:, None] == jnp.arange(count), axis=0)
    grad_in = jnp.swapaxes(returned, 0, 1).at[:, inverse].get(mode="promise_in_bounds")
    small_sums = jnp.concatenate(
        (
            jnp.stack(
                (
                    grad_query_b,
                    grad_value_b,
                    grad_output_b,
                    grad_gain_one,
                    grad_shift_one,
                    grad_outer_b,
                    grad_gain_two,
                    grad_shift_two,
                )
            ),
            grad_inner_b.reshape(4, width),
            jnp.zeros((4, width), jnp.float32),
        )
    )
    *attention_w, small_sums = sum_gradients(
        [
            part.reshape(count, 2, shard // 2, width)
            for part in (grad_query_w, grad_key_w, grad_value_w)
        ],
        small_sums,
    )
    attention_w = [
        jnp.swapaxes(part.reshape(2, 2, shard // 2, width // 2), 1, 2)
        .reshape(shard, width)
        .astype(jnp.float32)
        for part in attention_w
    ]
    output_w = jnp.swapaxes(output_w, 0, 1).reshape(shard, width).astype(jnp.float32)
    inner_w = jnp.swapaxes(inner_w, 0, 1).reshape(shard, 4 * width).astype(jnp.float32)
    outer_w = outer_w.reshape(4 * shard, width).astype(jnp.float32)
    small = lax.dynamic_slice_in_dim(small_sums[:8], group * shard, shard, axis=1)
    inner_b = lax.dynamic_slice_in_dim(
        small_sums[8:12].reshape(-1), group * 4 * shard, 4 * shard, axis=0
    )
    return (
        layer_out,
        grad_in,
        attention_w[0],
        small[0],
        attention_w[1],
        attention_w[2],
        small[1],
        output_w,
        small[2],
        small[3],
        small[4],
        inner_w,
        inner_b,
        outer_w,
        small[5],
        small[6],
        small[7],
    )


def solution(mesh):
    placed = (
        P(("ctx", "fsdp"), None, None),
        P(),
        P(),
        P("fsdp", None),
        P("fsdp"),
        P("fsdp", None),
        P("fsdp", None),
        P("fsdp"),
        P("fsdp", None),
        P("fsdp"),
        P("fsdp"),
        P("fsdp"),
        P("fsdp", None),
        P("fsdp"),
        P("fsdp", None),
        P("fsdp"),
        P("fsdp"),
        P("fsdp"),
        P("ctx", "fsdp", None),
    )
    return jax.shard_map(
        on_device,
        mesh=mesh,
        in_specs=placed,
        out_specs=(
            P("ctx", "fsdp", None),
            P(("ctx", "fsdp"), None, None),
            P("fsdp", None),
            P("fsdp"),
            P("fsdp", None),
            P("fsdp", None),
            P("fsdp"),
            P("fsdp", None),
            P("fsdp"),
            P("fsdp"),
            P("fsdp"),
            P("fsdp", None),
            P("fsdp"),
            P("fsdp", None),
            P("fsdp"),
            P("fsdp"),
            P("fsdp"),
        ),
        check_vma=False,
    )
```

```python
import functools

import jax
import jax.numpy as jnp
from jax import lax
from jax.experimental import pallas as pl
from jax.experimental.pallas import tpu as pltpu
from jax.sharding import PartitionSpec as P

SCALE = 64 ** (-0.5)
LOG2E = 1.4426950408889634
LAST_SLOT = 12
VMEM_BYTES = 60 * 2**20

NORM_EPSILON = 1e-12
NEG_BIG = -1e30
ROOT_HALF = 0.7071067811865476
ROOT_TWO_PI = 2.5066282746310002


def norm_forward(source, gain_vec, shift_vec):
    centre = source - jnp.mean(source, axis=-1, keepdims=True)
    inv_scale = lax.rsqrt(jnp.mean(centre * centre, axis=-1, keepdims=True) + NORM_EPSILON)
    unit_rows = centre * inv_scale
    return (unit_rows * gain_vec + shift_vec, unit_rows, inv_scale)


def norm_backward(upstream, unit_rows, inv_scale, gain_vec):
    scaled = upstream * gain_vec
    plain_mean = jnp.mean(scaled, axis=-1, keepdims=True)
    cross_mean = jnp.mean(scaled * unit_rows, axis=-1, keepdims=True)
    d_source = inv_scale * (scaled - plain_mean - unit_rows * cross_mean)
    return (d_source, jnp.sum(upstream * unit_rows, axis=0), jnp.sum(upstream, axis=0))


def gelu_exact(source):
    return 0.5 * source * (1.0 + jax.scipy.special.erf(source * ROOT_HALF))


def gelu_slope(source):
    return (
        0.5 * (1.0 + jax.scipy.special.erf(source * ROOT_HALF))
        + source * jnp.exp(-0.5 * source * source) / ROOT_TWO_PI
    )


def product(left, right, dims):
    return lax.dot_general(left, right, (dims, ((), ())), preferred_element_type=jnp.float32)


def lane_is_low():
    return lax.broadcasted_iota(jnp.int32, (1, 128), 1) < 64


def split_query(query_pair, low_half):
    scaled = query_pair * (SCALE * LOG2E)
    high = scaled.astype(jnp.bfloat16).astype(jnp.float32)
    rest = pltpu.roll(scaled - high, 64, 1)
    return (
        jnp.where(low_half, high, rest).astype(jnp.bfloat16),
        jnp.where(low_half, rest, high).astype(jnp.bfloat16),
    )


def twice(pair, low_half):
    other = pltpu.roll(pair, 64, 1)
    return (
        jnp.where(low_half, pair, other).astype(jnp.bfloat16),
        jnp.where(low_half, other, pair).astype(jnp.bfloat16),
    )


MESH = pl.DeviceIdType.MESH
DMA = pltpu.SemaphoreType.DMA
ANY = pl.BlockSpec(memory_space=pl.ANY)
SUM_PLAN = {
    3: ((0, "after_core"),),
    4: ((1, "after_core"), (2, "after_core")),
    8: ((0, "after_pair"),),
    12: ((1, "after_pair"),),
    13: ((2, "after_pair"),),
    15: ((0, "after_line"),),
    18: ((0, "after_across"),),
    19: ((1, "after_line"),),
    20: ((2, "after_line"),),
    22: ((1, "after_across"),),
    23: ((2, "after_across"),),
}
STAGES = ("start", "after_core", "after_across", "after_group", "finish")


def places():
    ctx, group = lax.axis_index("ctx"), lax.axis_index("fsdp")
    return ctx, group, lax.rem(ctx + 2, 4), ctx + 1 - 2 * lax.rem(ctx, 2)


def remote(source, target, send_sem, recv_sem, where):
    return pltpu.make_async_remote_copy(
        src_ref=source,
        dst_ref=target,
        send_sem=send_sem,
        recv_sem=recv_sem,
        device_id=where,
        device_id_type=MESH,
    )


def greet(count):
    ctx, group, _, _ = places()
    barrier = pltpu.get_barrier_semaphore()

    def one(step, carry):
        pl.semaphore_signal(
            barrier,
            inc=1,
            device_id={"fsdp": lax.rem(group + step, count)},
            device_id_type=MESH,
        )
        return carry

    lax.fori_loop(1, count, one, 0)
    for other in range(1, 4):
        pl.semaphore_signal(
            barrier, inc=1, device_id={"ctx": lax.rem(ctx + other, 4)}, device_id_type=MESH
        )
    pl.semaphore_wait(barrier, count - 1 + 3)


class Gather:
    SCRATCH = 11

    def __init__(self, kinds, sems, count, over_x=True):
        self.kinds, self.count, self.over_x = kinds, count, over_x
        self.right_send, self.left_send, self.line_recv = sems[:3]
        self.y_send, self.y_recv, self.x_send, self.x_recv = sems[3:7]
        self.s_send, self.s_recv, self.r_send, self.r_recv = sems[7:11]
        self.ctx, self.group, self.across, self.sibling = places()
        self.line, self.side, self.length = self.group // 2, lax.rem(self.group, 2), count // 2

    @staticmethod
    def scratch(kinds, count):
        return [DMA((kinds, count))] * Gather.SCRATCH

    def copy(self, kind, block, quarter, send, recv, where, own=False):
        mine, place = self.kinds[kind]
        target = place(block, quarter)
        source = mine(quarter) if own else target
        return remote(source, target, send.at[kind, block], recv.at[kind, block], where)

    def right(self, kind, block, own=False):
        there = {"fsdp": lax.rem(self.group + 2, self.count)}
        return self.copy(kind, block, self.ctx, self.right_send, self.line_recv, there, own)

    def left(self, kind, block, own=False):
        there = {"fsdp": lax.rem(self.group - 2 + self.count, self.count)}
        return self.copy(kind, block, self.ctx, self.left_send, self.line_recv, there, own)

    def pair(self, kind, block, own=False):
        there = {"fsdp": self.group + 1 - 2 * self.side}
        return self.copy(kind, block, self.ctx, self.y_send, self.y_recv, there, own)

    def cross(self, kind, block):
        return self.copy(kind, block, self.ctx, self.x_send, self.x_recv, {"ctx": self.across})

    def share(self, kind, block):
        return self.copy(kind, block, self.ctx, self.s_send, self.s_recv, {"ctx": self.sibling})

    def relay(self, kind, block):
        return self.copy(kind, block, self.across, self.r_send, self.r_recv, {"ctx": self.sibling})

    def hand_over(self, kind, block):
        if self.over_x:
            self.cross(kind, block).start()
        self.share(kind, block).start()

    def at(self, line, side):
        return 2 * line + side

    def every(self, body):
        for kind in range(len(self.kinds)):
            body(kind)

    def before(self, distance, body):
        @pl.when(self.line - distance >= 0)
        def _():
            body(self.line - distance)

    def after(self, distance, body):
        @pl.when(self.line + distance < self.length)
        def _():
            body(self.line + distance)

    def start(self):
        block = self.group

        def body(kind):
            self.after(1, lambda _: self.right(kind, block, True).start())
            self.before(1, lambda _: self.left(kind, block, True).start())
            self.pair(kind, block, True).start()

        self.every(body)

    def along(self, distance):
        def from_left(line):
            block = self.at(line, self.side)

            def body(kind):
                self.right(kind, block).wait_recv()
                self.after(1, lambda _: self.right(kind, block).start())
                self.pair(kind, block).start()
                self.hand_over(kind, block)

            self.every(body)

        def from_right(line):
            block = self.at(line, self.side)

            def body(kind):
                self.left(kind, block).wait_recv()
                self.before(1, lambda _: self.left(kind, block).start())
                self.pair(kind, block).start()
                self.hand_over(kind, block)

            self.every(body)

        self.before(distance, from_left)
        self.after(distance, from_right)

    def both(self, distance, side, body):
        if isinstance(distance, int) and distance == 0:
            body(self.at(self.line, side))
        else:
            self.before(distance, lambda line: body(self.at(line, side)))
            self.after(distance, lambda line: body(self.at(line, side)))

    def beside(self, distance):
        def one(block):
            def body(kind):
                self.pair(kind, block).wait_recv()
                self.hand_over(kind, block)

            self.every(body)

        self.both(distance, 1 - self.side, one)

    def crossed(self, distance, side):
        def one(block):
            def body(kind):
                self.cross(kind, block).wait_recv()
                self.relay(kind, block).start()

            self.every(body)

        self.both(distance, self.side if side == 0 else 1 - self.side, one)

    def finish(self):
        def passed(block):
            def body(kind):
                self.share(kind, block).wait()
                if self.over_x:
                    self.cross(kind, block).wait_send()
                    self.relay(kind, block).wait()

            self.every(body)

        def own(kind):
            self.after(1, lambda _: self.right(kind, self.group).wait_send())
            self.before(1, lambda _: self.left(kind, self.group).wait_send())
            self.pair(kind, self.group).wait_send()

        self.every(own)

        def one(distance, carry):
            def lefts(line):
                block = self.at(line, self.side)

                def body(kind):
                    self.after(1, lambda _: self.right(kind, block).wait_send())
                    self.pair(kind, block).wait_send()

                self.every(body)
                passed(block)

            def rights(line):
                block = self.at(line, self.side)

                def body(kind):
                    self.before(1, lambda _: self.left(kind, block).wait_send())
                    self.pair(kind, block).wait_send()

                self.every(body)
                passed(block)

            self.before(distance, lefts)
            self.after(distance, rights)
            self.both(distance, 1 - self.side, passed)
            return carry

        lax.fori_loop(1, self.length, one, 0)
        passed(self.at(self.line, 1 - self.side))


def arrival_kernel(
    placed,
    weights,
    small,
    tokens,
    gathered,
    small_all,
    tok_stage,
    w_stage,
    small_stage,
    local_sem,
    tok_send,
    tok_recv,
    small_send,
    small_recv,
    x_send,
    x_recv,
    s_send,
    s_recv,
    r_send,
    r_recv,
    *sems,
    count,
):
    ctx, group, across, sibling = places()
    half = pl.ds(2 * lax.rem(ctx, 2), 2)
    kind = (lambda q: weights.at[half], lambda b, q: gathered.at[half, b])
    gather = Gather((kind,), sems, count, over_x=False)
    own_tok = pltpu.make_async_copy(placed.at[group], tok_stage, local_sem.at[0])
    own_w = pltpu.make_async_copy(weights, w_stage, local_sem.at[1])
    own_small = pltpu.make_async_copy(small, small_stage, local_sem.at[2])
    own_tok.start()
    own_w.start()
    own_small.start()
    greet(count)

    def tok_copy(peer, step):
        return remote(
            placed.at[peer],
            tokens.at[ctx, group],
            tok_send.at[step],
            tok_recv.at[step],
            {"fsdp": peer},
        )

    def small_copy(peer, step):
        return remote(
            small, small_all.at[group], small_send.at[step], small_recv.at[step], {"fsdp": peer}
        )

    def pass_on(block, quarter, send, recv, target):
        place = tokens.at[quarter, block]
        return remote(place, place, send.at[block], recv.at[block], {"ctx": target})

    def across_copy(block):
        return pass_on(block, ctx, x_send, x_recv, across)

    def sibling_copy(block):
        return pass_on(block, ctx, s_send, s_recv, sibling)

    def relay_copy(block):
        return pass_on(block, across, r_send, r_recv, sibling)

    def send(step, carry):
        peer = lax.rem(group + step, count)
        tok_copy(peer, step).start()
        small_copy(peer, step).start()
        return carry

    gather.start()
    lax.fori_loop(1, count, send, 0)
    own_tok.wait()
    own_w.wait()
    own_small.wait()
    put_tok = pltpu.make_async_copy(tok_stage, tokens.at[ctx, group], local_sem.at[0])
    put_w = pltpu.make_async_copy(w_stage, gathered.at[:, group], local_sem.at[1])
    put_small = pltpu.make_async_copy(small_stage, small_all.at[group], local_sem.at[2])
    put_tok.start()
    put_w.start()
    put_small.start()
    put_tok.wait()
    across_copy(group).start()
    sibling_copy(group).start()
    put_w.wait()
    put_small.wait()

    def arrive(step, carry):
        origin = lax.rem(group - step + count, count)
        tok_copy(origin, step).wait_recv()
        across_copy(origin).start()
        sibling_copy(origin).start()
        return carry

    length = count // 2
    gather.along(1)
    gather.beside(0)
    lax.fori_loop(1, 3, arrive, 0)

    def advance(distance, carry):
        gather.along(distance)
        gather.beside(distance - 1)
        lax.fori_loop(2 * distance - 1, 2 * distance + 1, arrive, 0)
        return carry

    lax.fori_loop(2, length, advance, 0)
    gather.beside(length - 1)
    lax.fori_loop(2 * length - 1, count, arrive, 0)

    def passed(step, carry):
        origin = lax.rem(group - step + count, count)
        across_copy(origin).wait_recv()
        relay_copy(origin).start()
        return carry

    lax.fori_loop(0, count, passed, 0)
    gather.finish()

    def finish(step, carry):
        origin = lax.rem(group - step + count, count)
        across_copy(origin).wait_send()
        sibling_copy(origin).wait()
        relay_copy(origin).wait()
        return carry

    lax.fori_loop(0, count, finish, 0)

    def sent(step, carry):
        peer = lax.rem(group + step, count)
        tok_copy(peer, step).wait_send()
        small_copy(peer, step).wait()
        return carry

    lax.fori_loop(1, count, sent, 0)


def bring_in(placed, weights, small):
    count, rows, width = placed.shape
    return pl.pallas_call(
        functools.partial(arrival_kernel, count=count),
        in_specs=[ANY] * 3,
        out_specs=[ANY] * 3,
        out_shape=[
            jax.ShapeDtypeStruct((4, count, rows, width), jnp.bfloat16),
            jax.ShapeDtypeStruct((4, count) + weights.shape[1:], jnp.bfloat16),
            jax.ShapeDtypeStruct((count,) + small.shape, jnp.bfloat16),
        ],
        scratch_shapes=[
            pltpu.VMEM((rows, width), jnp.bfloat16),
            pltpu.VMEM((4,) + weights.shape[1:], jnp.bfloat16),
            pltpu.VMEM(small.shape, jnp.bfloat16),
            DMA((3,)),
        ]
        + [DMA((count,))] * 10
        + Gather.scratch(1, count),
        compiler_params=pltpu.CompilerParams(
            collective_id=0, has_side_effects=True, vmem_limit_bytes=8 * 2**20
        ),
        name="bring_in",
    )(placed, weights, small)


class Sum:
    SCRATCH = 16

    def __init__(self, ref, out, scratch, count):
        self.ref, self.out, self.count = ref, out, count
        self.near, self.far, self.got_near, self.got_far = scratch[:4]
        self.got_across, self.got_group, self.done = scratch[4:7]
        self.load, self.c_send, self.c_recv, self.x_send, self.x_recv = scratch[7:12]
        self.g_send, self.g_recv, self.o_send, self.o_recv = scratch[12:16]
        self.ctx, self.group, self.across, self.sibling = places()
        self.width = self.near.shape[-1]

    @staticmethod
    def scratch(count, rows, width):
        return (
            [pltpu.VMEM((count, rows, width), jnp.bfloat16)] * 6
            + [pltpu.VMEM((rows, width), jnp.bfloat16)]
            + [DMA((2,))] * 3
            + [DMA((count,))] * 4
            + [DMA((4,))] * 2
        )

    def quarter(self, index):
        start = pl.multiple_of(lax.rem(index, 2) * self.width, self.width)
        return self.ref.at[:, index // 2, :, pl.ds(start, self.width)]

    def loads(self):
        return (
            pltpu.make_async_copy(self.quarter(self.across), self.far, self.load.at[0]),
            pltpu.make_async_copy(self.quarter(self.ctx), self.near, self.load.at[1]),
        )

    def cores(self):
        beyond = lax.rem(self.sibling + 2, 4)
        there = {"ctx": self.sibling}
        return (
            remote(self.quarter(beyond), self.got_far, self.c_send.at[0], self.c_recv.at[0], there),
            remote(
                self.quarter(self.sibling),
                self.got_near,
                self.c_send.at[1],
                self.c_recv.at[1],
                there,
            ),
        )

    def x_copy(self, block):
        return remote(
            self.far.at[block],
            self.got_across.at[block],
            self.x_send.at[block],
            self.x_recv.at[block],
            {"ctx": self.across},
        )

    def g_copy(self, peer, step):
        return remote(
            self.near.at[peer],
            self.got_group.at[step],
            self.g_send.at[step],
            self.g_recv.at[step],
            {"fsdp": peer},
        )

    def o_copy(self, other):
        return remote(
            self.done,
            self.out.at[self.ctx],
            self.o_send.at[other],
            self.o_recv.at[other],
            {"ctx": lax.rem(self.ctx + other, 4)},
        )

    def own_out(self):
        return pltpu.make_async_copy(self.done, self.out.at[self.ctx], self.load.at[0])

    def add(self, total, other):
        def one(block, carry):
            both = total[block].astype(jnp.float32) + other[block].astype(jnp.float32)
            total[block] = both.astype(jnp.bfloat16)
            return carry

        lax.fori_loop(0, self.count, one, 0)

    def start(self):
        for copy in self.loads() + self.cores():
            copy.start()

    def after_core(self):
        loads, cores = self.loads(), self.cores()
        loads[0].wait()
        cores[0].wait_recv()
        self.add(self.far, self.got_far)

        def send(step, carry):
            self.x_copy(lax.rem(self.group + 1 + step, self.count)).start()
            return carry

        lax.fori_loop(0, self.count, send, 0)
        loads[1].wait()
        cores[1].wait_recv()
        self.add(self.near, self.got_near)
        cores[0].wait_send()
        cores[1].wait_send()

    def after_across(self):
        def one(step, carry):
            block = lax.rem(self.group + step, self.count)
            self.x_copy(block).wait()
            both = self.near[block].astype(jnp.float32) + self.got_across[block].astype(jnp.float32)
            self.near[block] = both.astype(jnp.bfloat16)
            self.g_copy(block, step).start()
            return carry

        lax.fori_loop(1, self.count, one, 0)
        self.x_copy(self.group).wait()

    def after_group(self):
        group = self.group
        total = self.near[group].astype(jnp.float32) + self.got_across[group].astype(jnp.float32)

        def one(step, total):
            self.g_copy(lax.rem(group + step, self.count), step).wait()
            return total + self.got_group[step].astype(jnp.float32)

        self.done[...] = lax.fori_loop(1, self.count, one, total).astype(jnp.bfloat16)
        self.own_out().start()
        for other in range(1, 4):
            self.o_copy(other).start()

    def finish(self):
        self.own_out().wait()
        for other in range(1, 4):
            self.o_copy(other).wait()


class VectorSum:
    SCRATCH = 9

    def __init__(self, ref, out, scratch, count):
        self.ref, self.out, self.count = ref, out, count
        self.total, self.got_ctx, self.got_group = scratch[:3]
        self.load, self.c_send, self.c_recv, self.g_send, self.g_recv = scratch[3:8]
        self.result = scratch[8]
        self.ctx, self.group, _, _ = places()

    @staticmethod
    def scratch(count, rows, width):
        return [
            pltpu.VMEM((rows, width), jnp.float32),
            pltpu.VMEM((4, rows, width), jnp.float32),
            pltpu.VMEM((count, rows, width), jnp.float32),
            DMA((2,)),
            DMA((4,)),
            DMA((4,)),
            DMA((count,)),
            DMA((count,)),
            pltpu.VMEM((rows, width), jnp.float32),
        ]

    def own(self):
        return pltpu.make_async_copy(self.ref, self.total, self.load.at[0])

    def own_out(self):
        return pltpu.make_async_copy(self.result, self.out, self.load.at[1])

    def c_copy(self, other):
        return remote(
            self.ref,
            self.got_ctx.at[other],
            self.c_send.at[other],
            self.c_recv.at[other],
            {"ctx": lax.rem(self.ctx + other, 4)},
        )

    def g_copy(self, step):
        return remote(
            self.total,
            self.got_group.at[step],
            self.g_send.at[step],
            self.g_recv.at[step],
            {"fsdp": lax.rem(self.group + step, self.count)},
        )

    def start(self):
        self.own().start()
        for other in range(1, 4):
            self.c_copy(other).start()

    def after_core(self):
        self.own().wait()
        total = self.total[...]
        for other in range(1, 4):
            self.c_copy(other).wait()
            total = total + self.got_ctx[other]
        self.total[...] = total

        def one(step, carry):
            self.g_copy(step).start()
            return carry

        lax.fori_loop(1, self.count, one, 0)

    def after_across(self):
        pass

    def after_group(self):
        def one(step, total):
            self.g_copy(step).wait()
            return total + self.got_group[step]

        self.result[...] = lax.fori_loop(1, self.count, one, self.total[...])
        self.own_out().start()

    def finish(self):
        self.own_out().wait()


class LateSum:
    SCRATCH = 19

    def __init__(self, view, out, scratch, count):
        self.view, self.out, self.count = view, out, count
        self.near, self.got, self.got_pair, self.got_line = scratch[:4]
        self.half, self.got_across, self.done = scratch[4:7]
        self.load, self.c_send, self.c_recv, self.p_send, self.p_recv = scratch[7:12]
        self.l_send, self.l_recv, self.x_send, self.x_recv = scratch[12:16]
        self.o_send, self.o_recv, self.put = scratch[16:19]
        self.ctx, self.group, self.across, self.sibling = places()
        self.core = lax.rem(self.ctx, 2)
        self.line, self.side, self.length = self.group // 2, lax.rem(self.group, 2), count // 2
        self.halves = self.half.shape[0]

    @staticmethod
    def scratch(count, halves, rows, width):
        def block(*lead):
            return pltpu.VMEM(lead + (halves, rows, width), jnp.bfloat16)

        return (
            [block(count), block(count), block(count // 2), block(count // 2)]
            + [block(), block(), block()]
            + [DMA((halves,))] * 3
            + [DMA((count // 2,))] * 4
            + [DMA((1,))] * 2
            + [DMA((halves,))] * 3
        )

    def load_copy(self, half):
        return pltpu.make_async_copy(
            self.view(2 * half + self.core), self.near.at[:, half], self.load.at[half]
        )

    def core_copy(self, half):
        return remote(
            self.view(2 * half + 1 - self.core),
            self.got.at[:, half],
            self.c_send.at[half],
            self.c_recv.at[half],
            {"ctx": self.sibling},
        )

    def pair_copy(self, line):
        return remote(
            self.near.at[2 * line + 1 - self.side],
            self.got_pair.at[line],
            self.p_send.at[line],
            self.p_recv.at[line],
            {"fsdp": self.group + 1 - 2 * self.side},
        )

    def line_copy(self, step):
        peer = 2 * lax.rem(self.line + step, self.length) + self.side
        return remote(
            self.near.at[peer],
            self.got_line.at[step],
            self.l_send.at[step],
            self.l_recv.at[step],
            {"fsdp": peer},
        )

    def x_copy(self):
        return remote(
            self.half, self.got_across, self.x_send.at[0], self.x_recv.at[0], {"ctx": self.across}
        )

    def out_copy(self, half):
        return remote(
            self.done.at[half],
            self.out.at[2 * half + self.core],
            self.o_send.at[half],
            self.o_recv.at[half],
            {"ctx": self.sibling},
        )

    def own_out(self, half):
        return pltpu.make_async_copy(
            self.done.at[half], self.out.at[2 * half + self.core], self.put.at[half]
        )

    def add(self, block, other):
        both = self.near[block].astype(jnp.float32) + other.astype(jnp.float32)
        self.near[block] = both.astype(jnp.bfloat16)

    def start(self):
        for half in range(self.halves):
            self.load_copy(half).start()
            self.core_copy(half).start()

    def after_core(self):
        for half in range(self.halves):
            self.load_copy(half).wait()
            self.core_copy(half).wait()

        def theirs(step, carry):
            line = lax.rem(self.line + step, self.length)
            block = 2 * line + 1 - self.side
            self.add(block, self.got[block])
            self.pair_copy(line).start()
            return carry

        lax.fori_loop(0, self.length, theirs, 0)

        def mine(line, carry):
            block = 2 * line + self.side
            self.add(block, self.got[block])
            return carry

        lax.fori_loop(0, self.length, mine, 0)

    def after_pair(self):
        def one(step, carry):
            line = lax.rem(self.line + step, self.length)
            self.pair_copy(line).wait()
            self.add(2 * line + self.side, self.got_pair[line])
            self.line_copy(step).start()
            return carry

        lax.fori_loop(1, self.length, one, 0)
        self.pair_copy(self.line).wait()
        self.add(self.group, self.got_pair[self.line])

    def after_line(self):
        def one(step, total):
            self.line_copy(step).wait()
            return total + self.got_line[step].astype(jnp.float32)

        total = lax.fori_loop(1, self.length, one, self.near[self.group].astype(jnp.float32))
        self.half[...] = total.astype(jnp.bfloat16)
        self.x_copy().start()

    def after_across(self):
        self.x_copy().wait()
        both = self.half[...].astype(jnp.float32) + self.got_across[...].astype(jnp.float32)
        self.done[...] = both.astype(jnp.bfloat16)
        for half in range(self.halves):
            self.own_out(half).start()
            self.out_copy(half).start()

    def finish(self):
        for half in range(self.halves):
            self.own_out(half).wait()
            self.out_copy(half).wait()


def sums_kernel(*refs, parts, count):
    ins, outs, rest = refs[: parts + 1], refs[parts + 1 : 2 * parts + 2], refs[2 * parts + 2 :]
    jobs = [VectorSum(ins[parts], outs[parts], rest[: VectorSum.SCRATCH], count)]
    rest = rest[VectorSum.SCRATCH :]
    for index in range(parts):
        own = rest[index * Sum.SCRATCH : (index + 1) * Sum.SCRATCH]
        jobs.append(Sum(ins[index], outs[index], own, count))
    greet(count)
    for stage in STAGES:
        for job in jobs:
            getattr(job, stage)()


def sum_gradients(parts, vectors):
    count, _, rows, width = parts[0].shape
    width = width // 2
    scratch = VectorSum.scratch(count, *vectors.shape)
    for _ in parts:
        scratch += Sum.scratch(count, rows, width)
    return pl.pallas_call(
        functools.partial(sums_kernel, parts=len(parts), count=count),
        in_specs=[ANY] * (len(parts) + 1),
        out_specs=[ANY] * (len(parts) + 1),
        out_shape=[jax.ShapeDtypeStruct((4, rows, width), jnp.bfloat16)] * len(parts)
        + [jax.ShapeDtypeStruct(vectors.shape, jnp.float32)],
        scratch_shapes=scratch,
        compiler_params=pltpu.CompilerParams(
            collective_id=1, has_side_effects=True, vmem_limit_bytes=VMEM_BYTES
        ),
        name="sum_gradients",
    )(*parts, vectors)


def gather_plan(length):
    stretch = max(length - 2, 1)
    slots = [[] for _ in range(LAST_SLOT + 1)]

    def put(name, at, over, first):
        for distance in range(1, length):
            slot = min(at + (distance - 1) * over // stretch, LAST_SLOT)
            events = slots[slot]
            if events and events[-1][0] == name:
                events[-1] = (name, events[-1][1], distance + 1)
            else:
                events.append((name, distance, distance + 1))
        if first:
            slots[first].append((name, 0, 1))

    put("along", 2, 4, 0)
    put("beside", 5, 4, 2)
    put("line", 7, 4, 0)
    put("pair", 9, 3, 7)
    return slots


def forward_kernel(
    limit_ref,
    query_ref,
    key_ref,
    value_ref,
    inner_ref,
    outer_ref,
    attended_ref,
    lse_ref,
    inner_all,
    outer_all,
    *scratch,
    key_rows,
    count,
):
    pair = pl.program_id(0)
    pairs = pl.num_programs(0) - 1
    inner_stage, outer_stage, local, *sems = scratch
    width = outer_ref.shape[-1]

    def columns(quarter):
        return pl.ds(pl.multiple_of(quarter * width, width), width)

    kinds = (
        (lambda q: inner_ref.at[:, columns(q)], lambda b, q: inner_all.at[b, :, columns(q)]),
        (lambda q: outer_ref.at[q], lambda b, q: outer_all.at[b, q]),
    )
    gather = Gather(kinds, sems, count)
    loads = (
        pltpu.make_async_copy(inner_ref, inner_stage, local.at[0]),
        pltpu.make_async_copy(outer_ref, outer_stage, local.at[1]),
    )
    puts = (
        pltpu.make_async_copy(inner_stage, inner_all.at[gather.group], local.at[2]),
        pltpu.make_async_copy(outer_stage, outer_all.at[gather.group], local.at[3]),
    )
    plan = gather_plan(count // 2)

    def communicate(events):
        for name, first, last in events:
            act = {
                "along": gather.along,
                "beside": gather.beside,
                "line": lambda distance: gather.crossed(distance, 0),
                "pair": lambda distance: gather.crossed(distance, 1),
            }[name]
            if last - first == 1:
                act(first)
            else:

                def one(distance, carry, act=act):
                    act(distance)
                    return carry

                lax.fori_loop(first, last, one, 0)

    @pl.when(pair == 0)
    def _():
        greet(count)
        for load in loads:
            load.start()
        gather.start()
        for load, put in zip(loads, puts):
            load.wait()
            put.start()

    @pl.when(pair == pairs)
    def _():
        communicate(plan[LAST_SLOT])
        gather.finish()
        for put in puts:
            put.wait()

    @pl.when(pair < pairs)
    def _():
        low_half = lane_is_low()
        limit = limit_ref[0]
        queries = split_query(query_ref[...].astype(jnp.float32), low_half)
        query_rows = query_ref.shape[0]

        def step(tile, state):
            for slot in range(1, LAST_SLOT):
                if plan[slot]:

                    @pl.when(2 * pair + tile == slot)
                    def _(slot=slot):
                        communicate(plan[slot])

            start = pl.multiple_of(tile * key_rows, key_rows)
            usable = start + lax.broadcasted_iota(jnp.int32, (key_rows, 1), 0) < limit
            key_tile = key_ref[pl.ds(start, key_rows), :].astype(jnp.float32)
            keys = twice(jnp.where(usable, key_tile, key_ref[0:1, :].astype(jnp.float32)), low_half)
            value_tile = value_ref[pl.ds(start, key_rows), :].astype(jnp.float32)
            value_tile = jnp.where(usable, value_tile, 0.0)
            count = jnp.where(usable, 1.0, 0.0)
            values = (
                jnp.where(low_half, value_tile, count).astype(jnp.bfloat16),
                jnp.where(low_half, count, value_tile).astype(jnp.bfloat16),
            )
            fresh = []
            for head in range(2):
                top, total = state[head]
                scores = product(queries[head], keys[head], ((1,), (1,)))
                new_top = jnp.maximum(top, jnp.max(scores, axis=1, keepdims=True))
                weights = jnp.exp2(scores - new_top).astype(jnp.bfloat16)
                total = total * jnp.exp2(top - new_top) + product(weights, values[head], ((1,), (0,)))
                fresh.append((new_top, total))
            return tuple(fresh)

        empty = (
            jnp.full((query_rows, 1), NEG_BIG, jnp.float32),
            jnp.zeros((query_rows, 128), jnp.float32),
        )
        (top_a, total_a), (top_b, total_b) = lax.fori_loop(
            0, key_ref.shape[0] // key_rows, step, (empty, empty)
        )
        mass_a, mass_b = total_a[:, 64:65], total_b[:, 0:1]
        attended_ref[...] = jnp.where(low_half, total_a / mass_a, total_b / mass_b)
        lse = jnp.where(low_half, top_a + jnp.log2(mass_a), top_b + jnp.log2(mass_b)).T
        lse_ref[0, 0:1, :] = lse[0:1, :]
        lse_ref[0, 1:2, :] = lse[64:65, :]


def attend_forward(queries, keys, values, limit, inner, outer, count):
    rows, width = queries.shape
    full = keys.shape[0]
    pairs = width // 128
    shard = inner.shape[0]
    now = lambda pair, *_: (0, jnp.minimum(pair, pairs - 1))
    row_spec = pl.BlockSpec((rows, 128), now)
    key_spec = pl.BlockSpec((full, 128), now)
    return pl.pallas_call(
        functools.partial(forward_kernel, key_rows=full // 2, count=count),
        grid_spec=pltpu.PrefetchScalarGridSpec(
            num_scalar_prefetch=1,
            grid=(pairs + 1,),
            in_specs=[row_spec, key_spec, key_spec, ANY, ANY],
            out_specs=[
                row_spec,
                pl.BlockSpec((1, 2, rows), lambda pair, *_: (jnp.minimum(pair, pairs - 1), 0, 0)),
                ANY,
                ANY,
            ],
            scratch_shapes=[
                pltpu.VMEM((shard, 4 * width), jnp.bfloat16),
                pltpu.VMEM((4, shard, width), jnp.bfloat16),
                DMA((4,)),
            ]
            + Gather.scratch(2, count),
        ),
        out_shape=[
            jax.ShapeDtypeStruct((rows, width), jnp.float32),
            jax.ShapeDtypeStruct((pairs, 2, rows), jnp.float32),
            jax.ShapeDtypeStruct((count, shard, 4 * width), jnp.bfloat16),
            jax.ShapeDtypeStruct((count, 4, shard, width), jnp.bfloat16),
        ],
        compiler_params=pltpu.CompilerParams(
            collective_id=3, has_side_effects=True, vmem_limit_bytes=VMEM_BYTES
        ),
        cost_estimate=pl.CostEstimate(
            flops=16 * rows * full * width, bytes_accessed=20_000_000, transcendentals=0
        ),
        name="attend_forward",
    )(limit, queries, keys, values, inner, outer)


def backward_kernel(
    limit_ref,
    query_ref,
    key_ref,
    value_ref,
    grad_ref,
    attended_ref,
    lse_ref,
    inner_ref,
    outer_ref,
    output_ref,
    d_query_ref,
    d_key_ref,
    d_value_ref,
    inner_out,
    outer_out,
    output_out,
    query_sum,
    part,
    got_core,
    far,
    near,
    got_x,
    core_send,
    core_recv,
    x_send,
    x_recv,
    *rest,
    count,
):
    pair = pl.program_id(0)
    pairs = pl.num_programs(0) - 1
    slot = lax.rem(pair, 2)
    ctx, _, across, sibling = places()
    key_rows = query_ref.shape[0]
    def columns(ref, parts):
        size = ref.shape[2] // parts
        return lambda index: ref.at[:, :, pl.ds(pl.multiple_of(index * size, size), size)]

    views = (columns(inner_ref, 4), lambda index: outer_ref.at[:, index], columns(output_ref, 2))
    jobs = [
        LateSum(
            view, out, rest[index * LateSum.SCRATCH : (index + 1) * LateSum.SCRATCH], count
        )
        for index, (view, out) in enumerate(zip(views, (inner_out, outer_out, output_out)))
    ]

    def core_copy(which):
        return remote(
            part.at[which],
            got_core.at[slot, which],
            core_send.at[which],
            core_recv.at[slot, which],
            {"ctx": sibling},
        )

    def x_copy(where):
        return remote(
            far.at[where], got_x.at[where], x_send.at[where], x_recv.at[where], {"ctx": across}
        )

    def settle():
        where = 1 - slot
        x_copy(where).wait()
        for kind, ref in enumerate((d_key_ref, d_value_ref)):
            both = near[where, kind].astype(jnp.float32) + got_x[where, kind].astype(jnp.float32)
            ref[...] = both.astype(jnp.bfloat16)

    @pl.when(pair == 0)
    def _():
        greet(count)
        for job in jobs:
            job.start()

    @pl.when(pair < pairs)
    def _():
        low_half = lane_is_low()
        high_half = jnp.logical_not(low_half)
        lane = lax.broadcasted_iota(jnp.int32, (1, 128), 1)
        limit = limit_ref[0]
        query_pair = query_ref[...].astype(jnp.float32)
        queries = split_query(query_pair, low_half)
        scaled = query_pair * SCALE
        grad_pair = grad_ref[...].astype(jnp.float32)
        overlap = grad_pair * attended_ref[...]
        own_query, own_grad, joined_grad = [], [], []
        for head in range(2):
            mine = low_half if head == 0 else high_half
            own_query.append(jnp.where(mine, scaled, 0.0).astype(jnp.bfloat16))
            own_grad.append(jnp.where(mine, grad_pair, 0.0).astype(jnp.bfloat16))
            delta = -jnp.sum(jnp.where(mine, overlap, 0.0), axis=1, keepdims=True)
            first = delta.astype(jnp.bfloat16).astype(jnp.float32)
            second = (delta - first).astype(jnp.bfloat16).astype(jnp.float32)
            third = delta - first - second
            spare = 64 * (1 - head)
            joined = jnp.where(lane == spare + 2, third, 0.0)
            joined = jnp.where(lane == spare + 1, second, joined)
            joined = jnp.where(lane == spare, first, joined)
            joined_grad.append(jnp.where(mine, grad_pair, joined).astype(jnp.bfloat16))
        query_sum[...] = jnp.zeros_like(query_sum)

        def step(tile, carry):
            for at, stages in SUM_PLAN.items():

                @pl.when(4 * pair + tile == at)
                def _(stages=stages):
                    for index, stage in stages:
                        getattr(jobs[index], stage)()

            odd = lax.rem(tile, 2)
            quarter = lax.rem(sibling + odd * (ctx - sibling) + 2 * (1 - tile // 2), 4)
            start = pl.multiple_of(quarter * key_rows, key_rows)
            usable = start + lax.broadcasted_iota(jnp.int32, (key_rows, 1), 0) < limit
            key_tile = key_ref[pl.ds(start, key_rows), :].astype(jnp.float32)
            value_tile = value_ref[pl.ds(start, key_rows), :].astype(jnp.float32)
            keys = twice(jnp.where(usable, key_tile, key_ref[0:1, :].astype(jnp.float32)), low_half)
            own_tile = jnp.where(usable, key_tile * SCALE, 0.0)
            key_piece = value_piece = None
            for head in range(2):
                mine = low_half if head == 0 else high_half
                values = jnp.where(mine, value_tile, 1.0).astype(jnp.bfloat16)
                own_key = jnp.where(mine, own_tile, 0.0).astype(jnp.bfloat16)
                scores = product(keys[head], queries[head], ((1,), (1,)))
                probs = jnp.exp2(scores - lse_ref[0, head : head + 1, :])
                slopes = product(values, joined_grad[head], ((1,), (1,)))
                score_grads = (probs * slopes).astype(jnp.bfloat16)
                value_term = product(probs.astype(jnp.bfloat16), own_grad[head], ((1,), (0,)))
                key_term = product(score_grads, own_query[head], ((1,), (0,)))
                value_piece = value_term if value_piece is None else value_piece + value_term
                key_piece = key_term if key_piece is None else key_piece + key_term
                query_sum[...] += product(own_key, score_grads, ((0,), (0,)))
            pieces = (jnp.where(usable, key_piece, 0.0), jnp.where(usable, value_piece, 0.0))

            @pl.when(odd == 0)
            def _():
                which = tile // 2
                for kind in range(2):
                    part[which, kind] = pieces[kind].astype(jnp.bfloat16)
                core_copy(which).start()

            @pl.when(tile == 1)
            def _():
                @pl.when(pair > 0)
                def _():
                    settle()

                core_copy(0).wait_recv()
                for kind in range(2):
                    both = pieces[kind] + got_core[slot, 0, kind].astype(jnp.float32)
                    far[slot, kind] = both.astype(jnp.bfloat16)
                x_copy(slot).start()

            @pl.when(tile == 3)
            def _():
                core_copy(1).wait_recv()
                for kind in range(2):
                    both = pieces[kind] + got_core[slot, 1, kind].astype(jnp.float32)
                    near[slot, kind] = both.astype(jnp.bfloat16)
                core_copy(0).wait_send()
                core_copy(1).wait_send()

            return carry

        lax.fori_loop(0, 4, step, 0)
        d_query_ref[...] = query_sum[...].T.astype(jnp.bfloat16)

    @pl.when(pair == pairs)
    def _():
        settle()
        for job in jobs:
            job.finish()


def attend_backward(queries, keys, values, limit, grad_rows, attended, lse, parts):
    rows, width = queries.shape
    full = keys.shape[0]
    pairs = width // 128
    count, shard = parts[0].shape[:2]
    now = lambda pair, *_: (0, jnp.minimum(pair, pairs - 1))
    before = lambda pair, *_: (0, jnp.maximum(pair - 1, 0))
    row_spec = pl.BlockSpec((rows, 128), now)
    key_spec = pl.BlockSpec((full, 128), now)
    sum_spec = pl.BlockSpec((rows, 128), before)
    tile = (2, rows, 128)
    return pl.pallas_call(
        functools.partial(backward_kernel, count=count),
        grid_spec=pltpu.PrefetchScalarGridSpec(
            num_scalar_prefetch=1,
            grid=(pairs + 1,),
            in_specs=[
                row_spec,
                key_spec,
                key_spec,
                row_spec,
                row_spec,
                pl.BlockSpec((1, 2, rows), lambda pair, *_: (jnp.minimum(pair, pairs - 1), 0, 0)),
                ANY,
                ANY,
                ANY,
            ],
            out_specs=[row_spec, sum_spec, sum_spec, ANY, ANY, ANY],
            scratch_shapes=[
                pltpu.VMEM((128, rows), jnp.float32),
                pltpu.VMEM((2,) + tile, jnp.bfloat16),
                pltpu.VMEM((2, 2) + tile, jnp.bfloat16),
                pltpu.VMEM((2,) + tile, jnp.bfloat16),
                pltpu.VMEM((2,) + tile, jnp.bfloat16),
                pltpu.VMEM((2,) + tile, jnp.bfloat16),
                DMA((2,)),
                DMA((2, 2)),
                DMA((2,)),
                DMA((2,)),
            ]
            + LateSum.scratch(count, 2, shard, width) * 2
            + LateSum.scratch(count, 1, shard, width // 2),
        ),
        out_shape=[jax.ShapeDtypeStruct((rows, width), jnp.bfloat16)] * 3
        + [jax.ShapeDtypeStruct((4, shard, width), jnp.bfloat16)] * 2
        + [jax.ShapeDtypeStruct((2, shard, width // 2), jnp.bfloat16)],
        compiler_params=pltpu.CompilerParams(
            collective_id=2, has_side_effects=True, vmem_limit_bytes=VMEM_BYTES
        ),
        cost_estimate=pl.CostEstimate(
            flops=40 * rows * full * width, bytes_accessed=40_000_000, transcendentals=0
        ),
        name="attend_backward",
    )(limit, queries, keys, values, grad_rows, attended, lse, *parts)


def on_device(
    hidden_in,
    lengths,
    seq_order,
    query_weight,
    query_bias,
    key_weight,
    value_weight,
    value_bias,
    output_weight,
    output_bias,
    norm1_gain,
    norm1_shift,
    inner_weight,
    inner_bias,
    outer_weight,
    outer_bias,
    norm2_gain,
    norm2_shift,
    cotangent,
):
    width = hidden_in.shape[2]
    count = lax.axis_size("fsdp")
    group = lax.axis_index("fsdp")
    shard = query_bias.shape[0]
    low = jnp.bfloat16
    placed = jnp.swapaxes(hidden_in, 0, 1).at[seq_order].get(mode="promise_in_bounds")
    vectors = jnp.concatenate(
        (
            jnp.stack(
                (
                    query_bias,
                    value_bias,
                    output_bias,
                    norm1_gain,
                    norm1_shift,
                    outer_bias,
                    norm2_gain,
                    norm2_shift,
                )
            ),
            inner_bias.reshape(4, shard),
        )
    )
    vectors = jnp.pad(vectors, ((0, 4), (0, 128 - shard)))
    weights = jnp.stack((query_weight, key_weight, value_weight, output_weight))
    tokens, weights, vectors = bring_in(placed, weights, vectors)
    w_query, w_key, w_value, w_output = (weights[i].reshape(width, width) for i in range(4))
    vectors = vectors[:, :12, :shard].astype(jnp.float32)
    b_query, b_value, b_output, gain_one, shift_one, b_outer, gain_two, shift_two = (
        vectors[:, i].reshape(width) for i in range(8)
    )
    b_inner = vectors[:, 8:].reshape(-1)
    limits = jnp.take(lengths, jnp.take(seq_order, group[None]))
    all_rows = tokens.reshape(-1, width)
    local_len = all_rows.shape[0] // 4
    token_rows = lax.dynamic_index_in_dim(tokens, lax.axis_index("ctx"), 0, False)
    token_rows = token_rows.reshape(local_len, width)
    queries = (product(token_rows, w_query, ((1,), (0,))) + b_query).astype(low)
    keys = product(all_rows, w_key, ((1,), (0,))).astype(low)
    values = (product(all_rows, w_value, ((1,), (0,))) + b_value).astype(low)
    attended, lse, w_inner, w_outer = attend_forward(
        queries,
        keys,
        values,
        limits,
        inner_weight,
        outer_weight.reshape(4, shard, width),
        count,
    )
    w_inner = w_inner.reshape(width, 4 * width)
    w_outer = w_outer.reshape(4 * width, width)
    mixed_low = attended.astype(low)
    branch = product(mixed_low, w_output, ((1,), (0,))) + b_output
    normed, unit_one, scale_one = norm_forward(
        token_rows.astype(jnp.float32) + branch, gain_one, shift_one
    )
    normed_low = normed.astype(low)
    inner_pre = product(normed_low, w_inner, ((1,), (0,))) + b_inner
    activated = gelu_exact(inner_pre).astype(low)
    outer_out = product(activated, w_outer, ((1,), (0,))) + b_outer
    second, unit_two, scale_two = norm_forward(normed + outer_out, gain_two, shift_two)
    layer_out = second.astype(low).reshape(local_len, 1, width)
    upstream = cotangent.reshape(local_len, width).astype(jnp.float32)
    d_second, grad_gain_two, grad_shift_two = norm_backward(upstream, unit_two, scale_two, gain_two)
    d_outer = d_second.astype(low)
    grad_outer_w = product(activated, d_outer, ((0,), (0,))).astype(low)
    grad_outer_b = jnp.sum(d_outer.astype(jnp.float32), axis=0)
    inner_grad = product(d_outer, w_outer, ((1,), (1,)))
    d_inner = (inner_grad * gelu_slope(inner_pre)).astype(low)
    grad_inner_w = product(normed_low, d_inner, ((0,), (0,))).astype(low)
    grad_inner_b = jnp.sum(d_inner.astype(jnp.float32), axis=0)
    d_normed = d_second + product(d_inner, w_inner, ((1,), (1,)))
    d_res, grad_gain_one, grad_shift_one = norm_backward(d_normed, unit_one, scale_one, gain_one)
    d_branch = d_res.astype(low)
    grad_output_w = product(mixed_low, d_branch, ((0,), (0,))).astype(low)
    grad_output_b = jnp.sum(d_branch.astype(jnp.float32), axis=0)
    d_mixed = product(d_branch, w_output, ((1,), (1,))).astype(low)
    d_query, d_keys, d_values, inner_w, outer_w, output_w = attend_backward(
        queries,
        keys,
        values,
        limits,
        d_mixed,
        attended,
        lse,
        (
            grad_inner_w.reshape(count, shard, 4 * width),
            grad_outer_w.reshape(count, 4, shard, width),
            grad_output_w.reshape(count, shard, width),
        ),
    )
    grad_query_w = product(token_rows, d_query, ((0,), (0,))).astype(low)
    grad_query_b = jnp.sum(d_query.astype(jnp.float32), axis=0)
    grad_key_w = product(token_rows, d_keys, ((0,), (0,))).astype(low)
    grad_value_w = product(token_rows, d_values, ((0,), (0,))).astype(low)
    grad_value_b = jnp.sum(d_values.astype(jnp.float32), axis=0)
    d_placed = d_res + product(d_query, w_query, ((1,), (1,)))
    d_placed = d_placed + product(d_keys, w_key, ((1,), (1,)))
    d_placed = d_placed + product(d_values, w_value, ((1,), (1,)))
    back_rows = d_placed.astype(low).reshape(count, local_len // count, width)
    returned = lax.all_to_all(back_rows, "fsdp", split_axis=0, concat_axis=0, tiled=True)
    inverse = jnp.argmax(seq_order[:, None] == jnp.arange(count), axis=0)
    grad_in = jnp.swapaxes(returned.at[inverse].get(mode="promise_in_bounds"), 0, 1)
    small_sums = jnp.concatenate(
        (
            jnp.stack(
                (
                    grad_query_b,
                    grad_value_b,
                    grad_output_b,
                    grad_gain_one,
                    grad_shift_one,
                    grad_outer_b,
                    grad_gain_two,
                    grad_shift_two,
                )
            ),
            grad_inner_b.reshape(4, width),
            jnp.zeros((4, width), jnp.float32),
        )
    )
    *attention_w, small_sums = sum_gradients(
        [
            part.reshape(count, 2, shard // 2, width)
            for part in (grad_query_w, grad_key_w, grad_value_w)
        ],
        small_sums,
    )
    attention_w = [
        jnp.swapaxes(part.reshape(2, 2, shard // 2, width // 2), 1, 2)
        .reshape(shard, width)
        .astype(jnp.float32)
        for part in attention_w
    ]
    output_w = jnp.swapaxes(output_w, 0, 1).reshape(shard, width).astype(jnp.float32)
    inner_w = jnp.swapaxes(inner_w, 0, 1).reshape(shard, 4 * width).astype(jnp.float32)
    outer_w = outer_w.reshape(4 * shard, width).astype(jnp.float32)
    small = lax.dynamic_slice_in_dim(small_sums[:8], group * shard, shard, axis=1)
    inner_b = lax.dynamic_slice_in_dim(
        small_sums[8:12].reshape(-1), group * 4 * shard, 4 * shard, axis=0
    )
    return (
        layer_out,
        grad_in,
        attention_w[0],
        small[0],
        attention_w[1],
        attention_w[2],
        small[1],
        output_w,
        small[2],
        small[3],
        small[4],
        inner_w,
        inner_b,
        outer_w,
        small[5],
        small[6],
        small[7],
    )


def solution(mesh):
    placed = (
        P(("ctx", "fsdp"), None, None),
        P(),
        P(),
        P("fsdp", None),
        P("fsdp"),
        P("fsdp", None),
        P("fsdp", None),
        P("fsdp"),
        P("fsdp", None),
        P("fsdp"),
        P("fsdp"),
        P("fsdp"),
        P("fsdp", None),
        P("fsdp"),
        P("fsdp", None),
        P("fsdp"),
        P("fsdp"),
        P("fsdp"),
        P("ctx", "fsdp", None),
    )
    return jax.shard_map(
        on_device,
        mesh=mesh,
        in_specs=placed,
        out_specs=(
            P("ctx", "fsdp", None),
            P(("ctx", "fsdp"), None, None),
            P("fsdp", None),
            P("fsdp"),
            P("fsdp", None),
            P("fsdp", None),
            P("fsdp"),
            P("fsdp", None),
            P("fsdp"),
            P("fsdp"),
            P("fsdp"),
            P("fsdp", None),
            P("fsdp"),
            P("fsdp", None),
            P("fsdp"),
            P("fsdp"),
            P("fsdp"),
        ),
        check_vma=False,
    )
```
